128 devices in a mesh: tile: 32 (over z_lo, x, y), wave: 4 (over z_hi, core).
Axes of the slice: x: 4, y: 4, z: 4 (z_hi: 2, z_lo: 2; z = z_hi * 2 + z_lo), core: 2. Of those that a mesh axis runs over, the one named last changes fastest.
Arguments:
- maps: float32 [4, 128, 4096], P(None, None, 'tile'), may hold values from 0 to 2
- measured: float32 [64, 128, 128], P('tile'), may hold values from 0 to 8
- offsets: int32 [64], P('tile'), may hold values from -64 to 64, as said below
- probe: float32 [48, 2, 128, 128], P('wave'), may hold values from -6 to 6
- spectrum: float32 [48], P('wave'), may hold values from 0.05 to 0.5
- wave_index: int32 [48], P('wave'), may hold values from 0 to 47, each once
- edge_band: int32 [48, 4], P('wave'), may hold values from 0 to 2
- band_coef: float32 [2, 3, 4], replicated, may hold values from 0.1 to 0.8
Outputs:
- new_maps: float32 [4, 128, 4096], P(None, None, 'tile')
The draws below stay inside these ranges and needn't reach their ends.
Inputs may be any that keep to these rules, and one draw needn't show every extreme that they name: `offsets`: a frame reaches at most 64 columns into either neighbouring tile; in every tile one frame starts exactly 64 columns before the tile and another ends exactly 64 columns after it. `wave_index`: each wavelength is held by exactly one slot.
All inputs are finite; a program needn't handle non-finite values.
Results may differ from the reference program's by a relative error of at most 0.0024.
Values sent between devices are 32-bit elements; how exact they have to be, the bound alone decides.
A program may use at most 64 MiB of HBM per device.

```python
import math
import jax
import jax.numpy as jnp
from jax import lax

FRAME = 128
COLS = 128
FRAMES = 2
WAVES = 48
MATERIALS = 4
BANDS = 3
TILECOLS = 4096
FRAMES_ALL = 64
N_TILE = 32


def draw_maps(key, part):
    base = jax.random.uniform(jax.random.fold_in(key, 11), (MATERIALS, FRAME, TILECOLS), jnp.float32)
    position = jnp.arange(TILECOLS, dtype=jnp.float32) / (TILECOLS - 1)
    thickness = 0.25 + 1.75 * position
    return base * thickness[None, None, :]


def draw_offsets(key, part):
    tiles = FRAMES_ALL // FRAMES
    margin = FRAME // 2
    lowest = 0 - margin
    highest = COLS + margin - FRAME
    spread = jax.random.randint(jax.random.fold_in(key, 21), (tiles, FRAMES), lowest, highest + 1, dtype=jnp.int32)
    first = jax.random.randint(jax.random.fold_in(key, 22), (tiles, 1), 0, FRAMES, dtype=jnp.int32)
    step_on = jax.random.randint(jax.random.fold_in(key, 23), (tiles, 1), 1, FRAMES, dtype=jnp.int32)
    second = (first + step_on) % FRAMES
    slots = jnp.arange(FRAMES, dtype=jnp.int32)[None, :]
    spread = jnp.where(slots == first, lowest, spread)
    spread = jnp.where(slots == second, highest, spread)
    return spread.reshape(FRAMES_ALL).astype(jnp.int32)


def touch_ends(result, own_key, smallest, top_value):
    extent = result.shape
    place = [jax.random.randint(jax.random.fold_in(own_key, axis), (), 0, extent[axis]) for axis in range(len(extent))]
    result = result.at[tuple(place)].set(smallest)
    longest = extent.index(max(extent))
    place[longest] = (place[longest] + 1) % extent[longest]
    return result.at[tuple(place)].set(top_value)


def block_scale(own_key, extent, split, low, largest):
    def one(axis_at, parts):
        steps = jax.random.uniform(jax.random.fold_in(jax.random.fold_in(own_key, 6), axis_at), (parts,), jnp.float32, low / len(split), largest / len(split))
        return jnp.repeat(jnp.exp(steps), extent[axis_at] // parts).reshape((-1,) + (1,) * (len(extent) - axis_at - 1))

    loudness = one(*split[0])
    for cut in split[1:]:
        loudness = loudness * one(*cut)
    return loudness


def gaussian(own_key, extent, deviation, most, pieces=(), kind=jnp.bfloat16):
    factor_of = block_scale(own_key, extent, pieces, -0.22, 0.18) if pieces else 1.0
    array = jax.random.normal(own_key, extent, jnp.float32) * deviation * factor_of
    return jnp.minimum(jnp.maximum(array, -most), most).astype(kind)


def setup_inputs(seed: int = 0) -> dict:
    key_list = jax.random.split(jax.random.key(seed), 9)
    return {
        "maps": draw_maps(jax.random.fold_in(key_list[8], 71), 0),
        "measured": jnp.clip(8.0 * jax.random.uniform(key_list[1], (FRAMES_ALL, FRAME, FRAME), jnp.float32) ** block_scale(key_list[1], (FRAMES_ALL, FRAME, FRAME), ((0, 32),), -0.2, 0.2), 0.0, 8.0),
        "offsets": draw_offsets(jax.random.fold_in(key_list[8], 71), 0),
        "probe": gaussian(key_list[3], (WAVES, 2, FRAME, FRAME), 1.0, 6.0, ((0, 4),), jnp.float32),
        "spectrum": jnp.clip(jnp.exp(math.log(0.5) - 2.3025851 * jax.random.uniform(key_list[4], (WAVES,), jnp.float32) ** block_scale(key_list[4], (WAVES,), ((0, 4),), -0.2, 0.2)), 0.05, 0.5),
        "wave_index": jax.random.permutation(key_list[5], WAVES).astype(jnp.int32),
        "edge_band": touch_ends(jax.random.randint(key_list[6], (WAVES, MATERIALS), 0, BANDS), jax.random.fold_in(key_list[6], 1), 0, BANDS - 1).astype(jnp.int32),
        "band_coef": jnp.clip(jax.random.uniform(key_list[7], (2, BANDS, MATERIALS), jnp.float32, 0.1, 0.8), 0.1, 0.8),
    }


relax = 4.0
floor_level = 1.0

def chirp_table(which_wave, length):
    centred = jnp.arange(length, dtype=jnp.int32) - length // 2
    product = (centred[:, None] * centred[None, :]).astype(jnp.float32)
    sampling = 0.6 + 0.4 * which_wave.astype(jnp.float32) / (WAVES - 1)
    phase_angle = -2.0 * math.pi / length * sampling[..., None, None] * product
    normaliser = 1.0 / math.sqrt(length)
    return ((jnp.cos(phase_angle) * normaliser).astype(jnp.bfloat16), (jnp.sin(phase_angle) * normaliser).astype(jnp.bfloat16))

def left_product(table, data):
    return jnp.einsum('skn,snj->skj', table.astype(jnp.float32), data.astype(jnp.float32), precision=lax.Precision.HIGHEST)

def right_product(data, table):
    return jnp.einsum('skn,snj->skj', data.astype(jnp.float32), table.astype(jnp.float32), precision=lax.Precision.HIGHEST)

def transform(table_re, table_im, data_re, data_im):
    mid_re = (left_product(table_re, data_re) - left_product(table_im, data_im)).astype(jnp.bfloat16)
    mid_im = (left_product(table_re, data_im) + left_product(table_im, data_re)).astype(jnp.bfloat16)
    out_re = right_product(mid_re, table_re) - right_product(mid_im, table_im)
    out_im = right_product(mid_re, table_im) + right_product(mid_im, table_re)
    return (out_re, out_im)

def reference(maps, measured, offsets, probe, spectrum, wave_index, edge_band, band_coef):
    materials = maps.shape[0]
    margin = FRAME // 2
    padded = jnp.pad(maps, ((0, 0), (0, 0), (margin, margin)))
    onehot = (edge_band[:, :, None] == jnp.arange(BANDS, dtype=jnp.int32)).astype(jnp.float32)
    coefficient = jnp.einsum('smb,cbm->csm', onehot, band_coef.astype(jnp.float32), precision=lax.Precision.HIGHEST)
    table_re, table_im = chirp_table(wave_index, FRAME)
    tile_of = jnp.arange(FRAMES * N_TILE, dtype=jnp.int32) // FRAMES
    starts = (tile_of * COLS + offsets + margin).astype(jnp.int32)
    weights = spectrum[:, None, None]

    def frame_step(accumulated, inputs):
        start_col, observed = inputs
        window = lax.dynamic_slice_in_dim(padded, start_col, FRAME, 2)
        absorb = jnp.einsum('sm,mrk->srk', coefficient[0], window, precision=lax.Precision.HIGHEST)
        phase_sum = jnp.einsum('sm,mrk->srk', coefficient[1], window, precision=lax.Precision.HIGHEST)
        damping = jnp.exp(-absorb)
        obj_re = damping * jnp.cos(phase_sum)
        obj_im = damping * jnp.sin(phase_sum)
        psi_re = probe[:, 0] * obj_re - probe[:, 1] * obj_im
        psi_im = probe[:, 0] * obj_im + probe[:, 1] * obj_re
        far_re, far_im = transform(table_re, table_im, psi_re.astype(jnp.bfloat16), psi_im.astype(jnp.bfloat16))
        intensity = lax.optimization_barrier(jnp.sum(weights * (far_re * far_re + far_im * far_im), axis=0))
        shortfall = jnp.sqrt(observed / jnp.maximum(intensity, floor_level)) - 1.0
        factor = weights * shortfall[None]
        back_re, back_im = transform(table_re, -table_im, (factor * far_re).astype(jnp.bfloat16), (factor * far_im).astype(jnp.bfloat16))
        cross_re = psi_re * back_re + psi_im * back_im
        cross_im = psi_re * back_im - psi_im * back_re
        gradient = jnp.einsum('sm,skj->mkj', -coefficient[0], cross_re, precision=lax.Precision.HIGHEST) + jnp.einsum('sm,skj->mkj', coefficient[1], cross_im, precision=lax.Precision.HIGHEST)
        power_sum = lax.optimization_barrier(jnp.sum(weights * (psi_re * psi_re + psi_im * psi_im), axis=0))
        term = jnp.concatenate([gradient, power_sum[None]], axis=0)
        current = lax.dynamic_slice_in_dim(accumulated, start_col, FRAME, 2)
        accumulated = lax.dynamic_update_slice_in_dim(accumulated, current + term, start_col, 2)
        return (accumulated, None)
    accumulated = jnp.zeros((materials + 1, FRAME, COLS * N_TILE + 2 * margin), jnp.float32)
    accumulated, _ = lax.scan(frame_step, accumulated, (starts, measured))
    reduced = accumulated[:, :, margin:margin + COLS * N_TILE]
    return maps + relax * reduced[:materials] / (reduced[materials] + 1.0)
```

```python
import functools
import math

import jax
import jax.numpy as jnp
from jax import lax
from jax.experimental import pallas as pl
from jax.experimental.pallas import tpu as pltpu
from jax.sharding import PartitionSpec as P

WAVES = 48
RELAX = 4.0
FLOOR = 1.0
MESH = pl.DeviceIdType.MESH
F32 = jnp.float32
BF16 = jnp.bfloat16

SIN = (6.283184916495429, -41.341589232688364, 81.5999433297776, -76.61447253120122, 41.34288235437901, -12.471243534763557)
COS = (0.9999999890590201, -19.739204499453688, 64.93911745988827, -85.45013953077586, 60.16763095018129, -25.96759924584206, 6.528658157862129)

HALO, MEAS, PW1, PWL, PWA, PWB, IN1, IN2, SF, GR1, GRL, GRA, GRB, OUT = range(14)
XIN1, XIN2, XSF, XPW1, XPWB, XGR1, XGRB = range(14, 21)
MESSAGES = 21


def sincos_turns(turns):
    f = turns - jnp.round(turns)
    z = f * f
    s = jnp.full_like(z, SIN[-1])
    for k in SIN[-2::-1]:
        s = s * z + k
    c = jnp.full_like(z, COS[-1])
    for k in COS[-2::-1]:
        c = c * z + k
    return c, s * f


def swap(x):
    return pltpu.roll(x, 64, x.ndim - 1)


def kernel(
    tiles,
    maps_hbm, meas_hbm, off_ref, probe_hbm, spec_ref, wave_ref, edge_ref, band_ref,
    out_ref,
    mp, ms, pb, w1, w2, win, winx, psir, psii, psib, farr, fari, psirx, psiix, farrx, farix, nbuf,
    halo_s, halo_r, ma_s, ma_r,
    inten, inten_r, half_i, half_r, sf, intenx, intenx_r, half_ix, half_rx, sfx,
    acc, acc_r, accx, accx_r,
    lpack, lrecv, rpack, ra, rb, rpx,
    copy_sem, send_sem, recv_sem,
):
    slots = spec_ref.shape[0]
    length = out_ref.shape[1]
    mid = length // 2
    t = lax.axis_index("tile")
    w = lax.axis_index("wave")
    core = lax.rem(w, 2)
    mate = w + 1 - 2 * core
    far_z = lax.rem(w + 2, 4)
    up = lax.rem(t + 1, tiles)
    down = lax.rem(t + tiles - 1, tiles)
    first = t == 0
    last = t == tiles - 1

    mine = pl.ds(pl.multiple_of(core * mid, mid), mid)
    other = pl.ds(pl.multiple_of((1 - core) * mid, mid), mid)

    barrier = pltpu.get_barrier_semaphore()
    for device in ((t, mate), (t, far_z), (up, w), (down, w), (up, far_z), (down, far_z)):
        pl.semaphore_signal(barrier, inc=1, device_id=device, device_id_type=MESH)

    load_maps = pltpu.make_async_copy(maps_hbm, mp, copy_sem.at[0])
    load_meas = pltpu.make_async_copy(meas_hbm, ms, copy_sem.at[1])
    load_probe = pltpu.make_async_copy(probe_hbm, pb, copy_sem.at[2])
    load_maps.start()
    load_meas.start()
    load_probe.start()

    def remote(k, src, dst, device):
        return pltpu.make_async_remote_copy(
            src_ref=src, dst_ref=dst, send_sem=send_sem.at[k], recv_sem=recv_sem.at[k],
            device_id=device, device_id_type=MESH,
        )

    lane_low = lax.broadcasted_iota(jnp.int32, (mid, length), 1) < mid
    lane_low32 = lax.broadcasted_iota(jnp.int32, (mid // 2, length), 1) < mid

    load_maps.wait()
    for m in range(4):
        halo_s[m] = jnp.where(lane_low, mp[m, 0:mid], swap(mp[m, mid:length]))
    pl.semaphore_wait(barrier, 6)

    send_halo = remote(HALO, halo_s, halo_r, (down, w))

    @pl.when(t > 0)
    def _():
        send_halo.start()

    load_meas.wait()
    low_first = off_ref[0] < off_ref[1]
    for r in range(0, length, 32):
        rows = pl.ds(r, 32)
        one, two = ms[0, rows, :], ms[1, rows, :]
        ma_s[rows, :] = jnp.where(low_first, one, two)
        ms[1, rows, :] = jnp.where(low_first, two, one)

    send_meas = remote(MEAS, ma_s.at[mine], ma_r, (down, w))

    @pl.when(t > 0)
    def _():
        send_meas.start()

    @pl.when(last)
    def _():
        halo_r[...] = jnp.zeros_like(halo_r)
        ma_r[...] = jnp.zeros_like(ma_r)

    column = lax.broadcasted_iota(jnp.int32, (32, length), 1) - mid
    row = lax.broadcasted_iota(jnp.int32, (32, length), 0) - mid
    normaliser = 1.0 / math.sqrt(length)

    def table_slot(s, carry):
        which = jnp.full((32, length), wave_ref[s], jnp.int32).astype(F32)
        sampling = (0.6 + 0.4 * which / (WAVES - 1)) * (1.0 / length)
        for r in range(0, length, 32):
            c, sn = sincos_turns(sampling * ((row + r) * column).astype(F32))
            re = (c * normaliser).astype(BF16)
            sn = sn * normaliser
            im = (-sn).astype(BF16)
            nim = sn.astype(BF16)
            top, low = pl.ds(r, 32), pl.ds(length + r, 32)
            left, right = pl.ds(0, length), pl.ds(length, length)
            w1[s, top, left] = re
            w1[s, top, right] = nim
            w1[s, low, left] = im
            w1[s, low, right] = re
            w2[s, top, left] = re
            w2[s, top, right] = im
            w2[s, low, left] = nim
            w2[s, low, right] = re
        return carry

    lax.fori_loop(0, slots, table_slot, 0)

    def coefficients(s):
        a, b = [], []
        for m in range(4):
            e = edge_ref[s, m]
            for row_of, into in ((0, a), (1, b)):
                c = [band_ref[row_of, k, m] for k in range(3)]
                into.append(jnp.where(e == 0, c[0], jnp.where(e == 1, c[1], c[2])))
        return a, b

    def waves_at_object(window, pr, pi, power):
        power[...] = jnp.zeros_like(power)

        def body(s, carry):
            a, b = coefficients(s)
            spec = spec_ref[s]
            for r in range(0, length, 32):
                rows = pl.ds(r, 32)
                planes = [window[m, rows, :] for m in range(4)]
                absorb = a[0] * planes[0] + a[1] * planes[1] + a[2] * planes[2] + a[3] * planes[3]
                phase = b[0] * planes[0] + b[1] * planes[1] + b[2] * planes[2] + b[3] * planes[3]
                damping = jnp.exp(-absorb)
                c, sn = sincos_turns(phase * (0.5 / math.pi))
                ore, oim = damping * c, damping * sn
                p_re, p_im = pb[s, 0, rows, :], pb[s, 1, rows, :]
                x = p_re * ore - p_im * oim
                y = p_re * oim + p_im * ore
                pr[s, rows, :] = x
                pi[s, rows, :] = y
                psib[s, rows, :] = x.astype(BF16)
                psib[s, pl.ds(length + r, 32), :] = y.astype(BF16)
                power[rows, :] = power[rows, :] + spec * (x * x + y * y)
            return carry

        lax.fori_loop(0, slots, body, 0)

    def forward(rows_at, fr, fi, total):
        rows = pl.ds(pl.multiple_of(rows_at, mid), mid)
        low_rows = pl.ds(pl.multiple_of(rows_at + length, mid), mid)
        total[rows, :] = jnp.zeros((mid, length), F32)

        def body(s, carry):
            left = jnp.concatenate([w1[s, rows, :], w1[s, low_rows, :]], axis=0)
            m = jnp.dot(left, psib[s], preferred_element_type=F32).astype(BF16)
            m = jnp.concatenate([m[:mid], m[mid:]], axis=1)
            far = jnp.dot(m, w2[s], preferred_element_type=F32)
            x, y = far[:, :length], far[:, length:]
            fr[s, rows, :] = x
            fi[s, rows, :] = y
            total[rows, :] = total[rows, :] + spec_ref[s] * (x * x + y * y)
            return carry

        lax.fori_loop(0, slots, body, 0)

    def back_left(short, fr, fi):
        def body(s, carry):
            factor = spec_ref[s] * short[...]
            d = jnp.concatenate(
                [(factor * fr[s]).astype(BF16), (factor * fi[s]).astype(BF16)], axis=0
            )
            nb = jnp.dot(w2[s], d, preferred_element_type=F32).astype(BF16)
            nbuf[s] = jnp.concatenate([nb[:length], nb[length:]], axis=1)
            return carry

        lax.fori_loop(0, slots, body, 0)

    def back_right(rows_at, pr, pi, into):
        rows = pl.ds(pl.multiple_of(rows_at, mid), mid)
        for m in range(4):
            into[m, rows, :] = jnp.zeros((mid, length), F32)

        def body(s, carry):
            a, b = coefficients(s)
            back = jnp.dot(nbuf[s, rows, :], w1[s], preferred_element_type=F32)
            br, bi = back[:, :length], back[:, length:]
            x, y = pr[s, rows, :], pi[s, rows, :]
            cr = x * br + y * bi
            ci = x * bi - y * br
            for m in range(4):
                into[m, rows, :] = into[m, rows, :] + (b[m] * ci - a[m] * cr)
            return carry

        lax.fori_loop(0, slots, body, 0)

    at_mine, at_other = core * mid, (1 - core) * mid
    frames_here = jnp.where(last, 1.0, 2.0)
    top32, low32 = pl.ds(0, mid // 2), pl.ds(mid // 2, mid // 2)

    def pack_right(y):
        return jnp.where(lane_low32, swap(y[: mid // 2]), y[mid // 2 :])

    def pack_left(y):
        return jnp.where(lane_low32, y[: mid // 2], swap(y[mid // 2 :]))

    sx_in1 = remote(XIN1, intenx.at[other], intenx_r, (t, mate))
    sx_in2 = remote(XIN2, half_ix, half_rx, (t, far_z))
    sx_sf = remote(XSF, sfx.at[mine], sfx.at[mine], (t, mate))
    sx_pw1 = remote(XPW1, accx.at[4, other], accx_r.at[4], (t, mate))
    sx_pwb = remote(XPWB, rpx.at[4], rb.at[4], (t, far_z))
    sx_gr1 = remote(XGR1, accx.at[pl.ds(0, 4), other], accx_r.at[pl.ds(0, 4)], (t, mate))
    sx_grb = remote(XGRB, rpx.at[pl.ds(0, 4)], rb.at[pl.ds(0, 4)], (t, far_z))

    load_probe.wait()

    @pl.when(first)
    def _():
        for m in range(4):
            for r in (0, mid):
                winx[m, pl.ds(r, mid), :] = jnp.where(lane_low, 0.0, swap(mp[m, pl.ds(r, mid), :]))
        waves_at_object(winx, psirx, psiix, accx.at[4])
        sx_pw1.start()
        forward(at_other, farrx, farix, intenx)
        sx_in1.start()
        forward(at_mine, farrx, farix, intenx)
        sx_in1.wait_recv()
        half_ix[...] = intenx[mine, :] + intenx_r[...]
        sx_in2.start()
        sx_pw1.wait_recv()
        power = pack_right(accx[4, mine, :] + accx_r[4])
        rpx[4] = power
        sx_pwb.start()

    @pl.when(t < tiles - 1)
    def _():
        send_halo.wait_recv()

    for m in range(4):
        h = halo_r[m]
        win[m, 0:mid, :] = swap(jnp.where(lane_low, h, mp[m, 0:mid]))
        win[m, mid:length, :] = jnp.where(lane_low, swap(mp[m, mid:length]), h)

    s_pw1 = remote(PW1, acc.at[4, other], acc_r.at[4], (t, mate))
    s_in1 = remote(IN1, inten.at[other], inten_r, (t, mate))
    s_in2 = remote(IN2, half_i, half_r, (t, far_z))
    s_sf = remote(SF, sf.at[mine], sf.at[mine], (t, mate))
    s_gr1 = remote(GR1, acc.at[pl.ds(0, 4), other], acc_r.at[pl.ds(0, 4)], (t, mate))
    s_pwl = remote(PWL, lpack.at[4], lrecv.at[4], (t, far_z))
    s_pwa = remote(PWA, rpack.at[4], ra.at[4], (up, w))
    s_pwb = remote(PWB, rpack.at[4], rb.at[4], (up, far_z))
    four = pl.ds(0, 4)
    s_grl = remote(GRL, lpack.at[four], lrecv.at[four], (t, far_z))
    s_gra = remote(GRA, rpack.at[four], ra.at[four], (up, w))
    s_grb = remote(GRB, rpack.at[four], rb.at[four], (up, far_z))

    waves_at_object(win, psir, psii, acc.at[4])
    s_pw1.start()
    forward(at_other, farr, fari, inten)
    s_in1.start()
    forward(at_mine, farr, fari, inten)
    s_in1.wait_recv()
    half_i[...] = inten[mine, :] + inten_r[...]
    s_in2.start()

    s_pw1.wait_recv()
    power = frames_here * (acc[4, mine, :] + acc_r[4])
    lpack[4] = pack_left(power)
    rpack[4] = pack_right(power)
    s_pwl.start()

    @pl.when(t < tiles - 1)
    def _():
        s_pwa.start()
        s_pwb.start()

    @pl.when(first)
    def _():
        sx_in2.wait_recv()
        inv = 1.0 / jnp.maximum(half_ix[...] + half_rx[...], FLOOR)
        sfx[mine, :] = jnp.sqrt(ma_s[mine, :] * inv) - 1.0
        sx_sf.start()
        sx_sf.wait_recv()
        back_left(sfx, farrx, farix)
        back_right(at_other, psirx, psiix, accx)
        sx_gr1.start()
        back_right(at_mine, psirx, psiix, accx)
        sx_gr1.wait_recv()
        for m in range(4):
            rpx[m] = pack_right(accx[m, mine, :] + accx_r[m])
        sx_grb.start()

    @pl.when(t < tiles - 1)
    def _():
        send_meas.wait_recv()

    s_in2.wait_recv()
    inv = 1.0 / jnp.maximum(half_i[...] + half_r[...], FLOOR)
    sf[mine, :] = jnp.sqrt(ms[1, mine, :] * inv) + jnp.sqrt(ma_r[...] * inv) - frames_here
    s_sf.start()
    s_sf.wait_recv()
    back_left(sf, farr, fari)
    back_right(at_other, psir, psii, acc)
    s_gr1.start()
    back_right(at_mine, psir, psii, acc)
    s_gr1.wait_recv()
    for m in range(4):
        y = acc[m, mine, :] + acc_r[m]
        lpack[m] = pack_left(y)
        rpack[m] = pack_right(y)
    s_grl.start()

    @pl.when(t < tiles - 1)
    def _():
        s_gra.start()
        s_grb.start()

    @pl.when(first)
    def _():
        sx_pwb.wait_recv()
        sx_grb.wait_recv()
        ra[...] = rpx[...]

    @pl.when(t > 0)
    def _():
        s_pwa.wait_recv()
        s_pwb.wait_recv()
        s_gra.wait_recv()
        s_grb.wait_recv()

    s_pwl.wait_recv()
    s_grl.wait_recv()

    def totals(m):
        l = lpack[m] + lrecv[m]
        r = ra[m] + rb[m]
        return jnp.where(lane_low32, r, swap(l)), jnp.where(lane_low32, swap(r), l)

    powers = [RELAX / (p + 1.0) for p in totals(4)]
    for m in range(4):
        for q, total in enumerate(totals(m)):
            rows = pl.ds(pl.multiple_of(at_mine + q * (mid // 2), mid // 2), mid // 2)
            out_ref[m, rows, :] = mp[m, rows, :] + total * powers[q]
    s_out = remote(OUT, out_ref.at[:, mine], out_ref.at[:, mine], (t, mate))
    s_out.start()
    s_out.wait_recv()

    for copy in (s_pw1, s_in1, s_in2, s_sf, s_gr1, s_pwl, s_grl, s_out):
        copy.wait_send()

    @pl.when(t > 0)
    def _():
        send_halo.wait_send()
        send_meas.wait_send()

    @pl.when(t < tiles - 1)
    def _():
        for copy in (s_pwa, s_pwb, s_gra, s_grb):
            copy.wait_send()

    @pl.when(first)
    def _():
        for copy in (sx_in1, sx_in2, sx_sf, sx_pw1, sx_pwb, sx_gr1, sx_grb):
            copy.wait_send()


def per_device(tiles, maps, measured, offsets, probe, spectrum, wave_index, edge_band, band_coef):
    _, length, columns = maps.shape
    slots = spectrum.shape[0]
    mid = length // 2
    vmem = lambda *shape: pltpu.VMEM(shape, F32)
    vmem16 = lambda *shape: pltpu.VMEM(shape, BF16)
    plane = (length, length)
    half = (mid, length)
    quarter = (mid // 2, length)
    scratch = [
        vmem(4, *plane), vmem(2, *plane), vmem(slots, 2, *plane),
        vmem16(slots, 2 * length, 2 * length), vmem16(slots, 2 * length, 2 * length),
        vmem(4, *plane), vmem(4, *plane),
        vmem(slots, *plane), vmem(slots, *plane), vmem16(slots, 2 * length, length),
        vmem(slots, *plane), vmem(slots, *plane),
        vmem(slots, *plane), vmem(slots, *plane), vmem(slots, *plane), vmem(slots, *plane),
        vmem16(slots, length, 2 * length),
        vmem(4, *half), vmem(4, *half), vmem(*plane), vmem(*half),
        vmem(*plane), vmem(*half), vmem(*half), vmem(*half), vmem(*plane),
        vmem(*plane), vmem(*half), vmem(*half), vmem(*half), vmem(*plane),
        vmem(5, *plane), vmem(5, *half), vmem(5, *plane), vmem(5, *half),
        vmem(5, *quarter), vmem(5, *quarter), vmem(5, *quarter), vmem(5, *quarter),
        vmem(5, *quarter), vmem(5, *quarter),
        pltpu.SemaphoreType.DMA((3,)),
        pltpu.SemaphoreType.DMA((MESSAGES,)),
        pltpu.SemaphoreType.DMA((MESSAGES,)),
    ]
    hbm = pl.BlockSpec(memory_space=pl.ANY)
    smem = pl.BlockSpec(memory_space=pltpu.SMEM)
    return pl.pallas_call(
        functools.partial(kernel, tiles),
        out_shape=jax.ShapeDtypeStruct(maps.shape, F32),
        in_specs=[hbm, hbm, smem, hbm, smem, smem, smem, smem],
        out_specs=pl.BlockSpec(memory_space=pltpu.VMEM),
        scratch_shapes=scratch,
        compiler_params=pltpu.CompilerParams(
            collective_id=0, has_side_effects=True, vmem_limit_bytes=56 << 20
        ),
    )(maps, measured, offsets, probe, spectrum, wave_index, edge_band, band_coef)


def solution(mesh):
    in_specs = (
        P(None, None, "tile"),
        P("tile", None, None),
        P("tile"),
        P("wave", None, None, None),
        P("wave"),
        P("wave"),
        P("wave", None),
        P(),
    )
    return jax.shard_map(
        functools.partial(per_device, mesh.shape["tile"]),
        mesh=mesh,
        in_specs=in_specs,
        out_specs=P(None, None, "tile"),
        check_vma=False,
    )
```

```python
import functools
import math

import jax
import jax.numpy as jnp
from jax import lax
from jax.experimental import pallas as pl
from jax.experimental.pallas import tpu as pltpu
from jax.sharding import PartitionSpec as P

WAVES = 48
RELAX = 4.0
FLOOR = 1.0
MESH = pl.DeviceIdType.MESH
F32 = jnp.float32
BF16 = jnp.bfloat16

SIN = (6.283184916495429, -41.341589232688364, 81.5999433297776, -76.61447253120122, 41.34288235437901, -12.471243534763557)
COS = (0.9999999890590201, -19.739204499453688, 64.93911745988827, -85.45013953077586, 60.16763095018129, -25.96759924584206, 6.528658157862129)

MEAS, PW1, PWL, PWA, PWB, IN1, IN2, SF, GR1, GRL, GRA, GRB, OUT = range(13)
XIN1, XIN2, XSF, XPW1, XPWB, XGR1, XGRB = range(13, 20)
HALO = 20
CHUNKS = 4
MESSAGES = HALO + CHUNKS


def sincos_turns(turns):
    f = turns - jnp.round(turns)
    z = f * f
    s = jnp.full_like(z, SIN[-1])
    for k in SIN[-2::-1]:
        s = s * z + k
    c = jnp.full_like(z, COS[-1])
    for k in COS[-2::-1]:
        c = c * z + k
    return c, s * f


def swap(x):
    return pltpu.roll(x, 64, x.ndim - 1)


def kernel(
    tiles,
    maps_hbm, meas_hbm, off_ref, probe_hbm, spec_ref, wave_ref, edge_ref, band_ref,
    out_ref,
    mp, ms, pb, w1, w2, win, psir, psii, psib, midb, farr, fari, psirx, psiix, farrx, farix, nbuf,
    halo_s, halo_r, ma_s, ma_r,
    inten, inten_r, half_i, half_r, sf, intenx, intenx_r, half_ix, half_rx, sfx,
    acc, acc_r, accx, accx_r,
    lpack, lrecv, rpack, ra, rb, rpx,
    coef, copy_sem, send_sem, recv_sem,
):
    slots = spec_ref.shape[0]
    length = out_ref.shape[1]
    mid = length // 2
    chunk = length // CHUNKS
    t = lax.axis_index("tile")
    w = lax.axis_index("wave")
    core = lax.rem(w, 2)
    mate = w + 1 - 2 * core
    far_z = lax.rem(w + 2, 4)
    up = lax.rem(t + 1, tiles)
    down = lax.rem(t + tiles - 1, tiles)
    first = t == 0
    last = t == tiles - 1
    has_down = t > 0
    has_up = t < tiles - 1

    mine = pl.ds(pl.multiple_of(core * mid, mid), mid)
    other = pl.ds(pl.multiple_of((1 - core) * mid, mid), mid)

    barrier = pltpu.get_barrier_semaphore()

    def greet(device):
        pl.semaphore_signal(barrier, inc=1, device_id=device, device_id_type=MESH)

    greet((t, mate))
    greet((t, far_z))

    @pl.when(has_down)
    def _():
        greet((down, w))

    @pl.when(has_up)
    def _():
        greet((up, w))

    load_maps = pltpu.make_async_copy(maps_hbm, mp, copy_sem.at[0])
    load_meas = pltpu.make_async_copy(meas_hbm, ms, copy_sem.at[1])
    load_probe = pltpu.make_async_copy(probe_hbm, pb, copy_sem.at[2])
    load_maps.start()
    load_meas.start()
    load_probe.start()

    def remote(k, src, dst, device):
        return pltpu.make_async_remote_copy(
            src_ref=src, dst_ref=dst, send_sem=send_sem.at[k], recv_sem=recv_sem.at[k],
            device_id=device, device_id_type=MESH,
        )

    def low_lanes(rows):
        return lax.broadcasted_iota(jnp.int32, (rows, length), 1) < mid

    def slot_coefficients(s, carry):
        for m in range(4):
            e = edge_ref[m, s]
            for k in range(2):
                c = [band_ref[n, k, m] for n in range(3)]
                coef[s, 4 * k + m] = jnp.where(e == 0, c[0], jnp.where(e == 1, c[1], c[2]))
        return carry

    lax.fori_loop(0, slots, slot_coefficients, 0)

    column = lax.broadcasted_iota(jnp.int32, (32, length), 1) - mid
    row = lax.broadcasted_iota(jnp.int32, (32, length), 0) - mid
    normaliser = 1.0 / math.sqrt(length)

    def table_slot(s, carry):
        which = jnp.full((32, length), wave_ref[s], jnp.int32).astype(F32)
        sampling = (0.6 + 0.4 * which / (WAVES - 1)) * (1.0 / length)
        for r in range(0, length, 32):
            c, sn = sincos_turns(sampling * ((row + r) * column).astype(F32))
            re = (c * normaliser).astype(BF16)
            sn = sn * normaliser
            im = (-sn).astype(BF16)
            nim = sn.astype(BF16)
            top, low = pl.ds(r, 32), pl.ds(length + r, 32)
            left, right = pl.ds(0, length), pl.ds(length, length)
            w1[s, top, left] = re
            w1[s, top, right] = nim
            w1[s, low, left] = im
            w1[s, low, right] = re
            w2[s, top, left] = re
            w2[s, top, right] = im
            w2[s, low, left] = nim
            w2[s, low, right] = re
        return carry

    load_maps.wait()
    for q in range(CHUNKS):
        r = q * chunk
        for m in range(4):
            halo_s[q, m] = jnp.where(
                low_lanes(chunk // 2), mp[m, r : r + chunk // 2], swap(mp[m, r + chunk // 2 : r + chunk])
            )
    lax.fori_loop(0, slots, table_slot, 0)

    pl.semaphore_wait(barrier, 2 + (t + tiles - 1) // tiles + (2 * tiles - 2 - t) // tiles)

    send_halo = [remote(HALO + q, halo_s.at[q], halo_r.at[q], (down, w)) for q in range(CHUNKS)]

    @pl.when(has_down)
    def _():
        for copy in send_halo:
            copy.start()

    load_meas.wait()
    low_first = off_ref[0] < off_ref[1]
    for r in range(0, length, 32):
        rows = pl.ds(r, 32)
        one, two = ms[0, rows, :], ms[1, rows, :]
        ma_s[rows, :] = jnp.where(low_first, one, two)
        ms[1, rows, :] = jnp.where(low_first, two, one)

    send_meas = remote(MEAS, ma_s.at[mine], ma_r, (down, w))

    @pl.when(has_down)
    def _():
        send_meas.start()

    @pl.when(last)
    def _():
        halo_r[...] = jnp.zeros_like(halo_r)
        ma_r[...] = jnp.zeros_like(ma_r)

    def groups(size, body, carry):
        def step(i, carry):
            return body([i * size + j for j in range(size)], carry)

        return lax.fori_loop(0, slots // size, step, carry)

    def waves_at_object(r, pr, pi, power):
        rows, low_rows = pl.ds(r, chunk), pl.ds(length + r, chunk)

        def body(group, total):
            for s in group:
                a = [coef[s, m] for m in range(4)]
                b = [coef[s, 4 + m] for m in range(4)]
                planes = [win[m, rows, :] for m in range(4)]
                absorb = a[0] * planes[0] + a[1] * planes[1] + a[2] * planes[2] + a[3] * planes[3]
                phase = b[0] * planes[0] + b[1] * planes[1] + b[2] * planes[2] + b[3] * planes[3]
                damping = jnp.exp(-absorb)
                c, sn = sincos_turns(phase * (0.5 / math.pi))
                ore, oim = damping * c, damping * sn
                p_re, p_im = pb[s, 0, rows, :], pb[s, 1, rows, :]
                x = p_re * ore - p_im * oim
                y = p_re * oim + p_im * ore
                pr[s, rows, :] = x
                pi[s, rows, :] = y
                psib[s, rows, :] = x.astype(BF16)
                psib[s, low_rows, :] = y.astype(BF16)
                total = total + spec_ref[s] * (x * x + y * y)
            return total

        power[rows, :] = groups(2, body, jnp.zeros((chunk, length), F32))

    def left_forward():
        def body(group, carry):
            for s in group:
                m = jnp.dot(w1[s], psib[s], preferred_element_type=F32).astype(BF16)
                midb[s, :, 0:length] = m[:length]
                midb[s, :, length : 2 * length] = m[length:]
            return carry

        groups(4, body, 0)

    def right_forward(rows_at, fr, fi, total):
        rows = pl.ds(pl.multiple_of(rows_at, mid), mid)

        def body(group, light):
            for s in group:
                far = jnp.dot(midb[s, rows, :], w2[s], preferred_element_type=F32)
                x, y = far[:, :length], far[:, length:]
                fr[s, rows, :] = x
                fi[s, rows, :] = y
                light = light + spec_ref[s] * (x * x + y * y)
            return light

        total[rows, :] = groups(4, body, jnp.zeros((mid, length), F32))

    def back_left(short, fr, fi):
        def body(group, carry):
            for s in group:
                factor = spec_ref[s] * short[...]
                d = jnp.concatenate(
                    [(factor * fr[s]).astype(BF16), (factor * fi[s]).astype(BF16)], axis=0
                )
                nb = jnp.dot(w2[s], d, preferred_element_type=F32).astype(BF16)
                nbuf[s, :, 0:length] = nb[:length]
                nbuf[s, :, length : 2 * length] = nb[length:]
            return carry

        groups(4, body, 0)

    def back_right(rows_at, pr, pi, into):
        rows = pl.ds(pl.multiple_of(rows_at, mid), mid)
        for m in range(4):
            into[m, rows, :] = jnp.zeros((mid, length), F32)

        def body(group, carry):
            back = [jnp.dot(nbuf[s, rows, :], w1[s], preferred_element_type=F32) for s in group]
            for r in range(0, mid, 16):
                part = pl.ds(pl.multiple_of(rows_at + r, 16), 16)
                sums = [into[m, part, :] for m in range(4)]
                for s, both in zip(group, back):
                    br, bi = both[r : r + 16, :length], both[r : r + 16, length:]
                    x, y = pr[s, part, :], pi[s, part, :]
                    cr = x * br + y * bi
                    ci = x * bi - y * br
                    for m in range(4):
                        sums[m] = sums[m] + (coef[s, 4 + m] * ci - coef[s, m] * cr)
                for m in range(4):
                    into[m, part, :] = sums[m]
            return carry

        groups(3, body, 0)

    at_mine, at_other = core * mid, (1 - core) * mid
    frames_here = jnp.where(last, 1.0, 2.0)
    quarter = mid // 2

    def pack_right(y):
        return jnp.where(low_lanes(quarter), swap(y[:quarter]), y[quarter:])

    def pack_left(y):
        return jnp.where(low_lanes(quarter), y[:quarter], swap(y[quarter:]))

    four = pl.ds(0, 4)
    sx_in1 = remote(XIN1, intenx.at[other], intenx_r, (t, mate))
    sx_in2 = remote(XIN2, half_ix, half_rx, (t, far_z))
    sx_sf = remote(XSF, sfx.at[mine], sfx.at[mine], (t, mate))
    sx_pw1 = remote(XPW1, accx.at[4, other], accx_r.at[4], (t, mate))
    sx_pwb = remote(XPWB, rpx.at[4], rb.at[4], (t, far_z))
    sx_gr1 = remote(XGR1, accx.at[four, other], accx_r.at[four], (t, mate))
    sx_grb = remote(XGRB, rpx.at[four], rb.at[four], (t, far_z))

    load_probe.wait()

    @pl.when(first)
    def _():
        for m in range(4):
            for r in (0, mid):
                win[m, pl.ds(r, mid), :] = jnp.where(low_lanes(mid), 0.0, swap(mp[m, pl.ds(r, mid), :]))

        def one_chunk(q, carry):
            waves_at_object(pl.multiple_of(q * chunk, chunk), psirx, psiix, accx.at[4])
            return carry

        lax.fori_loop(0, CHUNKS, one_chunk, 0)
        sx_pw1.start()
        left_forward()
        right_forward(at_other, farrx, farix, intenx)
        sx_in1.start()
        right_forward(at_mine, farrx, farix, intenx)
        sx_in1.wait_recv()
        half_ix[...] = intenx[mine, :] + intenx_r[...]
        sx_in2.start()
        sx_pw1.wait_recv()
        rpx[4] = pack_right(accx[4, mine, :] + accx_r[4])
        sx_pwb.start()

    for q in range(CHUNKS):

        @pl.when(has_up)
        def _():
            send_halo[q].wait_recv()

        r, h2 = q * chunk, chunk // 2
        for m in range(4):
            h = halo_r[q, m]
            win[m, r : r + h2, :] = swap(jnp.where(low_lanes(h2), h, mp[m, r : r + h2]))
            win[m, r + h2 : r + chunk, :] = jnp.where(low_lanes(h2), swap(mp[m, r + h2 : r + chunk]), h)
        waves_at_object(r, psir, psii, acc.at[4])

    s_pw1 = remote(PW1, acc.at[4, other], acc_r.at[4], (t, mate))
    s_in1 = remote(IN1, inten.at[other], inten_r, (t, mate))
    s_in2 = remote(IN2, half_i, half_r, (t, far_z))
    s_sf = remote(SF, sf.at[mine], sf.at[mine], (t, mate))
    s_gr1 = remote(GR1, acc.at[four, other], acc_r.at[four], (t, mate))
    s_pwl = remote(PWL, lpack.at[4], lrecv.at[4], (t, far_z))
    s_pwa = remote(PWA, rpack.at[4], ra.at[4], (up, w))
    s_pwb = remote(PWB, rpack.at[4], rb.at[4], (up, far_z))
    s_grl = remote(GRL, lpack.at[four], lrecv.at[four], (t, far_z))
    s_gra = remote(GRA, rpack.at[four], ra.at[four], (up, w))
    s_grb = remote(GRB, rpack.at[four], rb.at[four], (up, far_z))

    s_pw1.start()
    left_forward()
    right_forward(at_other, farr, fari, inten)
    s_in1.start()
    right_forward(at_mine, farr, fari, inten)
    s_in1.wait_recv()
    half_i[...] = inten[mine, :] + inten_r[...]
    s_in2.start()

    @pl.when(first)
    def _():
        sx_in2.wait_recv()
        inv = 1.0 / jnp.maximum(half_ix[...] + half_rx[...], FLOOR)
        sfx[mine, :] = jnp.sqrt(ma_s[mine, :] * inv) - 1.0
        sx_sf.start()

    s_pw1.wait_recv()
    power = frames_here * (acc[4, mine, :] + acc_r[4])
    lpack[4] = pack_left(power)
    rpack[4] = pack_right(power)

    @pl.when(first)
    def _():
        sx_sf.wait_recv()
        back_left(sfx, farrx, farix)
        back_right(at_other, psirx, psiix, accx)
        sx_gr1.start()
        back_right(at_mine, psirx, psiix, accx)
        sx_gr1.wait_recv()
        for m in range(4):
            rpx[m] = pack_right(accx[m, mine, :] + accx_r[m])
        sx_grb.start()

    @pl.when(has_up)
    def _():
        send_meas.wait_recv()

    s_in2.wait_recv()
    inv = 1.0 / jnp.maximum(half_i[...] + half_r[...], FLOOR)
    sf[mine, :] = jnp.sqrt(ms[1, mine, :] * inv) + jnp.sqrt(ma_r[...] * inv) - frames_here
    s_sf.start()
    s_pwl.start()

    @pl.when(has_up)
    def _():
        s_pwa.start()
        s_pwb.start()

    s_sf.wait_recv()
    back_left(sf, farr, fari)
    back_right(at_other, psir, psii, acc)
    s_gr1.start()
    back_right(at_mine, psir, psii, acc)
    s_gr1.wait_recv()
    for m in range(4):
        y = acc[m, mine, :] + acc_r[m]
        lpack[m] = pack_left(y)
        rpack[m] = pack_right(y)
    s_grl.start()

    @pl.when(has_up)
    def _():
        s_gra.start()
        s_grb.start()

    @pl.when(first)
    def _():
        sx_pwb.wait_recv()
        sx_grb.wait_recv()
        ra[...] = rpx[...]

    @pl.when(has_down)
    def _():
        s_pwa.wait_recv()
        s_pwb.wait_recv()
        s_gra.wait_recv()
        s_grb.wait_recv()

    s_pwl.wait_recv()
    s_grl.wait_recv()

    def totals(m):
        l = lpack[m] + lrecv[m]
        r = ra[m] + rb[m]
        return jnp.where(low_lanes(quarter), r, swap(l)), jnp.where(low_lanes(quarter), swap(r), l)

    powers = [RELAX / (p + 1.0) for p in totals(4)]
    for m in range(4):
        for q, total in enumerate(totals(m)):
            rows = pl.ds(pl.multiple_of(at_mine + q * quarter, quarter), quarter)
            out_ref[m, rows, :] = mp[m, rows, :] + total * powers[q]
    s_out = remote(OUT, out_ref.at[:, mine], out_ref.at[:, mine], (t, mate))
    s_out.start()
    s_out.wait_recv()

    for copy in (s_pw1, s_in1, s_in2, s_sf, s_gr1, s_pwl, s_grl, s_out):
        copy.wait_send()

    @pl.when(has_down)
    def _():
        for copy in (*send_halo, send_meas):
            copy.wait_send()

    @pl.when(has_up)
    def _():
        for copy in (s_pwa, s_pwb, s_gra, s_grb):
            copy.wait_send()

    @pl.when(first)
    def _():
        for copy in (sx_in1, sx_in2, sx_sf, sx_pw1, sx_pwb, sx_gr1, sx_grb):
            copy.wait_send()


def per_device(tiles, maps, measured, offsets, probe, spectrum, wave_index, edge_band, band_coef):
    _, length, columns = maps.shape
    slots = spectrum.shape[0]
    mid = length // 2
    vmem = lambda *shape: pltpu.VMEM(shape, F32)
    vmem16 = lambda *shape: pltpu.VMEM(shape, BF16)
    plane = (length, length)
    half = (mid, length)
    quarter = (mid // 2, length)
    halo = vmem(CHUNKS, 4, length // CHUNKS // 2, length)
    scratch = [
        vmem(4, *plane), vmem(2, *plane), vmem(slots, 2, *plane),
        vmem16(slots, 2 * length, 2 * length), vmem16(slots, 2 * length, 2 * length),
        vmem(4, *plane),
        vmem(slots, *plane), vmem(slots, *plane), vmem16(slots, 2 * length, length),
        vmem16(slots, length, 2 * length),
        vmem(slots, *plane), vmem(slots, *plane),
        vmem(slots, *plane), vmem(slots, *plane), vmem(slots, *plane), vmem(slots, *plane),
        vmem16(slots, length, 2 * length),
        halo, halo, vmem(*plane), vmem(*half),
        vmem(*plane), vmem(*half), vmem(*half), vmem(*half), vmem(*plane),
        vmem(*plane), vmem(*half), vmem(*half), vmem(*half), vmem(*plane),
        vmem(5, *plane), vmem(5, *half), vmem(5, *plane), vmem(5, *half),
        vmem(5, *quarter), vmem(5, *quarter), vmem(5, *quarter), vmem(5, *quarter),
        vmem(5, *quarter), vmem(5, *quarter),
        pltpu.SMEM((slots, 8), F32),
        pltpu.SemaphoreType.DMA((3,)),
        pltpu.SemaphoreType.DMA((MESSAGES,)),
        pltpu.SemaphoreType.DMA((MESSAGES,)),
    ]
    hbm = pl.BlockSpec(memory_space=pl.ANY)
    smem = pl.BlockSpec(memory_space=pltpu.SMEM)
    return pl.pallas_call(
        functools.partial(kernel, tiles),
        out_shape=jax.ShapeDtypeStruct(maps.shape, F32),
        in_specs=[hbm, hbm, smem, hbm, smem, smem, smem, smem],
        out_specs=pl.BlockSpec(memory_space=pltpu.VMEM),
        scratch_shapes=scratch,
        compiler_params=pltpu.CompilerParams(
            collective_id=0, has_side_effects=True, vmem_limit_bytes=56 << 20
        ),
    )(maps, measured, offsets, probe, spectrum, wave_index, edge_band.T, band_coef.transpose(1, 0, 2))


def solution(mesh):
    in_specs = (
        P(None, None, "tile"),
        P("tile", None, None),
        P("tile"),
        P("wave", None, None, None),
        P("wave"),
        P("wave"),
        P("wave", None),
        P(),
    )
    return jax.shard_map(
        functools.partial(per_device, mesh.shape["tile"]),
        mesh=mesh,
        in_specs=in_specs,
        out_specs=P(None, None, "tile"),
        check_vma=False,
    )
```

```python
import functools
import math

import jax
import jax.numpy as jnp
from jax import lax
from jax.experimental import pallas as pl
from jax.experimental.pallas import tpu as pltpu
from jax.sharding import PartitionSpec as P

WAVES = 48
RELAX = 4.0
FLOOR = 1.0
MESH = pl.DeviceIdType.MESH
F32 = jnp.float32
BF16 = jnp.bfloat16

SIN = (6.283184916495429, -41.341589232688364, 81.5999433297776, -76.61447253120122, 41.34288235437901, -12.471243534763557)
COS = (0.9999999890590201, -19.739204499453688, 64.93911745988827, -85.45013953077586, 60.16763095018129, -25.96759924584206, 6.528658157862129)

MEAS, PW1, PWL, PWA, PWB, IN1, IN2, SF, GR1, GRL, GRA, GRB, OUT = range(13)
XIN1, XIN2, XSF, XPW1, XPWB, XGR1, XGRB = range(13, 20)
LHALO, LMEAS, LPASS = 20, 21, 22
HALO = 23
CHUNKS = 4
PASS = HALO + CHUNKS
MESSAGES = PASS + CHUNKS


def sincos_turns(turns):
    f = turns - jnp.round(turns)
    z = f * f
    s = jnp.full_like(z, SIN[-1])
    for k in SIN[-2::-1]:
        s = s * z + k
    c = jnp.full_like(z, COS[-1])
    for k in COS[-2::-1]:
        c = c * z + k
    return c, s * f


def swap(x):
    return pltpu.roll(x, 64, x.ndim - 1)


def kernel(
    tiles,
    maps_hbm, meas_hbm, off_ref, probe_hbm, spec_ref, wave_ref, edge_ref, band_ref,
    out_ref,
    mp, ms, pb, w1, w2, obj, psir, psii, psib, midb, farr, fari, psirx, psiix, farrx, farix, nbuf,
    halo_s, halo_r, right_s, left_r, ma_s, ma_r, mb_r,
    inten, inten_r, half_i, half_r, sf, intenx, intenx_r, half_ix, half_rx, sfx,
    acc, acc_r, accx, accx_r,
    lpack, lrecv, rpack, ra, rb, rpx,
    coef, copy_sem, send_sem, recv_sem,
):
    slots = spec_ref.shape[0]
    length = mp.shape[1]
    mid = length // 2
    chunk = length // CHUNKS
    t = lax.axis_index("tile")
    w = lax.axis_index("wave")
    core = lax.rem(w, 2)
    mate = w + 1 - 2 * core
    far_z = lax.rem(w + 2, 4)
    up = lax.rem(t + 1, tiles)
    down = lax.rem(t + tiles - 1, tiles)
    first = t == 0
    last = t == tiles - 1
    has_down = t > 0
    has_up = t < tiles - 1
    extra = lax.rem(t, tiles // 2) == 0
    next_extra = lax.rem(t + 1, tiles // 2) == 0

    mine = pl.ds(pl.multiple_of(core * mid, mid), mid)
    other = pl.ds(pl.multiple_of((1 - core) * mid, mid), mid)

    barrier = pltpu.get_barrier_semaphore()

    def greet(device):
        pl.semaphore_signal(barrier, inc=1, device_id=device, device_id_type=MESH)

    greet((t, mate))
    greet((t, far_z))

    @pl.when(has_down)
    def _():
        greet((down, w))

    @pl.when(has_up)
    def _():
        greet((up, w))

    load_maps = pltpu.make_async_copy(maps_hbm, mp, copy_sem.at[0])
    load_meas = pltpu.make_async_copy(meas_hbm, ms, copy_sem.at[1])
    load_probe = pltpu.make_async_copy(probe_hbm, pb, copy_sem.at[2])
    load_maps.start()
    load_meas.start()
    load_probe.start()

    def remote(k, src, dst, device):
        return pltpu.make_async_remote_copy(
            src_ref=src, dst_ref=dst, send_sem=send_sem.at[k], recv_sem=recv_sem.at[k],
            device_id=device, device_id_type=MESH,
        )

    def low_lanes(rows):
        return lax.broadcasted_iota(jnp.int32, (rows, length), 1) < mid

    def slot_coefficients(s, carry):
        for m in range(4):
            e = edge_ref[m, s]
            for k in range(2):
                c = [band_ref[n, k, m] for n in range(3)]
                coef[s, 4 * k + m] = jnp.where(e == 0, c[0], jnp.where(e == 1, c[1], c[2]))
        return carry

    lax.fori_loop(0, slots, slot_coefficients, 0)

    column = lax.broadcasted_iota(jnp.int32, (32, length), 1) - mid
    row = lax.broadcasted_iota(jnp.int32, (32, length), 0) - mid
    normaliser = 1.0 / math.sqrt(length)

    def table_slot(s, carry):
        which = jnp.full((32, length), wave_ref[s], jnp.int32).astype(F32)
        sampling = (0.6 + 0.4 * which / (WAVES - 1)) * (1.0 / length)
        for r in range(0, length, 32):
            c, sn = sincos_turns(sampling * ((row + r) * column).astype(F32))
            re = (c * normaliser).astype(BF16)
            sn = sn * normaliser
            im = (-sn).astype(BF16)
            nim = sn.astype(BF16)
            top, low = pl.ds(r, 32), pl.ds(length + r, 32)
            left, right = pl.ds(0, length), pl.ds(length, length)
            w1[s, top, left] = re
            w1[s, top, right] = nim
            w1[s, low, left] = im
            w1[s, low, right] = re
            w2[s, top, left] = re
            w2[s, top, right] = im
            w2[s, low, left] = nim
            w2[s, low, right] = re
        return carry

    load_maps.wait()
    hc = chunk // 2
    low_hc = low_lanes(hc)
    for q in range(CHUNKS):
        r = q * chunk
        for m in range(4):
            top, bottom = mp[m, r : r + hc], mp[m, r + hc : r + chunk]
            halo_s[q, m] = jnp.where(low_hc, top, swap(bottom))
            right_s[q, m] = jnp.where(low_hc, swap(top), bottom)
    lax.fori_loop(0, slots, table_slot, 0)

    def groups(size, body, carry):
        def step(i, carry):
            return body([i * size + j for j in range(size)], carry)

        return lax.fori_loop(0, slots // size, step, carry)

    def transmission(s, planes):
        a = [coef[s, m] for m in range(4)]
        b = [coef[s, 4 + m] for m in range(4)]
        absorb = a[0] * planes[0] + a[1] * planes[1] + a[2] * planes[2] + a[3] * planes[3]
        phase = b[0] * planes[0] + b[1] * planes[1] + b[2] * planes[2] + b[3] * planes[3]
        damping = jnp.exp(-absorb)
        c, sn = sincos_turns(phase * (0.5 / math.pi))
        return damping * c, damping * sn

    def left_object(packed):
        def body(group, carry):
            for q in range(CHUNKS):
                planes = [packed[q, m] for m in range(4)]
                for s in group:
                    re, im = transmission(s, planes)
                    obj[s, 0, pl.ds(q * hc, hc), :] = re
                    obj[s, 1, pl.ds(q * hc, hc), :] = im
            return carry

        groups(3, body, 0)

    def waves_at_object(q, packed, pr, pi, power):
        at = pl.ds(q * hc, hc)

        def body(group, totals):
            totals = list(totals)
            planes = [packed[q, m] for m in range(4)]
            for s in group:
                nre, nim = transmission(s, planes)
                ore, oim = obj[s, 0, at, :], obj[s, 1, at, :]
                for half, (re, im) in enumerate((
                    (jnp.where(low_hc, ore, swap(nre)), jnp.where(low_hc, oim, swap(nim))),
                    (jnp.where(low_hc, swap(ore), nre), jnp.where(low_hc, swap(oim), nim)),
                )):
                    rows = pl.ds(q * chunk + half * hc, hc)
                    p_re, p_im = pb[s, 0, rows, :], pb[s, 1, rows, :]
                    x = p_re * re - p_im * im
                    y = p_re * im + p_im * re
                    pr[s, rows, :] = x
                    pi[s, rows, :] = y
                    psib[s, rows, :] = x.astype(BF16)
                    psib[s, pl.ds(length + q * chunk + half * hc, hc), :] = y.astype(BF16)
                    totals[half] = totals[half] + spec_ref[s] * (x * x + y * y)
            return tuple(totals)

        zero = jnp.zeros((hc, length), F32)
        for half, total in enumerate(groups(6, body, (zero, zero))):
            power[pl.ds(q * chunk + half * hc, hc), :] = total

    def left_forward():
        def body(group, carry):
            for s in group:
                m = jnp.dot(w1[s], psib[s], preferred_element_type=F32).astype(BF16)
                midb[s, :, 0:length] = m[:length]
                midb[s, :, length : 2 * length] = m[length:]
            return carry

        groups(6, body, 0)

    def right_forward(rows_at, fr, fi, total):
        rows = pl.ds(pl.multiple_of(rows_at, mid), mid)

        def body(group, light):
            for s in group:
                far = jnp.dot(midb[s, rows, :], w2[s], preferred_element_type=F32)
                x, y = far[:, :length], far[:, length:]
                fr[s, rows, :] = x
                fi[s, rows, :] = y
                light = light + spec_ref[s] * (x * x + y * y)
            return light

        total[rows, :] = groups(6, body, jnp.zeros((mid, length), F32))

    def back_left(short, fr, fi):
        def body(group, carry):
            for s in group:
                factor = spec_ref[s] * short[...]
                d = jnp.concatenate(
                    [(factor * fr[s]).astype(BF16), (factor * fi[s]).astype(BF16)], axis=0
                )
                nb = jnp.dot(w2[s], d, preferred_element_type=F32).astype(BF16)
                nbuf[s, :, 0:length] = nb[:length]
                nbuf[s, :, length : 2 * length] = nb[length:]
            return carry

        groups(6, body, 0)

    def back_right(rows_at, pr, pi, into):
        rows = pl.ds(pl.multiple_of(rows_at, mid), mid)
        for m in range(4):
            into[m, rows, :] = jnp.zeros((mid, length), F32)

        def body(group, carry):
            back = [jnp.dot(nbuf[s, rows, :], w1[s], preferred_element_type=F32) for s in group]
            for r in range(0, mid, 16):
                part = pl.ds(pl.multiple_of(rows_at + r, 16), 16)
                sums = [into[m, part, :] for m in range(4)]
                for s, both in zip(group, back):
                    br, bi = both[r : r + 16, :length], both[r : r + 16, length:]
                    x, y = pr[s, part, :], pi[s, part, :]
                    cr = x * br + y * bi
                    ci = x * bi - y * br
                    for m in range(4):
                        sums[m] = sums[m] + (coef[s, 4 + m] * ci - coef[s, m] * cr)
                for m in range(4):
                    into[m, part, :] = sums[m]
            return carry

        groups(6, body, 0)

    at_mine, at_other = core * mid, (1 - core) * mid
    frames_here = jnp.where(last, 1.0, 2.0)
    quarter = mid // 2

    def pack_right(y):
        return jnp.where(low_lanes(quarter), swap(y[:quarter]), y[quarter:])

    def pack_left(y):
        return jnp.where(low_lanes(quarter), y[:quarter], swap(y[quarter:]))

    four = pl.ds(0, 4)
    sx_in1 = remote(XIN1, intenx.at[other], intenx_r, (t, mate))
    sx_in2 = remote(XIN2, half_ix, half_rx, (t, far_z))
    sx_sf = remote(XSF, sfx.at[mine], sfx.at[mine], (t, mate))
    sx_pw1 = remote(XPW1, accx.at[4, other], accx_r.at[4], (t, mate))
    sx_pwb = remote(XPWB, rpx.at[4], rb.at[4], (t, far_z))
    sx_gr1 = remote(XGR1, accx.at[four, other], accx_r.at[four], (t, mate))
    sx_grb = remote(XGRB, rpx.at[four], rb.at[four], (t, far_z))

    def extra_objects():
        left_object(left_r)
        for q in range(CHUNKS):
            waves_at_object(q, halo_s, psirx, psiix, accx.at[4])
        left_forward()

    def extra_forward():
        sx_pw1.start()
        right_forward(at_other, farrx, farix, intenx)
        sx_in1.start()
        right_forward(at_mine, farrx, farix, intenx)
        sx_in1.wait_recv()
        half_ix[...] = intenx[mine, :] + intenx_r[...]
        sx_in2.start()
        sx_pw1.wait_recv()
        frames = jnp.where(first, 1.0, 2.0)
        rpx[4] = pack_right(frames * (accx[4, mine, :] + accx_r[4]))

    def extra_shortfall():
        sx_in2.wait_recv()
        frames = jnp.where(first, 1.0, 2.0)
        inv = 1.0 / jnp.maximum(half_ix[...] + half_rx[...], FLOOR)
        sfx[mine, :] = jnp.sqrt(ma_s[mine, :] * inv) + jnp.sqrt(mb_r[...] * inv) - frames
        sx_sf.start()
        sx_pwb.start()

    def extra_backward():
        sx_sf.wait_recv()
        back_left(sfx, farrx, farix)
        back_right(at_other, psirx, psiix, accx)
        sx_gr1.start()
        back_right(at_mine, psirx, psiix, accx)
        sx_gr1.wait_recv()
        for m in range(4):
            rpx[m] = pack_right(accx[m, mine, :] + accx_r[m])
        sx_grb.start()

    @pl.when(first)
    def _():
        left_r[...] = jnp.zeros_like(left_r)
        mb_r[...] = jnp.zeros_like(mb_r)
        load_probe.wait()
        extra_objects()

    @pl.when(last)
    def _():
        halo_r[...] = jnp.zeros_like(halo_r)
        ma_r[...] = jnp.zeros_like(ma_r)

    pl.semaphore_wait(barrier, 2 + (t + tiles - 1) // tiles + (2 * tiles - 2 - t) // tiles)

    fetches = core == 1
    send_halo = [remote(HALO + q, halo_s.at[q], halo_r.at[q], (down, w)) for q in range(CHUNKS)]
    pass_halo = [remote(PASS + q, halo_r.at[q], halo_r.at[q], (t, mate)) for q in range(CHUNKS)]
    send_right = remote(LHALO, right_s, left_r, (up, w))
    pass_right = remote(LPASS, left_r, left_r, (t, mate))
    send_meas = remote(MEAS, ma_s.at[mine], ma_r, (down, w))
    send_meas_up = remote(LMEAS, ms.at[1, mine], mb_r, (up, w))
    sends_right = has_up & next_extra

    @pl.when(fetches & has_down)
    def _():
        for copy in send_halo:
            copy.start()

    @pl.when(fetches & sends_right)
    def _():
        send_right.start()

    load_meas.wait()
    low_first = off_ref[0] < off_ref[1]
    for r in range(0, length, 32):
        rows = pl.ds(r, 32)
        one, two = ms[0, rows, :], ms[1, rows, :]
        ma_s[rows, :] = jnp.where(low_first, one, two)
        ms[1, rows, :] = jnp.where(low_first, two, one)

    @pl.when(has_down)
    def _():
        send_meas.start()

    @pl.when(sends_right)
    def _():
        send_meas_up.start()

    @pl.when(first)
    def _():
        extra_forward()

    left_object(right_s)

    @pl.when(jnp.logical_not(first))
    def _():
        load_probe.wait()

    def arrived(q):
        @pl.when(has_up & fetches)
        def _():
            send_halo[q].wait_recv()
            pass_halo[q].start()

    arrived(0)
    for q in range(CHUNKS):
        if q + 1 < CHUNKS:
            arrived(q + 1)

        @pl.when(has_up & jnp.logical_not(fetches))
        def _():
            pass_halo[q].wait_recv()

        waves_at_object(q, halo_r, psir, psii, acc.at[4])

    s_pw1 = remote(PW1, acc.at[4, other], acc_r.at[4], (t, mate))
    s_in1 = remote(IN1, inten.at[other], inten_r, (t, mate))
    s_in2 = remote(IN2, half_i, half_r, (t, far_z))
    s_sf = remote(SF, sf.at[mine], sf.at[mine], (t, mate))
    s_gr1 = remote(GR1, acc.at[four, other], acc_r.at[four], (t, mate))
    s_pwl = remote(PWL, lpack.at[4], lrecv.at[4], (t, far_z))
    s_pwa = remote(PWA, rpack.at[4], ra.at[4], (up, w))
    s_pwb = remote(PWB, rpack.at[4], rb.at[4], (up, far_z))
    s_grl = remote(GRL, lpack.at[four], lrecv.at[four], (t, far_z))
    s_gra = remote(GRA, rpack.at[four], ra.at[four], (up, w))
    s_grb = remote(GRB, rpack.at[four], rb.at[four], (up, far_z))

    s_pw1.start()
    left_forward()
    right_forward(at_other, farr, fari, inten)
    s_in1.start()
    right_forward(at_mine, farr, fari, inten)
    s_in1.wait_recv()
    half_i[...] = inten[mine, :] + inten_r[...]
    s_in2.start()

    s_pw1.wait_recv()
    power = frames_here * (acc[4, mine, :] + acc_r[4])
    lpack[4] = pack_left(power)
    rpack[4] = pack_right(power)

    extra_late = extra & has_down

    @pl.when(extra_late & fetches)
    def _():
        send_right.wait_recv()
        pass_right.start()

    @pl.when(extra_late & jnp.logical_not(fetches))
    def _():
        pass_right.wait_recv()

    @pl.when(extra_late)
    def _():
        extra_objects()
        extra_forward()

    @pl.when(first)
    def _():
        extra_shortfall()
        extra_backward()

    @pl.when(has_up)
    def _():
        send_meas.wait_recv()

    s_in2.wait_recv()
    inv = 1.0 / jnp.maximum(half_i[...] + half_r[...], FLOOR)
    sf[mine, :] = jnp.sqrt(ms[1, mine, :] * inv) + jnp.sqrt(ma_r[...] * inv) - frames_here
    s_sf.start()
    s_pwl.start()

    rim_up = has_up & jnp.logical_not(next_extra)
    rim_down = jnp.logical_not(extra)

    @pl.when(rim_up)
    def _():
        s_pwa.start()
        s_pwb.start()

    s_sf.wait_recv()
    back_left(sf, farr, fari)
    back_right(at_other, psir, psii, acc)
    s_gr1.start()
    back_right(at_mine, psir, psii, acc)
    s_gr1.wait_recv()
    for m in range(4):
        y = acc[m, mine, :] + acc_r[m]
        lpack[m] = pack_left(y)
        rpack[m] = pack_right(y)
    s_grl.start()

    @pl.when(rim_up)
    def _():
        s_gra.start()
        s_grb.start()

    @pl.when(extra_late)
    def _():
        send_meas_up.wait_recv()
        extra_shortfall()
        extra_backward()

    @pl.when(extra)
    def _():
        sx_pwb.wait_recv()
        sx_grb.wait_recv()
        ra[...] = rpx[...]

    @pl.when(rim_down)
    def _():
        s_pwa.wait_recv()
        s_pwb.wait_recv()
        s_gra.wait_recv()
        s_grb.wait_recv()

    s_pwl.wait_recv()
    s_grl.wait_recv()

    def totals(m):
        l = lpack[m] + lrecv[m]
        r = ra[m] + rb[m]
        return jnp.where(low_lanes(quarter), r, swap(l)), jnp.where(low_lanes(quarter), swap(r), l)

    powers = [RELAX / (p + 1.0) for p in totals(4)]
    for m in range(4):
        for q, total in enumerate(totals(m)):
            rows = pl.ds(pl.multiple_of(at_mine + q * quarter, quarter), quarter)
            out_ref[m, rows, :] = mp[m, rows, :] + total * powers[q]
    s_out = remote(OUT, out_ref.at[:, mine], out_ref.at[:, mine], (t, mate))
    s_out.start()

    for copy in (s_pw1, s_in1, s_in2, s_sf, s_gr1, s_pwl, s_grl):
        copy.wait_send()

    @pl.when(has_down)
    def _():
        send_meas.wait_send()

    @pl.when(has_down & fetches)
    def _():
        for copy in send_halo:
            copy.wait_send()

    @pl.when(has_up & fetches)
    def _():
        for copy in pass_halo:
            copy.wait_send()

    @pl.when(sends_right & fetches)
    def _():
        send_right.wait_send()

    @pl.when(extra_late & fetches)
    def _():
        pass_right.wait_send()

    @pl.when(rim_up)
    def _():
        for copy in (s_pwa, s_pwb, s_gra, s_grb):
            copy.wait_send()

    @pl.when(sends_right)
    def _():
        send_meas_up.wait_send()

    @pl.when(extra)
    def _():
        for copy in (sx_in1, sx_in2, sx_sf, sx_pw1, sx_pwb, sx_gr1, sx_grb):
            copy.wait_send()

    s_out.wait()


def per_device(tiles, maps, measured, offsets, probe, spectrum, wave_index, edge_band, band_coef):
    _, length, columns = maps.shape
    slots = spectrum.shape[0]
    mid = length // 2
    vmem = lambda *shape: pltpu.VMEM(shape, F32)
    vmem16 = lambda *shape: pltpu.VMEM(shape, BF16)
    plane = (length, length)
    half = (mid, length)
    quarter = (mid // 2, length)
    halo = vmem(CHUNKS, 4, length // CHUNKS // 2, length)
    scratch = [
        vmem(4, *plane), vmem(2, *plane), vmem(slots, 2, *plane),
        vmem16(slots, 2 * length, 2 * length), vmem16(slots, 2 * length, 2 * length),
        vmem(slots, 2, *half),
        vmem(slots, *plane), vmem(slots, *plane), vmem16(slots, 2 * length, length),
        vmem16(slots, length, 2 * length),
        vmem(slots, *plane), vmem(slots, *plane),
        vmem(slots, *plane), vmem(slots, *plane), vmem(slots, *plane), vmem(slots, *plane),
        vmem16(slots, length, 2 * length),
        halo, halo, halo, halo, vmem(*plane), vmem(*half), vmem(*half),
        vmem(*plane), vmem(*half), vmem(*half), vmem(*half), vmem(*plane),
        vmem(*plane), vmem(*half), vmem(*half), vmem(*half), vmem(*plane),
        vmem(5, *plane), vmem(5, *half), vmem(5, *plane), vmem(5, *half),
        vmem(5, *quarter), vmem(5, *quarter), vmem(5, *quarter), vmem(5, *quarter),
        vmem(5, *quarter), vmem(5, *quarter),
        pltpu.SMEM((slots, 8), F32),
        pltpu.SemaphoreType.DMA((3,)),
        pltpu.SemaphoreType.DMA((MESSAGES,)),
        pltpu.SemaphoreType.DMA((MESSAGES,)),
    ]
    hbm = pl.BlockSpec(memory_space=pl.ANY)
    smem = pl.BlockSpec(memory_space=pltpu.SMEM)
    return pl.pallas_call(
        functools.partial(kernel, tiles),
        out_shape=pltpu.VMEM(maps.shape, F32),
        in_specs=[hbm, hbm, smem, hbm, smem, smem, smem, smem],
        out_specs=pl.BlockSpec(memory_space=pltpu.VMEM),
        scratch_shapes=scratch,
        compiler_params=pltpu.CompilerParams(
            collective_id=0, has_side_effects=True, vmem_limit_bytes=56 << 20
        ),
    )(maps, measured, offsets, probe, spectrum, wave_index, edge_band.T, band_coef.transpose(1, 0, 2))


def solution(mesh):
    in_specs = (
        P(None, None, "tile"),
        P("tile", None, None),
        P("tile"),
        P("wave", None, None, None),
        P("wave"),
        P("wave"),
        P("wave", None),
        P(),
    )
    return jax.shard_map(
        functools.partial(per_device, mesh.shape["tile"]),
        mesh=mesh,
        in_specs=in_specs,
        out_specs=P(None, None, "tile"),
        check_vma=False,
    )
```

```python
import functools
import math

import jax
import jax.numpy as jnp
from jax import lax
from jax.experimental import pallas as pl
from jax.experimental.pallas import tpu as pltpu
from jax.sharding import PartitionSpec as P

WAVES = 48
RELAX = 4.0
FLOOR = 1.0
MESH = pl.DeviceIdType.MESH
F32 = jnp.float32
BF16 = jnp.bfloat16

SIN = (6.283184916495429, -41.341589232688364, 81.5999433297776, -76.61447253120122, 41.34288235437901, -12.471243534763557)
COS = (0.9999999890590201, -19.739204499453688, 64.93911745988827, -85.45013953077586, 60.16763095018129, -25.96759924584206, 6.528658157862129)

MEAS, PW1, PWL, PWA, PWB, IN1, IN1B, IN2, IN2M, GR1, GRL, GRA, GRB, OUT = range(14)
XIN1, XIN1B, XIN2, XIN2M, XPW1, XPWB, XGR1, XGRB, LMEAS = range(14, 23)
CHUNKS = 4
HALO, PASS, LHALO, LPASS = (23 + CHUNKS * k for k in range(4))
MESSAGES = 23 + CHUNKS * 4


def sincos_turns(turns):
    f = turns - jnp.round(turns)
    z = f * f
    s = jnp.full_like(z, SIN[-1])
    for k in SIN[-2::-1]:
        s = s * z + k
    c = jnp.full_like(z, COS[-1])
    for k in COS[-2::-1]:
        c = c * z + k
    return c, s * f


def swap(x):
    return pltpu.roll(x, 64, x.ndim - 1)


def kernel(
    tiles,
    maps_hbm, meas_hbm, off_ref, probe_hbm, spec_ref, wave_ref, edge_ref, band_ref,
    out_ref,
    mp, ms, pb, w1, w2, obj, psir, psii, psib, midb, farr, fari, psirx, psiix, farrx, farix, nbuf,
    halo_s, halo_r, right_s, left_r, ma_s, ma_r, mb_r,
    inten, inten_r, pair_i, far_i, sf, intenx, intenx_r, pair_ix, far_ix, sfx,
    acc, acc_r, accx, accx_r,
    lpack, lrecv, rpack, ra, rb, rpx,
    coef, copy_sem, send_sem, recv_sem,
):
    slots = spec_ref.shape[0]
    length = mp.shape[1]
    mid = length // 2
    chunk = length // CHUNKS
    t = lax.axis_index("tile")
    w = lax.axis_index("wave")
    core = lax.rem(w, 2)
    mate = w + 1 - 2 * core
    far_z = lax.rem(w + 2, 4)
    far_mate = lax.rem(mate + 2, 4)
    up = lax.rem(t + 1, tiles)
    down = lax.rem(t + tiles - 1, tiles)
    first = t == 0
    last = t == tiles - 1
    has_down = t > 0
    has_up = t < tiles - 1
    extra = lax.rem(t, tiles // 2) == 0
    next_extra = lax.rem(t + 1, tiles // 2) == 0

    mine = pl.ds(pl.multiple_of(core * mid, mid), mid)
    other = pl.ds(pl.multiple_of((1 - core) * mid, mid), mid)

    barrier = pltpu.get_barrier_semaphore()

    def greet(device):
        pl.semaphore_signal(barrier, inc=1, device_id=device, device_id_type=MESH)

    greet((t, mate))
    greet((t, far_z))
    greet((t, far_mate))

    @pl.when(has_down)
    def _():
        greet((down, w))

    @pl.when(has_up)
    def _():
        greet((up, w))

    load_maps = pltpu.make_async_copy(maps_hbm, mp, copy_sem.at[0])
    load_meas = pltpu.make_async_copy(meas_hbm, ms, copy_sem.at[1])
    load_probe = pltpu.make_async_copy(probe_hbm, pb, copy_sem.at[2])
    load_maps.start()
    load_meas.start()
    load_probe.start()

    def remote(k, src, dst, device):
        return pltpu.make_async_remote_copy(
            src_ref=src, dst_ref=dst, send_sem=send_sem.at[k], recv_sem=recv_sem.at[k],
            device_id=device, device_id_type=MESH,
        )

    def low_lanes(rows):
        return lax.broadcasted_iota(jnp.int32, (rows, length), 1) < mid

    def slot_coefficients(s, carry):
        for m in range(4):
            e = edge_ref[m, s]
            for k in range(2):
                c = [band_ref[n, k, m] for n in range(3)]
                coef[s, 4 * k + m] = jnp.where(e == 0, c[0], jnp.where(e == 1, c[1], c[2]))
        return carry

    lax.fori_loop(0, slots, slot_coefficients, 0)

    column = lax.broadcasted_iota(jnp.int32, (32, length), 1) - mid
    row = lax.broadcasted_iota(jnp.int32, (32, length), 0) - mid
    normaliser = 1.0 / math.sqrt(length)

    def table_slot(s, carry):
        which = jnp.full((32, length), wave_ref[s], jnp.int32).astype(F32)
        sampling = (0.6 + 0.4 * which / (WAVES - 1)) * (1.0 / length)
        for r in range(0, length, 32):
            c, sn = sincos_turns(sampling * ((row + r) * column).astype(F32))
            re = (c * normaliser).astype(BF16)
            sn = sn * normaliser
            im = (-sn).astype(BF16)
            nim = sn.astype(BF16)
            top, low = pl.ds(r, 32), pl.ds(length + r, 32)
            left, right = pl.ds(0, length), pl.ds(length, length)
            w1[s, top, left] = re
            w1[s, top, right] = nim
            w1[s, low, left] = im
            w1[s, low, right] = re
            w2[s, top, left] = re
            w2[s, top, right] = im
            w2[s, low, left] = nim
            w2[s, low, right] = re
        return carry

    load_maps.wait()
    hc = chunk // 2
    low_hc = low_lanes(hc)
    for q in range(CHUNKS):
        r = q * chunk
        for m in range(4):
            top, bottom = mp[m, r : r + hc], mp[m, r + hc : r + chunk]
            halo_s[q, m] = jnp.where(low_hc, top, swap(bottom))
            right_s[q, m] = jnp.where(low_hc, swap(top), bottom)
    tables_first = w < 2

    @pl.when(tables_first)
    def _():
        lax.fori_loop(0, slots, table_slot, 0)


    def groups(size, body, carry):
        def step(i, carry):
            return body([i * size + j for j in range(size)], carry)

        return lax.fori_loop(0, slots // size, step, carry)

    def transmission(s, planes):
        a = [coef[s, m] for m in range(4)]
        b = [coef[s, 4 + m] for m in range(4)]
        absorb = a[0] * planes[0] + a[1] * planes[1] + a[2] * planes[2] + a[3] * planes[3]
        phase = b[0] * planes[0] + b[1] * planes[1] + b[2] * planes[2] + b[3] * planes[3]
        damping = jnp.exp(-absorb)
        c, sn = sincos_turns(phase * (0.5 / math.pi))
        return damping * c, damping * sn

    def half_object(packed):
        def body(group, carry):
            for q in range(CHUNKS):
                planes = [packed[q, m] for m in range(4)]
                for s in group:
                    re, im = transmission(s, planes)
                    obj[s, 0, pl.ds(q * hc, hc), :] = re
                    obj[s, 1, pl.ds(q * hc, hc), :] = im
            return carry

        groups(3, body, 0)

    def waves_at_object(q, packed, pr, pi, power, fresh_low=False):
        at = pl.ds(q * hc, hc)

        def body(group, totals):
            totals = list(totals)
            planes = [packed[q, m] for m in range(4)]
            for s in group:
                nre, nim = transmission(s, planes)
                ore, oim = obj[s, 0, at, :], obj[s, 1, at, :]
                if fresh_low:
                    nre, nim, ore, oim = ore, oim, nre, nim
                for half, (re, im) in enumerate((
                    (jnp.where(low_hc, ore, swap(nre)), jnp.where(low_hc, oim, swap(nim))),
                    (jnp.where(low_hc, swap(ore), nre), jnp.where(low_hc, swap(oim), nim)),
                )):
                    rows = pl.ds(q * chunk + half * hc, hc)
                    p_re, p_im = pb[s, 0, rows, :], pb[s, 1, rows, :]
                    x = p_re * re - p_im * im
                    y = p_re * im + p_im * re
                    pr[s, rows, :] = x
                    pi[s, rows, :] = y
                    psib[s, rows, :] = x.astype(BF16)
                    psib[s, pl.ds(length + q * chunk + half * hc, hc), :] = y.astype(BF16)
                    totals[half] = totals[half] + spec_ref[s] * (x * x + y * y)
            return tuple(totals)

        zero = jnp.zeros((hc, length), F32)
        for half, total in enumerate(groups(6, body, (zero, zero))):
            power[pl.ds(q * chunk + half * hc, hc), :] = total

    def left_forward():
        def body(group, carry):
            for s in group:
                m = jnp.dot(w1[s], psib[s], preferred_element_type=F32).astype(BF16)
                midb[s, :, 0:length] = m[:length]
                midb[s, :, length : 2 * length] = m[length:]
            return carry

        groups(6, body, 0)

    def right_forward(rows_at, fr, fi, total):
        rows = pl.ds(pl.multiple_of(rows_at, mid), mid)

        def body(group, light):
            for s in group:
                far = jnp.dot(midb[s, rows, :], w2[s], preferred_element_type=F32)
                x, y = far[:, :length], far[:, length:]
                fr[s, rows, :] = x
                fi[s, rows, :] = y
                light = light + spec_ref[s] * (x * x + y * y)
            return light

        total[rows, :] = groups(6, body, jnp.zeros((mid, length), F32))

    def back_left(short, fr, fi):
        def body(group, carry):
            for s in group:
                factor = spec_ref[s] * short[...]
                d = jnp.concatenate(
                    [(factor * fr[s]).astype(BF16), (factor * fi[s]).astype(BF16)], axis=0
                )
                nb = jnp.dot(w2[s], d, preferred_element_type=F32).astype(BF16)
                nbuf[s, :, 0:length] = nb[:length]
                nbuf[s, :, length : 2 * length] = nb[length:]
            return carry

        groups(6, body, 0)

    def back_right(rows_at, pr, pi, into):
        rows = pl.ds(pl.multiple_of(rows_at, mid), mid)
        for m in range(4):
            into[m, rows, :] = jnp.zeros((mid, length), F32)

        def body(group, carry):
            back = [jnp.dot(nbuf[s, rows, :], w1[s], preferred_element_type=F32) for s in group]
            for r in range(0, mid, 16):
                part = pl.ds(pl.multiple_of(rows_at + r, 16), 16)
                sums = [into[m, part, :] for m in range(4)]
                for s, both in zip(group, back):
                    br, bi = both[r : r + 16, :length], both[r : r + 16, length:]
                    x, y = pr[s, part, :], pi[s, part, :]
                    cr = x * br + y * bi
                    ci = x * bi - y * br
                    for m in range(4):
                        sums[m] = sums[m] + (coef[s, 4 + m] * ci - coef[s, m] * cr)
                for m in range(4):
                    into[m, part, :] = sums[m]
            return carry

        groups(6, body, 0)

    at_mine, at_other = core * mid, (1 - core) * mid
    frames_here = jnp.where(last, 1.0, 2.0)
    frames_left = jnp.where(first, 1.0, 2.0)
    quarter = mid // 2

    def pack_right(y):
        return jnp.where(low_lanes(quarter), swap(y[:quarter]), y[quarter:])

    def pack_left(y):
        return jnp.where(low_lanes(quarter), y[:quarter], swap(y[quarter:]))

    four = pl.ds(0, 4)
    sx_in1 = remote(XIN1, intenx.at[other], intenx_r.at[other], (t, mate))
    sx_in1b = remote(XIN1B, intenx.at[mine], intenx_r.at[mine], (t, mate))
    sx_in2 = remote(XIN2, pair_ix.at[mine], far_ix.at[mine], (t, far_z))
    sx_in2m = remote(XIN2M, pair_ix.at[mine], far_ix.at[mine], (t, far_mate))
    sx_pw1 = remote(XPW1, accx.at[4, other], accx_r.at[4], (t, mate))
    sx_pwb = remote(XPWB, rpx.at[4], rb.at[4], (t, far_z))
    sx_gr1 = remote(XGR1, accx.at[four, other], accx_r.at[four], (t, mate))
    sx_grb = remote(XGRB, rpx.at[four], rb.at[four], (t, far_z))

    def light_of_both(partial, received, pair, first_half, second_half, far_one, far_two):
        second_half.start()
        first_half.wait_recv()
        pair[mine, :] = partial[mine, :] + received[mine, :]
        far_one.start()
        far_two.start()

    def factors(partial, received, pair, far, one, two, frames, into):
        pair[other, :] = partial[other, :] + received[other, :]
        for r in range(0, length, 32):
            rows = pl.ds(r, 32)
            inv = 1.0 / jnp.maximum(pair[rows, :] + far[rows, :], FLOOR)
            into[rows, :] = jnp.sqrt(one[rows, :] * inv) + jnp.sqrt(two[rows, :] * inv) - frames

    def extra_forward():
        sx_pw1.start()
        left_forward()
        right_forward(at_other, farrx, farix, intenx)
        sx_in1.start()
        right_forward(at_mine, farrx, farix, intenx)
        light_of_both(intenx, intenx_r, pair_ix, sx_in1, sx_in1b, sx_in2, sx_in2m)
        sx_pw1.wait_recv()
        rpx[4] = pack_right(frames_left * (accx[4, mine, :] + accx_r[4]))
        sx_pwb.start()

    def extra_shortfall():
        sx_in1b.wait_recv()
        sx_in2.wait_recv()
        sx_in2m.wait_recv()
        factors(intenx, intenx_r, pair_ix, far_ix, ma_s, mb_r, frames_left, sfx)

    def extra_backward():
        back_left(sfx, farrx, farix)
        back_right(at_other, psirx, psiix, accx)
        sx_gr1.start()
        back_right(at_mine, psirx, psiix, accx)
        sx_gr1.wait_recv()
        for m in range(4):
            rpx[m] = pack_right(accx[m, mine, :] + accx_r[m])
        sx_grb.start()

    @pl.when(first)
    def _():
        left_r[...] = jnp.zeros_like(left_r)
        mb_r[...] = jnp.zeros_like(mb_r)

    @pl.when(last)
    def _():
        halo_r[...] = jnp.zeros_like(halo_r)
        ma_r[...] = jnp.zeros_like(ma_r)

    pl.semaphore_wait(barrier, 3 + (t + tiles - 1) // tiles + (2 * tiles - 2 - t) // tiles)

    fetches = core == 1
    send_halo = [remote(HALO + q, halo_s.at[q], halo_r.at[q], (down, w)) for q in range(CHUNKS)]
    pass_halo = [remote(PASS + q, halo_r.at[q], halo_r.at[q], (t, mate)) for q in range(CHUNKS)]
    send_right = [remote(LHALO + q, right_s.at[q], left_r.at[q], (up, w)) for q in range(CHUNKS)]
    pass_right = [remote(LPASS + q, left_r.at[q], left_r.at[q], (t, mate)) for q in range(CHUNKS)]
    send_meas = remote(MEAS, ma_s, ma_r, (down, w))
    send_meas_up = remote(LMEAS, ms.at[1], mb_r, (up, w))
    sends_right = has_up & next_extra

    @pl.when(fetches & has_down)
    def _():
        for copy in send_halo:
            copy.start()

    @pl.when(fetches & sends_right)
    def _():
        for copy in send_right:
            copy.start()

    load_meas.wait()
    low_first = off_ref[0] < off_ref[1]
    for r in range(0, length, 32):
        rows = pl.ds(r, 32)
        one, two = ms[0, rows, :], ms[1, rows, :]
        ma_s[rows, :] = jnp.where(low_first, one, two)
        ms[1, rows, :] = jnp.where(low_first, two, one)

    @pl.when(jnp.logical_not(tables_first))
    def _():
        lax.fori_loop(0, slots, table_slot, 0)

    half_object(right_s)

    load_probe.wait()

    def arrived(q):
        @pl.when(has_up & fetches)
        def _():
            send_halo[q].wait_recv()
            pass_halo[q].start()

    arrived(0)
    for q in range(CHUNKS):
        if q + 1 < CHUNKS:
            arrived(q + 1)

        @pl.when(has_up & jnp.logical_not(fetches))
        def _():
            pass_halo[q].wait_recv()

        waves_at_object(q, halo_r, psir, psii, acc.at[4])

    @pl.when(has_down)
    def _():
        send_meas.start()

    @pl.when(sends_right)
    def _():
        send_meas_up.start()

    s_pw1 = remote(PW1, acc.at[4, other], acc_r.at[4], (t, mate))
    s_in1 = remote(IN1, inten.at[other], inten_r.at[other], (t, mate))
    s_in1b = remote(IN1B, inten.at[mine], inten_r.at[mine], (t, mate))
    s_in2 = remote(IN2, pair_i.at[mine], far_i.at[mine], (t, far_z))
    s_in2m = remote(IN2M, pair_i.at[mine], far_i.at[mine], (t, far_mate))
    s_gr1 = remote(GR1, acc.at[four, other], acc_r.at[four], (t, mate))
    s_pwl = remote(PWL, lpack.at[4], lrecv.at[4], (t, far_z))
    s_pwa = remote(PWA, rpack.at[4], ra.at[4], (up, w))
    s_pwb = remote(PWB, rpack.at[4], rb.at[4], (up, far_z))
    s_grl = remote(GRL, lpack.at[four], lrecv.at[four], (t, far_z))
    s_gra = remote(GRA, rpack.at[four], ra.at[four], (up, w))
    s_grb = remote(GRB, rpack.at[four], rb.at[four], (up, far_z))

    s_pw1.start()
    left_forward()
    right_forward(at_other, farr, fari, inten)
    s_in1.start()
    right_forward(at_mine, farr, fari, inten)
    light_of_both(inten, inten_r, pair_i, s_in1, s_in1b, s_in2, s_in2m)

    s_pw1.wait_recv()
    power = frames_here * (acc[4, mine, :] + acc_r[4])
    lpack[4] = pack_left(power)
    rpack[4] = pack_right(power)

    extra_late = extra & has_down

    @pl.when(extra_late & fetches)
    def _():
        for arriving, passed in zip(send_right, pass_right):
            arriving.wait_recv()
            passed.start()

    @pl.when(extra)
    def _():
        half_object(halo_s)
        for q in range(CHUNKS):

            @pl.when(extra_late & jnp.logical_not(fetches))
            def _():
                pass_right[q].wait_recv()

            waves_at_object(q, left_r, psirx, psiix, accx.at[4], fresh_low=True)
        extra_forward()

    @pl.when(has_up)
    def _():
        send_meas.wait_recv()

    s_in1b.wait_recv()
    s_in2.wait_recv()
    s_in2m.wait_recv()
    factors(inten, inten_r, pair_i, far_i, ms.at[1], ma_r, frames_here, sf)
    s_pwl.start()

    rim_up = has_up & jnp.logical_not(next_extra)
    rim_down = jnp.logical_not(extra)

    @pl.when(rim_up)
    def _():
        s_pwa.start()
        s_pwb.start()

    back_left(sf, farr, fari)
    back_right(at_other, psir, psii, acc)
    s_gr1.start()
    back_right(at_mine, psir, psii, acc)
    s_gr1.wait_recv()
    for m in range(4):
        y = acc[m, mine, :] + acc_r[m]
        lpack[m] = pack_left(y)
        rpack[m] = pack_right(y)

    @pl.when(rim_up)
    def _():
        s_grb.start()

    s_grl.start()

    @pl.when(rim_up)
    def _():
        s_gra.start()

    @pl.when(extra_late)
    def _():
        send_meas_up.wait_recv()

    @pl.when(extra)
    def _():
        extra_shortfall()
        extra_backward()
        sx_pwb.wait_recv()
        sx_grb.wait_recv()
        ra[...] = rpx[...]

    @pl.when(rim_down)
    def _():
        s_pwa.wait_recv()
        s_pwb.wait_recv()
        s_gra.wait_recv()
        s_grb.wait_recv()

    s_pwl.wait_recv()
    s_grl.wait_recv()

    def totals(m):
        l = lpack[m] + lrecv[m]
        r = ra[m] + rb[m]
        return jnp.where(low_lanes(quarter), r, swap(l)), jnp.where(low_lanes(quarter), swap(r), l)

    powers = [RELAX / (p + 1.0) for p in totals(4)]
    for m in range(4):
        for q, total in enumerate(totals(m)):
            rows = pl.ds(pl.multiple_of(at_mine + q * quarter, quarter), quarter)
            out_ref[m, rows, :] = mp[m, rows, :] + total * powers[q]
    s_out = remote(OUT, out_ref.at[:, mine], out_ref.at[:, mine], (t, mate))
    s_out.start()

    for copy in (s_pw1, s_in1, s_in1b, s_in2, s_in2m, s_gr1, s_pwl, s_grl):
        copy.wait_send()

    @pl.when(has_down)
    def _():
        send_meas.wait_send()

    @pl.when(has_down & fetches)
    def _():
        for copy in send_halo:
            copy.wait_send()

    @pl.when(has_up & fetches)
    def _():
        for copy in pass_halo:
            copy.wait_send()

    @pl.when(sends_right & fetches)
    def _():
        for copy in send_right:
            copy.wait_send()

    @pl.when(extra_late & fetches)
    def _():
        for copy in pass_right:
            copy.wait_send()

    @pl.when(rim_up)
    def _():
        for copy in (s_pwa, s_pwb, s_gra, s_grb):
            copy.wait_send()

    @pl.when(sends_right)
    def _():
        send_meas_up.wait_send()

    @pl.when(extra)
    def _():
        for copy in (sx_in1, sx_in1b, sx_in2, sx_in2m, sx_pw1, sx_pwb, sx_gr1, sx_grb):
            copy.wait_send()

    s_out.wait()


def per_device(tiles, maps, measured, offsets, probe, spectrum, wave_index, edge_band, band_coef):
    _, length, columns = maps.shape
    slots = spectrum.shape[0]
    mid = length // 2
    vmem = lambda *shape: pltpu.VMEM(shape, F32)
    vmem16 = lambda *shape: pltpu.VMEM(shape, BF16)
    plane = (length, length)
    half = (mid, length)
    quarter = (mid // 2, length)
    halo = vmem(CHUNKS, 4, length // CHUNKS // 2, length)
    scratch = [
        vmem(4, *plane), vmem(2, *plane), vmem(slots, 2, *plane),
        vmem16(slots, 2 * length, 2 * length), vmem16(slots, 2 * length, 2 * length),
        vmem(slots, 2, *half),
        vmem(slots, *plane), vmem(slots, *plane), vmem16(slots, 2 * length, length),
        vmem16(slots, length, 2 * length),
        vmem(slots, *plane), vmem(slots, *plane),
        vmem(slots, *plane), vmem(slots, *plane), vmem(slots, *plane), vmem(slots, *plane),
        vmem16(slots, length, 2 * length),
        halo, halo, halo, halo, vmem(*plane), vmem(*plane), vmem(*plane),
        vmem(*plane), vmem(*plane), vmem(*plane), vmem(*plane), vmem(*plane),
        vmem(*plane), vmem(*plane), vmem(*plane), vmem(*plane), vmem(*plane),
        vmem(5, *plane), vmem(5, *half), vmem(5, *plane), vmem(5, *half),
        vmem(5, *quarter), vmem(5, *quarter), vmem(5, *quarter), vmem(5, *quarter),
        vmem(5, *quarter), vmem(5, *quarter),
        pltpu.SMEM((slots, 8), F32),
        pltpu.SemaphoreType.DMA((3,)),
        pltpu.SemaphoreType.DMA((MESSAGES,)),
        pltpu.SemaphoreType.DMA((MESSAGES,)),
    ]
    hbm = pl.BlockSpec(memory_space=pl.ANY)
    smem = pl.BlockSpec(memory_space=pltpu.SMEM)
    return pl.pallas_call(
        functools.partial(kernel, tiles),
        out_shape=pltpu.VMEM(maps.shape, F32),
        in_specs=[hbm, hbm, smem, hbm, smem, smem, smem, smem],
        out_specs=pl.BlockSpec(memory_space=pltpu.VMEM),
        scratch_shapes=scratch,
        compiler_params=pltpu.CompilerParams(
            collective_id=0, has_side_effects=True, vmem_limit_bytes=56 << 20
        ),
    )(maps, measured, offsets, probe, spectrum, wave_index, edge_band.T, band_coef.transpose(1, 0, 2))


def solution(mesh):
    in_specs = (
        P(None, None, "tile"),
        P("tile", None, None),
        P("tile"),
        P("wave", None, None, None),
        P("wave"),
        P("wave"),
        P("wave", None),
        P(),
    )
    return jax.shard_map(
        functools.partial(per_device, mesh.shape["tile"]),
        mesh=mesh,
        in_specs=in_specs,
        out_specs=P(None, None, "tile"),
        check_vma=False,
    )
```

```python
import functools
import math

import jax
import jax.numpy as jnp
from jax import lax
from jax.experimental import pallas as pl
from jax.experimental.pallas import tpu as pltpu
from jax.sharding import PartitionSpec as P

WAVES = 48
RELAX = 4.0
FLOOR = 1.0
MESH = pl.DeviceIdType.MESH
F32 = jnp.float32
BF16 = jnp.bfloat16

SIN = (6.283184916495429, -41.341589232688364, 81.5999433297776, -76.61447253120122, 41.34288235437901, -12.471243534763557)
COS = (0.9999999890590201, -19.739204499453688, 64.93911745988827, -85.45013953077586, 60.16763095018129, -25.96759924584206, 6.528658157862129)

MEAS, PW1, PWR, PWA, PWB, IN1, IN1B, IN2, IN2M, GR1, GRR, GRA, GRB, OUT = range(14)
XIN1, XIN1B, XIN2, XIN2M, XPW1, XPWB, XGR1, XGRB = range(14, 22)
CHUNKS = 4
HALO, PASS = (22 + CHUNKS * k for k in range(2))
MESSAGES = 22 + CHUNKS * 2


def sincos_turns(turns):
    f = turns - jnp.round(turns)
    z = f * f
    s = jnp.full_like(z, SIN[-1])
    for k in SIN[-2::-1]:
        s = s * z + k
    c = jnp.full_like(z, COS[-1])
    for k in COS[-2::-1]:
        c = c * z + k
    return c, s * f


def swap(x):
    return pltpu.roll(x, 64, x.ndim - 1)


def kernel(
    tiles,
    maps_hbm, meas_hbm, off_ref, probe_hbm, spec_ref, wave_ref, edge_ref, band_ref,
    out_ref,
    mp, ms, pb, w1, w2, obj, psir, psii, psib, midb, farr, fari, psirx, psiix, farrx, farix, nbuf,
    left_s, right_s, halo_r, none_r, ma_s, mb_r, none_m,
    inten, inten_r, pair_i, far_i, sf, intenx, intenx_r, pair_ix, far_ix, sfx,
    acc, acc_r, accx, accx_r,
    rpack, rrecv, lpack, la, lb, lpx,
    coef, enter, copy_sem, send_sem, recv_sem,
):
    slots = spec_ref.shape[0]
    length = mp.shape[1]
    mid = length // 2
    chunk = length // CHUNKS
    t = lax.axis_index("tile")
    w = lax.axis_index("wave")
    core = lax.rem(w, 2)
    mate = w + 1 - 2 * core
    far_z = lax.rem(w + 2, 4)
    far_mate = lax.rem(mate + 2, 4)
    up = lax.rem(t + 1, tiles)
    down = lax.rem(t + tiles - 1, tiles)
    first = t == 0
    last = t == tiles - 1
    has_down = t > 0
    has_up = t < tiles - 1
    mine = pl.ds(pl.multiple_of(core * mid, mid), mid)
    other = pl.ds(pl.multiple_of((1 - core) * mid, mid), mid)

    barrier = pltpu.get_barrier_semaphore()

    def greet(device):
        pl.semaphore_signal(barrier, inc=1, device_id=device, device_id_type=MESH)

    greet((t, mate))
    @pl.when(w < 2)
    def _():
        greet((t, far_z))
        greet((t, far_mate))

    @pl.when(has_down)
    def _():
        greet((down, w))

    greetings = 1 + 2 * (w // 2) + (2 * tiles - 2 - t) // tiles

    load_maps = pltpu.make_async_copy(maps_hbm, mp, copy_sem.at[0])
    load_meas = pltpu.make_async_copy(meas_hbm, ms, copy_sem.at[1])
    load_probe = pltpu.make_async_copy(probe_hbm, pb, copy_sem.at[2])
    load_maps.start()
    load_meas.start()
    load_probe.start()

    def remote(k, src, dst, device):
        return pltpu.make_async_remote_copy(
            src_ref=src, dst_ref=dst, send_sem=send_sem.at[k], recv_sem=recv_sem.at[k],
            device_id=device, device_id_type=MESH,
        )

    def low_lanes(rows):
        return lax.broadcasted_iota(jnp.int32, (rows, length), 1) < mid

    def slot_coefficients(s, carry):
        for m in range(4):
            e = edge_ref[m, s]
            for k in range(2):
                c = [band_ref[n, k, m] for n in range(3)]
                coef[s, 4 * k + m] = jnp.where(e == 0, c[0], jnp.where(e == 1, c[1], c[2]))
        return carry

    lax.fori_loop(0, slots, slot_coefficients, 0)

    column = lax.broadcasted_iota(jnp.int32, (32, length), 1) - mid
    row = lax.broadcasted_iota(jnp.int32, (32, length), 0) - mid
    normaliser = 1.0 / math.sqrt(length)

    def table_slot(s, carry):
        which = jnp.full((32, length), wave_ref[s], jnp.int32).astype(F32)
        sampling = (0.6 + 0.4 * which / (WAVES - 1)) * (1.0 / length)
        for r in range(0, length, 32):
            c, sn = sincos_turns(sampling * ((row + r) * column).astype(F32))
            re = (c * normaliser).astype(BF16)
            sn = sn * normaliser
            im = (-sn).astype(BF16)
            nim = sn.astype(BF16)
            top, low = pl.ds(r, 32), pl.ds(length + r, 32)
            left, right = pl.ds(0, length), pl.ds(length, length)
            w1[s, top, left] = re
            w1[s, top, right] = nim
            w1[s, low, left] = im
            w1[s, low, right] = re
            w2[s, top, left] = re
            w2[s, top, right] = im
            w2[s, low, left] = nim
            w2[s, low, right] = re
        return carry

    pl.semaphore_wait(barrier, greetings)

    @pl.when(w >= 2)
    def _():
        for device in ((t, far_z), (t, far_mate)):
            pl.semaphore_signal(enter, inc=1, device_id=device, device_id_type=MESH)

    load_maps.wait()
    hc = chunk // 2
    low_hc = low_lanes(hc)
    for q in range(CHUNKS):
        r = q * chunk
        for m in range(4):
            top, bottom = mp[m, r : r + hc], mp[m, r + hc : r + chunk]
            left_s[q, m] = jnp.where(low_hc, top, swap(bottom))
            right_s[q, m] = jnp.where(low_hc, swap(top), bottom)


    def groups(size, body, carry):
        def step(i, carry):
            return body([i * size + j for j in range(size)], carry)

        return lax.fori_loop(0, slots // size, step, carry)

    def transmission(s, planes):
        a = [coef[s, m] for m in range(4)]
        b = [coef[s, 4 + m] for m in range(4)]
        absorb = a[0] * planes[0] + a[1] * planes[1] + a[2] * planes[2] + a[3] * planes[3]
        phase = b[0] * planes[0] + b[1] * planes[1] + b[2] * planes[2] + b[3] * planes[3]
        damping = jnp.exp(-absorb)
        c, sn = sincos_turns(phase * (0.5 / math.pi))
        return damping * c, damping * sn

    def half_object(packed):
        def body(group, carry):
            for q in range(CHUNKS):
                planes = [packed[q, m] for m in range(4)]
                for s in group:
                    re, im = transmission(s, planes)
                    obj[s, 0, pl.ds(q * hc, hc), :] = re
                    obj[s, 1, pl.ds(q * hc, hc), :] = im
            return carry

        groups(3, body, 0)

    def waves_at_object(q, packed, pr, pi, power, fresh_low=False):
        at = pl.ds(q * hc, hc)

        def body(group, totals):
            totals = list(totals)
            planes = [packed[q, m] for m in range(4)]
            for s in group:
                nre, nim = transmission(s, planes)
                ore, oim = obj[s, 0, at, :], obj[s, 1, at, :]
                if fresh_low:
                    nre, nim, ore, oim = ore, oim, nre, nim
                for half, (re, im) in enumerate((
                    (jnp.where(low_hc, ore, swap(nre)), jnp.where(low_hc, oim, swap(nim))),
                    (jnp.where(low_hc, swap(ore), nre), jnp.where(low_hc, swap(oim), nim)),
                )):
                    rows = pl.ds(q * chunk + half * hc, hc)
                    p_re, p_im = pb[s, 0, rows, :], pb[s, 1, rows, :]
                    x = p_re * re - p_im * im
                    y = p_re * im + p_im * re
                    pr[s, rows, :] = x
                    pi[s, rows, :] = y
                    psib[s, rows, :] = x.astype(BF16)
                    psib[s, pl.ds(length + q * chunk + half * hc, hc), :] = y.astype(BF16)
                    totals[half] = totals[half] + spec_ref[s] * (x * x + y * y)
            return tuple(totals)

        zero = jnp.zeros((hc, length), F32)
        for half, total in enumerate(groups(6, body, (zero, zero))):
            power[pl.ds(q * chunk + half * hc, hc), :] = total

    def left_forward():
        def body(group, carry):
            for s in group:
                m = jnp.dot(w1[s], psib[s], preferred_element_type=F32).astype(BF16)
                midb[s, :, 0:length] = m[:length]
                midb[s, :, length : 2 * length] = m[length:]
            return carry

        groups(6, body, 0)

    def right_forward(rows_at, fr, fi, total):
        rows = pl.ds(pl.multiple_of(rows_at, mid), mid)

        def body(group, light):
            for s in group:
                far = jnp.dot(midb[s, rows, :], w2[s], preferred_element_type=F32)
                x, y = far[:, :length], far[:, length:]
                fr[s, rows, :] = x
                fi[s, rows, :] = y
                light = light + spec_ref[s] * (x * x + y * y)
            return light

        total[rows, :] = groups(6, body, jnp.zeros((mid, length), F32))

    def back_left(short, fr, fi):
        def body(group, carry):
            for s in group:
                factor = spec_ref[s] * short[...]
                d = jnp.concatenate(
                    [(factor * fr[s]).astype(BF16), (factor * fi[s]).astype(BF16)], axis=0
                )
                nb = jnp.dot(w2[s], d, preferred_element_type=F32).astype(BF16)
                nbuf[s, :, 0:length] = nb[:length]
                nbuf[s, :, length : 2 * length] = nb[length:]
            return carry

        groups(6, body, 0)

    def back_right(rows_at, pr, pi, into):
        rows = pl.ds(pl.multiple_of(rows_at, mid), mid)
        for m in range(4):
            into[m, rows, :] = jnp.zeros((mid, length), F32)

        def body(group, carry):
            back = [jnp.dot(nbuf[s, rows, :], w1[s], preferred_element_type=F32) for s in group]
            for r in range(0, mid, 16):
                part = pl.ds(pl.multiple_of(rows_at + r, 16), 16)
                sums = [into[m, part, :] for m in range(4)]
                for s, both in zip(group, back):
                    br, bi = both[r : r + 16, :length], both[r : r + 16, length:]
                    x, y = pr[s, part, :], pi[s, part, :]
                    cr = x * br + y * bi
                    ci = x * bi - y * br
                    for m in range(4):
                        sums[m] = sums[m] + (coef[s, 4 + m] * ci - coef[s, m] * cr)
                for m in range(4):
                    into[m, part, :] = sums[m]
            return carry

        groups(6, body, 0)

    at_mine, at_other = core * mid, (1 - core) * mid
    frames_here = jnp.where(first, 1.0, 2.0)
    quarter = mid // 2

    def pack_right(y):
        return jnp.where(low_lanes(quarter), swap(y[:quarter]), y[quarter:])

    def pack_left(y):
        return jnp.where(low_lanes(quarter), y[:quarter], swap(y[quarter:]))

    four = pl.ds(0, 4)
    sx_in1 = remote(XIN1, intenx.at[other], intenx_r.at[other], (t, mate))
    sx_in1b = remote(XIN1B, intenx.at[mine], intenx_r.at[mine], (t, mate))
    sx_in2 = remote(XIN2, pair_ix.at[mine], far_ix.at[mine], (t, far_z))
    sx_in2m = remote(XIN2M, pair_ix.at[mine], far_ix.at[mine], (t, far_mate))
    sx_pw1 = remote(XPW1, accx.at[4, other], accx_r.at[4], (t, mate))
    sx_pwb = remote(XPWB, lpx.at[4], lb.at[4], (t, far_z))
    sx_gr1 = remote(XGR1, accx.at[four, other], accx_r.at[four], (t, mate))
    sx_grb = remote(XGRB, lpx.at[four], lb.at[four], (t, far_z))

    def light_of_both(partial, received, pair, first_half, second_half, far_one, far_two):
        second_half.start()
        first_half.wait_recv()
        pair[mine, :] = partial[mine, :] + received[mine, :]
        far_one.start()
        far_two.start()

    def factors(partial, received, pair, far, one, two, frames, into):
        pair[other, :] = partial[other, :] + received[other, :]
        for r in range(0, length, 32):
            rows = pl.ds(r, 32)
            inv = 1.0 / jnp.maximum(pair[rows, :] + far[rows, :], FLOOR)
            into[rows, :] = jnp.sqrt(one[rows, :] * inv) + jnp.sqrt(two[rows, :] * inv) - frames

    def extra_forward():
        sx_pw1.start()
        left_forward()
        right_forward(at_other, farrx, farix, intenx)
        sx_in1.start()
        right_forward(at_mine, farrx, farix, intenx)
        light_of_both(intenx, intenx_r, pair_ix, sx_in1, sx_in1b, sx_in2, sx_in2m)
        sx_pw1.wait_recv()
        lpx[4] = pack_left(accx[4, mine, :] + accx_r[4])
        sx_pwb.start()

    def extra_shortfall():
        sx_in1b.wait_recv()
        sx_in2.wait_recv()
        sx_in2m.wait_recv()
        factors(intenx, intenx_r, pair_ix, far_ix, ms.at[1], none_m, 1.0, sfx)

    def extra_backward():
        back_left(sfx, farrx, farix)
        back_right(at_other, psirx, psiix, accx)
        sx_gr1.start()
        back_right(at_mine, psirx, psiix, accx)
        sx_gr1.wait_recv()
        for m in range(4):
            lpx[m] = pack_left(accx[m, mine, :] + accx_r[m])
        sx_grb.start()

    @pl.when(first)
    def _():
        halo_r[...] = jnp.zeros_like(halo_r)
        mb_r[...] = jnp.zeros_like(mb_r)

    @pl.when(last)
    def _():
        none_r[...] = jnp.zeros_like(none_r)
        none_m[...] = jnp.zeros_like(none_m)

    fetches = core == 1
    send_halo = [remote(HALO + q, right_s.at[q], halo_r.at[q], (up, w)) for q in range(CHUNKS)]
    pass_halo = [remote(PASS + q, halo_r.at[q], halo_r.at[q], (t, mate)) for q in range(CHUNKS)]
    send_meas = remote(MEAS, ms.at[1], mb_r, (up, w))

    @pl.when(fetches & has_up)
    def _():
        for copy in send_halo:
            copy.start()

    load_meas.wait()
    low_first = off_ref[0] < off_ref[1]
    for r in range(0, length, 32):
        rows = pl.ds(r, 32)
        one, two = ms[0, rows, :], ms[1, rows, :]
        ma_s[rows, :] = jnp.where(low_first, one, two)
        ms[1, rows, :] = jnp.where(low_first, two, one)

    lax.fori_loop(0, slots, table_slot, 0)

    half_object(left_s)

    load_probe.wait()

    def arrived(q):
        @pl.when(has_down & fetches)
        def _():
            send_halo[q].wait_recv()
            pass_halo[q].start()

    arrived(0)
    for q in range(CHUNKS):
        if q + 1 < CHUNKS:
            arrived(q + 1)

        @pl.when(has_down & jnp.logical_not(fetches))
        def _():
            pass_halo[q].wait_recv()

        waves_at_object(q, halo_r, psir, psii, acc.at[4], fresh_low=True)

        if q == 1:

            @pl.when(has_up)
            def _():
                send_meas.start()

    s_pw1 = remote(PW1, acc.at[4, other], acc_r.at[4], (t, mate))
    s_in1 = remote(IN1, inten.at[other], inten_r.at[other], (t, mate))
    s_in1b = remote(IN1B, inten.at[mine], inten_r.at[mine], (t, mate))
    s_in2 = remote(IN2, pair_i.at[mine], far_i.at[mine], (t, far_z))
    s_in2m = remote(IN2M, pair_i.at[mine], far_i.at[mine], (t, far_mate))
    s_gr1 = remote(GR1, acc.at[four, other], acc_r.at[four], (t, mate))
    s_pwr = remote(PWR, rpack.at[4], rrecv.at[4], (t, far_z))
    s_pwa = remote(PWA, lpack.at[4], la.at[4], (down, w))
    s_pwb = remote(PWB, lpack.at[4], lb.at[4], (down, far_z))
    s_grr = remote(GRR, rpack.at[four], rrecv.at[four], (t, far_z))
    s_gra = remote(GRA, lpack.at[four], la.at[four], (down, w))
    s_grb = remote(GRB, lpack.at[four], lb.at[four], (down, far_z))

    s_pw1.start()
    left_forward()
    right_forward(at_other, farr, fari, inten)
    s_in1.start()
    right_forward(at_mine, farr, fari, inten)

    @pl.when(w < 2)
    def _():
        pl.semaphore_wait(enter, 2)

    light_of_both(inten, inten_r, pair_i, s_in1, s_in1b, s_in2, s_in2m)

    s_pw1.wait_recv()
    power = frames_here * (acc[4, mine, :] + acc_r[4])
    lpack[4] = pack_left(power)
    rpack[4] = pack_right(power)

    @pl.when(last)
    def _():
        half_object(right_s)
        for q in range(CHUNKS):
            waves_at_object(q, none_r, psirx, psiix, accx.at[4])
        extra_forward()

    @pl.when(has_down)
    def _():
        send_meas.wait_recv()

    s_in1b.wait_recv()
    s_in2.wait_recv()
    s_in2m.wait_recv()
    factors(inten, inten_r, pair_i, far_i, ma_s, mb_r, frames_here, sf)
    s_pwr.start()


    @pl.when(has_down)
    def _():
        s_pwa.start()
        s_pwb.start()

    back_left(sf, farr, fari)
    back_right(at_other, psir, psii, acc)
    s_gr1.start()
    back_right(at_mine, psir, psii, acc)
    s_gr1.wait_recv()
    for m in range(4):
        y = acc[m, mine, :] + acc_r[m]
        lpack[m] = pack_left(y)
        rpack[m] = pack_right(y)

    @pl.when(has_down)
    def _():
        s_grb.start()

    s_grr.start()

    @pl.when(has_down)
    def _():
        s_gra.start()

    @pl.when(last)
    def _():
        extra_shortfall()
        extra_backward()
        sx_pwb.wait_recv()
        sx_grb.wait_recv()
        la[...] = lpx[...]

    @pl.when(has_up)
    def _():
        s_pwa.wait_recv()
        s_pwb.wait_recv()
        s_gra.wait_recv()
        s_grb.wait_recv()

    s_pwr.wait_recv()
    s_grr.wait_recv()

    def totals(m):
        l = la[m] + lb[m]
        r = rpack[m] + rrecv[m]
        return jnp.where(low_lanes(quarter), r, swap(l)), jnp.where(low_lanes(quarter), swap(r), l)

    powers = [RELAX / (p + 1.0) for p in totals(4)]
    for m in range(4):
        for q, total in enumerate(totals(m)):
            rows = pl.ds(pl.multiple_of(at_mine + q * quarter, quarter), quarter)
            out_ref[m, rows, :] = mp[m, rows, :] + total * powers[q]
    s_out = remote(OUT, out_ref.at[:, mine], out_ref.at[:, mine], (t, mate))
    s_out.start()

    for copy in (s_pw1, s_in1, s_in1b, s_in2, s_in2m, s_gr1, s_pwr, s_grr):
        copy.wait_send()

    @pl.when(has_up)
    def _():
        send_meas.wait_send()

    @pl.when(has_up & fetches)
    def _():
        for copy in send_halo:
            copy.wait_send()

    @pl.when(has_down & fetches)
    def _():
        for copy in pass_halo:
            copy.wait_send()

    @pl.when(has_down)
    def _():
        for copy in (s_pwa, s_pwb, s_gra, s_grb):
            copy.wait_send()

    @pl.when(last)
    def _():
        for copy in (sx_in1, sx_in1b, sx_in2, sx_in2m, sx_pw1, sx_pwb, sx_gr1, sx_grb):
            copy.wait_send()

    s_out.wait()


def per_device(tiles, maps, measured, offsets, probe, spectrum, wave_index, edge_band, band_coef):
    _, length, columns = maps.shape
    slots = spectrum.shape[0]
    mid = length // 2
    vmem = lambda *shape: pltpu.VMEM(shape, F32)
    vmem16 = lambda *shape: pltpu.VMEM(shape, BF16)
    plane = (length, length)
    half = (mid, length)
    quarter = (mid // 2, length)
    halo = vmem(CHUNKS, 4, length // CHUNKS // 2, length)
    scratch = [
        vmem(4, *plane), vmem(2, *plane), vmem(slots, 2, *plane),
        vmem16(slots, 2 * length, 2 * length), vmem16(slots, 2 * length, 2 * length),
        vmem(slots, 2, *half),
        vmem(slots, *plane), vmem(slots, *plane), vmem16(slots, 2 * length, length),
        vmem16(slots, length, 2 * length),
        vmem(slots, *plane), vmem(slots, *plane),
        vmem(slots, *plane), vmem(slots, *plane), vmem(slots, *plane), vmem(slots, *plane),
        vmem16(slots, length, 2 * length),
        halo, halo, halo, halo, vmem(*plane), vmem(*plane), vmem(*plane),
        vmem(*plane), vmem(*plane), vmem(*plane), vmem(*plane), vmem(*plane),
        vmem(*plane), vmem(*plane), vmem(*plane), vmem(*plane), vmem(*plane),
        vmem(5, *plane), vmem(5, *half), vmem(5, *plane), vmem(5, *half),
        vmem(5, *quarter), vmem(5, *quarter), vmem(5, *quarter), vmem(5, *quarter),
        vmem(5, *quarter), vmem(5, *quarter),
        pltpu.SMEM((slots, 8), F32),
        pltpu.SemaphoreType.REGULAR,
        pltpu.SemaphoreType.DMA((3,)),
        pltpu.SemaphoreType.DMA((MESSAGES,)),
        pltpu.SemaphoreType.DMA((MESSAGES,)),
    ]
    hbm = pl.BlockSpec(memory_space=pl.ANY)
    smem = pl.BlockSpec(memory_space=pltpu.SMEM)
    return pl.pallas_call(
        functools.partial(kernel, tiles),
        out_shape=pltpu.VMEM(maps.shape, F32),
        in_specs=[hbm, hbm, smem, hbm, smem, smem, smem, smem],
        out_specs=pl.BlockSpec(memory_space=pltpu.VMEM),
        scratch_shapes=scratch,
        compiler_params=pltpu.CompilerParams(
            collective_id=0, has_side_effects=True, vmem_limit_bytes=56 << 20
        ),
    )(maps, measured, offsets, probe, spectrum, wave_index, edge_band.T, band_coef.transpose(1, 0, 2))


def solution(mesh):
    in_specs = (
        P(None, None, "tile"),
        P("tile", None, None),
        P("tile"),
        P("wave", None, None, None),
        P("wave"),
        P("wave"),
        P("wave", None),
        P(),
    )
    return jax.shard_map(
        functools.partial(per_device, mesh.shape["tile"]),
        mesh=mesh,
        in_specs=in_specs,
        out_specs=P(None, None, "tile"),
        check_vma=False,
    )
```

```python
import functools
import math

import jax
import jax.numpy as jnp
from jax import lax
from jax.experimental import pallas as pl
from jax.experimental.pallas import tpu as pltpu
from jax.sharding import PartitionSpec as P

WAVES = 48
RELAX = 4.0
FLOOR = 1.0
MESH = pl.DeviceIdType.MESH
F32 = jnp.float32
BF16 = jnp.bfloat16

SIN = (6.283184916495429, -41.341589232688364, 81.5999433297776, -76.61447253120122, 41.34288235437901, -12.471243534763557)
COS = (0.9999999890590201, -19.739204499453688, 64.93911745988827, -85.45013953077586, 60.16763095018129, -25.96759924584206, 6.528658157862129)

MEAS, PW1, PWR, PWA, PWB, IN1, IN1B, IN2, IN2M, GR1, GRR, GRA, GRB, OUT = range(14)
XIN1, XIN1B, XIN2, XIN2M, XPW1, XPWB, XGR1, XGRB = range(14, 22)
CHUNKS = 4
HALO, PASS = (22 + CHUNKS * k for k in range(2))
MESSAGES = 22 + CHUNKS * 2


def sincos_turns(turns):
    f = turns - jnp.round(turns)
    z = f * f
    s = jnp.full_like(z, SIN[-1])
    for k in SIN[-2::-1]:
        s = s * z + k
    c = jnp.full_like(z, COS[-1])
    for k in COS[-2::-1]:
        c = c * z + k
    return c, s * f


def swap(x):
    return pltpu.roll(x, 64, x.ndim - 1)


def kernel(
    tiles,
    maps_hbm, meas_hbm, off_hbm, probe_hbm, spec_hbm, wave_hbm, edge_hbm, band_hbm,
    out_ref,
    mp, ms, pb, w1, w2, obj, psir, psii, psib, midb, farr, fari, psirx, psiix, farrx, farix, nbuf,
    left_s, right_s, halo_r, none_r, ma_s, mb_r, none_m, out_half,
    inten, inten_r, pair_i, far_i, sf, intenx, intenx_r, pair_ix, far_ix, sfx,
    acc, acc_r, accx, accx_r,
    rpack, rrecv, lpack, la, lb, lpx,
    off_ref, spec_ref, wave_ref, edge_ref, band_ref, coef, enter, copy_sem, send_sem, recv_sem,
):
    slots = spec_ref.shape[0]
    length = mp.shape[1]
    mid = length // 2
    chunk = length // CHUNKS
    t = lax.axis_index("tile")
    w = lax.axis_index("wave")
    core = lax.rem(w, 2)
    mate = w + 1 - 2 * core
    far_z = lax.rem(w + 2, 4)
    far_mate = lax.rem(mate + 2, 4)
    up = lax.rem(t + 1, tiles)
    down = lax.rem(t + tiles - 1, tiles)
    first = t == 0
    last = t == tiles - 1
    has_down = t > 0
    has_up = t < tiles - 1
    mine = pl.ds(pl.multiple_of(core * mid, mid), mid)
    other = pl.ds(pl.multiple_of((1 - core) * mid, mid), mid)

    barrier = pltpu.get_barrier_semaphore()

    def greet(device):
        pl.semaphore_signal(barrier, inc=1, device_id=device, device_id_type=MESH)

    greet((t, mate))
    @pl.when(w < 2)
    def _():
        greet((t, far_z))
        greet((t, far_mate))

    @pl.when(has_down)
    def _():
        greet((down, w))

    greetings = 1 + 2 * (w // 2) + (2 * tiles - 2 - t) // tiles

    load_maps = pltpu.make_async_copy(maps_hbm, mp, copy_sem.at[0])
    load_meas = pltpu.make_async_copy(meas_hbm, ms, copy_sem.at[1])
    load_probe = pltpu.make_async_copy(probe_hbm, pb, copy_sem.at[2])
    load_maps.start()
    small = [
        pltpu.make_async_copy(source, target, copy_sem.at[3 + k])
        for k, (source, target) in enumerate((
            (off_hbm, off_ref), (spec_hbm, spec_ref), (wave_hbm, wave_ref),
            (edge_hbm, edge_ref), (band_hbm, band_ref),
        ))
    ]
    for copy in small:
        copy.start()
    load_meas.start()
    load_probe.start()

    def remote(k, src, dst, device):
        return pltpu.make_async_remote_copy(
            src_ref=src, dst_ref=dst, send_sem=send_sem.at[k], recv_sem=recv_sem.at[k],
            device_id=device, device_id_type=MESH,
        )

    def low_lanes(rows):
        return lax.broadcasted_iota(jnp.int32, (rows, length), 1) < mid

    def slot_coefficients(s, carry):
        for m in range(4):
            e = edge_ref[m, s]
            for k in range(2):
                c = [band_ref[n, k, m] for n in range(3)]
                coef[s, 4 * k + m] = jnp.where(e == 0, c[0], jnp.where(e == 1, c[1], c[2]))
        return carry

    for copy in small:
        copy.wait()
    lax.fori_loop(0, slots, slot_coefficients, 0)

    def groups(size, body, carry):
        def step(i, carry):
            return body([i * size + j for j in range(size)], carry)

        return lax.fori_loop(0, slots // size, step, carry)

    column = lax.broadcasted_iota(jnp.int32, (32, length), 1) - mid
    row = lax.broadcasted_iota(jnp.int32, (32, length), 0) - mid
    normaliser = 1.0 / math.sqrt(length)

    def table_slot(s, carry):
        which = jnp.full((32, length), wave_ref[s], jnp.int32).astype(F32)
        sampling = (0.6 + 0.4 * which / (WAVES - 1)) * (1.0 / length)
        c, sn = sincos_turns(sampling * (row * column).astype(F32))
        c, sn = c * normaliser, sn * normaliser
        step_c, step_s = sincos_turns(sampling[0:8] * (32 * column[0:8]).astype(F32))
        step_c, step_s = jnp.tile(step_c, (4, 1)), jnp.tile(step_s, (4, 1))
        for r in range(0, length, 32):
            if r:
                c, sn = c * step_c - sn * step_s, c * step_s + sn * step_c
            re = c.astype(BF16)
            im = (-sn).astype(BF16)
            nim = sn.astype(BF16)
            top, low = pl.ds(r, 32), pl.ds(length + r, 32)
            left, right = pl.ds(0, length), pl.ds(length, length)
            w1[s, top, left] = re
            w1[s, top, right] = nim
            w1[s, low, left] = im
            w1[s, low, right] = re
            w2[s, top, left] = re
            w2[s, top, right] = im
            w2[s, low, left] = nim
            w2[s, low, right] = re
        return carry

    load_maps.wait()
    hc = chunk // 2
    low_hc = low_lanes(hc)
    for q in range(CHUNKS):
        r = q * chunk
        for m in range(4):
            top, bottom = mp[m, r : r + hc], mp[m, r + hc : r + chunk]
            left_s[q, m] = jnp.where(low_hc, top, swap(bottom))
            right_s[q, m] = jnp.where(low_hc, swap(top), bottom)

    pl.semaphore_wait(barrier, greetings)

    @pl.when(w >= 2)
    def _():
        for device in ((t, far_z), (t, far_mate)):
            pl.semaphore_signal(enter, inc=1, device_id=device, device_id_type=MESH)


    def transmission(s, planes):
        a = [coef[s, m] for m in range(4)]
        b = [coef[s, 4 + m] for m in range(4)]
        absorb = a[0] * planes[0] + a[1] * planes[1] + a[2] * planes[2] + a[3] * planes[3]
        phase = b[0] * planes[0] + b[1] * planes[1] + b[2] * planes[2] + b[3] * planes[3]
        damping = jnp.exp(-absorb)
        c, sn = sincos_turns(phase * (0.5 / math.pi))
        return damping * c, damping * sn

    def half_object(packed):
        def body(group, carry):
            for q in range(CHUNKS):
                planes = [packed[q, m] for m in range(4)]
                for s in group:
                    re, im = transmission(s, planes)
                    obj[s, 0, pl.ds(q * hc, hc), :] = re
                    obj[s, 1, pl.ds(q * hc, hc), :] = im
            return carry

        groups(12, body, 0)

    def waves_at_object(q, packed, pr, pi, power, fresh_low=False):
        at = pl.ds(q * hc, hc)

        def body(group, totals):
            totals = list(totals)
            planes = [packed[q, m] for m in range(4)]
            for s in group:
                nre, nim = transmission(s, planes)
                ore, oim = obj[s, 0, at, :], obj[s, 1, at, :]
                if fresh_low:
                    nre, nim, ore, oim = ore, oim, nre, nim
                for half, (re, im) in enumerate((
                    (jnp.where(low_hc, ore, swap(nre)), jnp.where(low_hc, oim, swap(nim))),
                    (jnp.where(low_hc, swap(ore), nre), jnp.where(low_hc, swap(oim), nim)),
                )):
                    rows = pl.ds(q * chunk + half * hc, hc)
                    p_re, p_im = pb[s, 0, rows, :], pb[s, 1, rows, :]
                    x = p_re * re - p_im * im
                    y = p_re * im + p_im * re
                    pr[s, rows, :] = x
                    pi[s, rows, :] = y
                    psib[s, rows, :] = x.astype(BF16)
                    psib[s, pl.ds(length + q * chunk + half * hc, hc), :] = y.astype(BF16)
                    totals[half] = totals[half] + spec_ref[s] * (x * x + y * y)
            return tuple(totals)

        zero = jnp.zeros((hc, length), F32)
        for half, total in enumerate(groups(12, body, (zero, zero))):
            power[pl.ds(q * chunk + half * hc, hc), :] = total

    def left_forward():
        def body(group, carry):
            for s in group:
                m = jnp.dot(w1[s], psib[s], preferred_element_type=F32).astype(BF16)
                midb[s, :, 0:length] = m[:length]
                midb[s, :, length : 2 * length] = m[length:]
            return carry

        groups(12, body, 0)

    def right_forward(rows_at, fr, fi, total):
        rows = pl.ds(pl.multiple_of(rows_at, mid), mid)

        def body(group, light):
            for s in group:
                far = jnp.dot(midb[s, rows, :], w2[s], preferred_element_type=F32)
                x, y = far[:, :length], far[:, length:]
                fr[s, rows, :] = x
                fi[s, rows, :] = y
                light = light + spec_ref[s] * (x * x + y * y)
            return light

        total[rows, :] = groups(12, body, jnp.zeros((mid, length), F32))

    def back_left(short, fr, fi):
        def body(group, carry):
            for s in group:
                factor = spec_ref[s] * short[...]
                d = jnp.concatenate(
                    [(factor * fr[s]).astype(BF16), (factor * fi[s]).astype(BF16)], axis=0
                )
                nb = jnp.dot(w2[s], d, preferred_element_type=F32).astype(BF16)
                nbuf[s, :, 0:length] = nb[:length]
                nbuf[s, :, length : 2 * length] = nb[length:]
            return carry

        groups(12, body, 0)

    def back_right(rows_at, pr, pi, into):
        rows = pl.ds(pl.multiple_of(rows_at, mid), mid)
        for m in range(4):
            into[m, rows, :] = jnp.zeros((mid, length), F32)

        def body(group, carry):
            back = [jnp.dot(nbuf[s, rows, :], w1[s], preferred_element_type=F32) for s in group]
            for r in range(0, mid, 16):
                part = pl.ds(pl.multiple_of(rows_at + r, 16), 16)
                sums = [into[m, part, :] for m in range(4)]
                for s, both in zip(group, back):
                    br, bi = both[r : r + 16, :length], both[r : r + 16, length:]
                    x, y = pr[s, part, :], pi[s, part, :]
                    cr = x * br + y * bi
                    ci = x * bi - y * br
                    for m in range(4):
                        sums[m] = sums[m] + (coef[s, 4 + m] * ci - coef[s, m] * cr)
                for m in range(4):
                    into[m, part, :] = sums[m]
            return carry

        groups(12, body, 0)

    at_mine, at_other = core * mid, (1 - core) * mid
    frames_here = jnp.where(first, 1.0, 2.0)
    quarter = mid // 2

    def pack_right(y):
        return jnp.where(low_lanes(quarter), swap(y[:quarter]), y[quarter:])

    def pack_left(y):
        return jnp.where(low_lanes(quarter), y[:quarter], swap(y[quarter:]))

    four = pl.ds(0, 4)
    sx_in1 = remote(XIN1, intenx.at[other], intenx_r.at[other], (t, mate))
    sx_in1b = remote(XIN1B, intenx.at[mine], intenx_r.at[mine], (t, mate))
    sx_in2 = remote(XIN2, pair_ix.at[mine], far_ix.at[mine], (t, far_z))
    sx_in2m = remote(XIN2M, pair_ix.at[mine], far_ix.at[mine], (t, far_mate))
    sx_pw1 = remote(XPW1, accx.at[4, other], accx_r.at[4], (t, mate))
    sx_pwb = remote(XPWB, lpx.at[4], lb.at[4], (t, far_z))
    sx_gr1 = remote(XGR1, accx.at[four, other], accx_r.at[four], (t, mate))
    sx_grb = remote(XGRB, lpx.at[four], lb.at[four], (t, far_z))

    def light_of_both(partial, received, pair, first_half, second_half, far_one, far_two):
        second_half.start()
        first_half.wait_recv()
        pair[mine, :] = partial[mine, :] + received[mine, :]
        far_one.start()
        far_two.start()

    def factors(partial, received, pair, far, one, two, frames, into):
        pair[other, :] = partial[other, :] + received[other, :]
        for r in range(0, length, 32):
            rows = pl.ds(r, 32)
            inv = 1.0 / jnp.maximum(pair[rows, :] + far[rows, :], FLOOR)
            into[rows, :] = jnp.sqrt(one[rows, :] * inv) + jnp.sqrt(two[rows, :] * inv) - frames

    def extra_forward():
        sx_pw1.start()
        left_forward()
        right_forward(at_other, farrx, farix, intenx)
        sx_in1.start()
        right_forward(at_mine, farrx, farix, intenx)
        light_of_both(intenx, intenx_r, pair_ix, sx_in1, sx_in1b, sx_in2, sx_in2m)
        sx_pw1.wait_recv()
        lpx[4] = pack_left(accx[4, mine, :] + accx_r[4])
        sx_pwb.start()

    def extra_shortfall():
        sx_in1b.wait_recv()
        sx_in2.wait_recv()
        sx_in2m.wait_recv()
        factors(intenx, intenx_r, pair_ix, far_ix, ms.at[1], none_m, 1.0, sfx)

    def extra_backward():
        back_left(sfx, farrx, farix)
        back_right(at_other, psirx, psiix, accx)
        sx_gr1.start()
        back_right(at_mine, psirx, psiix, accx)
        sx_gr1.wait_recv()
        for m in range(4):
            lpx[m] = pack_left(accx[m, mine, :] + accx_r[m])
        sx_grb.start()

    @pl.when(first)
    def _():
        halo_r[...] = jnp.zeros_like(halo_r)
        mb_r[...] = jnp.zeros_like(mb_r)

    @pl.when(last)
    def _():
        none_r[...] = jnp.zeros_like(none_r)
        none_m[...] = jnp.zeros_like(none_m)

    fetches = core == 1
    send_halo = [remote(HALO + q, right_s.at[q], halo_r.at[q], (up, w)) for q in range(CHUNKS)]
    pass_halo = [remote(PASS + q, halo_r.at[q], halo_r.at[q], (t, mate)) for q in range(CHUNKS)]
    send_meas = remote(MEAS, ms.at[1], mb_r, (up, w))

    @pl.when(fetches & has_up)
    def _():
        for copy in send_halo:
            copy.start()

    load_meas.wait()
    low_first = off_ref[0] < off_ref[1]
    for r in range(0, length, 32):
        rows = pl.ds(r, 32)
        one, two = ms[0, rows, :], ms[1, rows, :]
        ma_s[rows, :] = jnp.where(low_first, one, two)
        ms[1, rows, :] = jnp.where(low_first, two, one)

    groups(4, lambda group, carry: [table_slot(s, carry) for s in group][0], 0)

    half_object(left_s)

    load_probe.wait()

    def arrived(q):
        @pl.when(has_down & fetches)
        def _():
            send_halo[q].wait_recv()
            pass_halo[q].start()

    arrived(0)
    for q in range(CHUNKS):
        if q + 1 < CHUNKS:
            arrived(q + 1)

        @pl.when(has_down & jnp.logical_not(fetches))
        def _():
            pass_halo[q].wait_recv()

        waves_at_object(q, halo_r, psir, psii, acc.at[4], fresh_low=True)

        if q == 1:

            @pl.when(has_up)
            def _():
                send_meas.start()

    s_pw1 = remote(PW1, acc.at[4, other], acc_r.at[4], (t, mate))
    s_in1 = remote(IN1, inten.at[other], inten_r.at[other], (t, mate))
    s_in1b = remote(IN1B, inten.at[mine], inten_r.at[mine], (t, mate))
    s_in2 = remote(IN2, pair_i.at[mine], far_i.at[mine], (t, far_z))
    s_in2m = remote(IN2M, pair_i.at[mine], far_i.at[mine], (t, far_mate))
    s_gr1 = remote(GR1, acc.at[four, other], acc_r.at[four], (t, mate))
    s_pwr = remote(PWR, rpack.at[4], rrecv.at[4], (t, far_z))
    s_pwa = remote(PWA, lpack.at[4], la.at[4], (down, w))
    s_pwb = remote(PWB, lpack.at[4], lb.at[4], (down, far_z))
    s_grr = remote(GRR, rpack.at[four], rrecv.at[four], (t, far_z))
    s_gra = remote(GRA, lpack.at[four], la.at[four], (down, w))
    s_grb = remote(GRB, lpack.at[four], lb.at[four], (down, far_z))

    s_pw1.start()
    left_forward()
    right_forward(at_other, farr, fari, inten)
    s_in1.start()
    right_forward(at_mine, farr, fari, inten)

    @pl.when(w < 2)
    def _():
        pl.semaphore_wait(enter, 2)

    light_of_both(inten, inten_r, pair_i, s_in1, s_in1b, s_in2, s_in2m)

    s_pw1.wait_recv()
    power = frames_here * (acc[4, mine, :] + acc_r[4])
    lpack[4] = pack_left(power)
    rpack[4] = pack_right(power)

    @pl.when(last)
    def _():
        half_object(right_s)
        for q in range(CHUNKS):
            waves_at_object(q, none_r, psirx, psiix, accx.at[4])
        extra_forward()

    @pl.when(has_down)
    def _():
        send_meas.wait_recv()

    s_in1b.wait_recv()
    s_in2.wait_recv()
    s_in2m.wait_recv()
    factors(inten, inten_r, pair_i, far_i, ma_s, mb_r, frames_here, sf)
    s_pwr.start()


    @pl.when(has_down)
    def _():
        s_pwa.start()
        s_pwb.start()

    back_left(sf, farr, fari)
    back_right(at_other, psir, psii, acc)
    s_gr1.start()
    back_right(at_mine, psir, psii, acc)
    s_gr1.wait_recv()
    for m in range(4):
        y = acc[m, mine, :] + acc_r[m]
        lpack[m] = pack_left(y)
        rpack[m] = pack_right(y)

    @pl.when(has_down)
    def _():
        s_grb.start()

    s_grr.start()

    @pl.when(has_down)
    def _():
        s_gra.start()

    @pl.when(last)
    def _():
        extra_shortfall()
        extra_backward()
        sx_pwb.wait_recv()
        sx_grb.wait_recv()
        la[...] = lpx[...]

    @pl.when(has_up)
    def _():
        s_pwa.wait_recv()
        s_pwb.wait_recv()
        s_gra.wait_recv()
        s_grb.wait_recv()

    s_pwr.wait_recv()
    s_grr.wait_recv()

    def totals(m):
        l = la[m] + lb[m]
        r = rpack[m] + rrecv[m]
        return jnp.where(low_lanes(quarter), r, swap(l)), jnp.where(low_lanes(quarter), swap(r), l)

    powers = [RELAX / (p + 1.0) for p in totals(4)]
    for m in range(4):
        for q, total in enumerate(totals(m)):
            rows = pl.ds(pl.multiple_of(at_mine + q * quarter, quarter), quarter)
            out_half[m, q * quarter : (q + 1) * quarter, :] = mp[m, rows, :] + total * powers[q]
    s_out = remote(OUT, out_half, out_ref.at[:, mine], (t, mate))
    s_out.start()
    keep_out = pltpu.make_async_copy(out_half, out_ref.at[:, mine], copy_sem.at[8])
    keep_out.start()

    for copy in (s_pw1, s_in1, s_in1b, s_in2, s_in2m, s_gr1, s_pwr, s_grr):
        copy.wait_send()

    @pl.when(has_up)
    def _():
        send_meas.wait_send()

    @pl.when(has_up & fetches)
    def _():
        for copy in send_halo:
            copy.wait_send()

    @pl.when(has_down & fetches)
    def _():
        for copy in pass_halo:
            copy.wait_send()

    @pl.when(has_down)
    def _():
        for copy in (s_pwa, s_pwb, s_gra, s_grb):
            copy.wait_send()

    @pl.when(last)
    def _():
        for copy in (sx_in1, sx_in1b, sx_in2, sx_in2m, sx_pw1, sx_pwb, sx_gr1, sx_grb):
            copy.wait_send()

    keep_out.wait()
    s_out.wait()


def per_device(tiles, maps, measured, offsets, probe, spectrum, wave_index, edge_band, band_coef):
    _, length, columns = maps.shape
    slots = spectrum.shape[0]
    mid = length // 2
    vmem = lambda *shape: pltpu.VMEM(shape, F32)
    vmem16 = lambda *shape: pltpu.VMEM(shape, BF16)
    plane = (length, length)
    half = (mid, length)
    quarter = (mid // 2, length)
    halo = vmem(CHUNKS, 4, length // CHUNKS // 2, length)
    scratch = [
        vmem(4, *plane), vmem(2, *plane), vmem(slots, 2, *plane),
        vmem16(slots, 2 * length, 2 * length), vmem16(slots, 2 * length, 2 * length),
        vmem(slots, 2, *half),
        vmem(slots, *plane), vmem(slots, *plane), vmem16(slots, 2 * length, length),
        vmem16(slots, length, 2 * length),
        vmem(slots, *plane), vmem(slots, *plane),
        vmem(slots, *plane), vmem(slots, *plane), vmem(slots, *plane), vmem(slots, *plane),
        vmem16(slots, length, 2 * length),
        halo, halo, halo, halo, vmem(*plane), vmem(*plane), vmem(*plane), vmem(4, *half),
        vmem(*plane), vmem(*plane), vmem(*plane), vmem(*plane), vmem(*plane),
        vmem(*plane), vmem(*plane), vmem(*plane), vmem(*plane), vmem(*plane),
        vmem(5, *plane), vmem(5, *half), vmem(5, *plane), vmem(5, *half),
        vmem(5, *quarter), vmem(5, *quarter), vmem(5, *quarter), vmem(5, *quarter),
        vmem(5, *quarter), vmem(5, *quarter),
        pltpu.SMEM(offsets.shape, jnp.int32),
        pltpu.SMEM((slots,), F32),
        pltpu.SMEM((slots,), jnp.int32),
        pltpu.SMEM((4, slots), jnp.int32),
        pltpu.SMEM((3, 2, 4), F32),
        pltpu.SMEM((slots, 8), F32),
        pltpu.SemaphoreType.REGULAR,
        pltpu.SemaphoreType.DMA((9,)),
        pltpu.SemaphoreType.DMA((MESSAGES,)),
        pltpu.SemaphoreType.DMA((MESSAGES,)),
    ]
    hbm = pl.BlockSpec(memory_space=pl.ANY)
    return pl.pallas_call(
        functools.partial(kernel, tiles),
        out_shape=pltpu.VMEM(maps.shape, F32),
        in_specs=[hbm] * 8,
        out_specs=pl.BlockSpec(memory_space=pl.ANY),
        scratch_shapes=scratch,
        compiler_params=pltpu.CompilerParams(
            collective_id=0, has_side_effects=True, vmem_limit_bytes=56 << 20
        ),
    )(maps, measured, offsets, probe, spectrum, wave_index, edge_band.T, band_coef.transpose(1, 0, 2))


def solution(mesh):
    in_specs = (
        P(None, None, "tile"),
        P("tile", None, None),
        P("tile"),
        P("wave", None, None, None),
        P("wave"),
        P("wave"),
        P("wave", None),
        P(),
    )
    return jax.shard_map(
        functools.partial(per_device, mesh.shape["tile"]),
        mesh=mesh,
        in_specs=in_specs,
        out_specs=P(None, None, "tile"),
        check_vma=False,
    )
```

```python
import functools
import math

import jax
import jax.numpy as jnp
from jax import lax
from jax.experimental import pallas as pl
from jax.experimental.pallas import tpu as pltpu
from jax.sharding import PartitionSpec as P

WAVES = 48
RELAX = 4.0
FLOOR = 1.0
MESH = pl.DeviceIdType.MESH
F32 = jnp.float32
BF16 = jnp.bfloat16

SIN = (6.283184916495429, -41.341589232688364, 81.5999433297776, -76.61447253120122, 41.34288235437901, -12.471243534763557)
COS = (0.9999999890590201, -19.739204499453688, 64.93911745988827, -85.45013953077586, 60.16763095018129, -25.96759924584206, 6.528658157862129)

MEAS, PW1, PWR, PWA, PWB, IN1, IN1B, IN2, IN2M, GR1, GRR, GRA, GRB, OUT = range(14)
XIN1, XIN1B, XIN2, XIN2M, XPW1, XPWB, XGR1, XGRB = range(14, 22)
CHUNKS = 4
HALO, PASS = (22 + CHUNKS * k for k in range(2))
MESSAGES = 22 + CHUNKS * 2


def sincos_turns(turns):
    f = turns - jnp.round(turns)
    z = f * f
    s = jnp.full_like(z, SIN[-1])
    for k in SIN[-2::-1]:
        s = s * z + k
    c = jnp.full_like(z, COS[-1])
    for k in COS[-2::-1]:
        c = c * z + k
    return c, s * f


def swap(x):
    return pltpu.roll(x, 64, x.ndim - 1)


def kernel(
    tiles,
    maps_hbm, meas_hbm, off_hbm, probe_hbm, spec_hbm, wave_hbm, edge_hbm, band_hbm,
    out_ref,
    mp, ms, pb, w1, w2, obj, psir, psii, psib, midb, farr, fari, psirx, psiix, farrx, farix, nbuf,
    left_s, right_s, halo_r, none_r, ma_s, mb_r, none_m, out_half,
    inten, inten_r, pair_i, far_i, sf, intenx, intenx_r, pair_ix, far_ix, sfx,
    acc, acc_r, accx, accx_r,
    rpack, rrecv, lpack, la, lb, lpx,
    off_ref, spec_ref, wave_ref, edge_ref, band_ref, coef, enter, copy_sem, send_sem, recv_sem,
):
    slots = spec_ref.shape[0]
    length = mp.shape[1]
    mid = length // 2
    chunk = length // CHUNKS
    t = lax.axis_index("tile")
    w = lax.axis_index("wave")
    core = lax.rem(w, 2)
    mate = w + 1 - 2 * core
    far_z = lax.rem(w + 2, 4)
    far_mate = lax.rem(mate + 2, 4)
    up = lax.rem(t + 1, tiles)
    down = lax.rem(t + tiles - 1, tiles)
    first = t == 0
    last = t == tiles - 1
    has_down = t > 0
    has_up = t < tiles - 1
    mine = pl.ds(pl.multiple_of(core * mid, mid), mid)
    other = pl.ds(pl.multiple_of((1 - core) * mid, mid), mid)

    barrier = pltpu.get_barrier_semaphore()

    def greet(device):
        pl.semaphore_signal(barrier, inc=1, device_id=device, device_id_type=MESH)

    greet((t, mate))
    @pl.when(w < 2)
    def _():
        greet((t, far_z))
        greet((t, far_mate))

    @pl.when(has_down)
    def _():
        greet((down, w))

    greetings = 1 + 2 * (w // 2) + (2 * tiles - 2 - t) // tiles

    load_maps = pltpu.make_async_copy(maps_hbm, mp, copy_sem.at[0])
    load_meas = pltpu.make_async_copy(meas_hbm, ms, copy_sem.at[1])
    load_probe = pltpu.make_async_copy(probe_hbm, pb, copy_sem.at[2])
    load_maps.start()
    small = [
        pltpu.make_async_copy(source, target, copy_sem.at[3 + k])
        for k, (source, target) in enumerate((
            (off_hbm, off_ref), (spec_hbm, spec_ref), (wave_hbm, wave_ref),
            (edge_hbm, edge_ref), (band_hbm, band_ref),
        ))
    ]
    for copy in small:
        copy.start()
    load_meas.start()
    load_probe.start()

    def remote(k, src, dst, device):
        return pltpu.make_async_remote_copy(
            src_ref=src, dst_ref=dst, send_sem=send_sem.at[k], recv_sem=recv_sem.at[k],
            device_id=device, device_id_type=MESH,
        )

    def low_lanes(rows):
        return lax.broadcasted_iota(jnp.int32, (rows, length), 1) < mid

    def slot_coefficients(s, carry):
        for m in range(4):
            e = edge_ref[m, s]
            for k in range(2):
                c = [band_ref[n, k, m] for n in range(3)]
                coef[s, 4 * k + m] = jnp.where(e == 0, c[0], jnp.where(e == 1, c[1], c[2]))
        return carry

    for copy in small:
        copy.wait()
    lax.fori_loop(0, slots, slot_coefficients, 0)

    def groups(size, body, carry):
        def step(i, carry):
            return body([i * size + j for j in range(size)], carry)

        return lax.fori_loop(0, slots // size, step, carry)

    column = lax.broadcasted_iota(jnp.int32, (32, length), 1) - mid
    row = lax.broadcasted_iota(jnp.int32, (32, length), 0) - mid
    normaliser = 1.0 / math.sqrt(length)

    def table_slot(s, carry):
        which = jnp.full((32, length), wave_ref[s], jnp.int32).astype(F32)
        sampling = (0.6 + 0.4 * which / (WAVES - 1)) * (1.0 / length)
        c, sn = sincos_turns(sampling * (row * column).astype(F32))
        c, sn = c * normaliser, sn * normaliser
        step_c, step_s = sincos_turns(sampling[0:8] * (32 * column[0:8]).astype(F32))
        step_c, step_s = jnp.tile(step_c, (4, 1)), jnp.tile(step_s, (4, 1))
        for r in range(0, length, 32):
            if r:
                c, sn = c * step_c - sn * step_s, c * step_s + sn * step_c
            re = c.astype(BF16)
            im = (-sn).astype(BF16)
            nim = sn.astype(BF16)
            top, low = pl.ds(r, 32), pl.ds(length + r, 32)
            left, right = pl.ds(0, length), pl.ds(length, length)
            w1[s, top, left] = re
            w1[s, top, right] = nim
            w1[s, low, left] = im
            w1[s, low, right] = re
            w2[s, top, left] = re
            w2[s, top, right] = im
            w2[s, low, left] = nim
            w2[s, low, right] = re
        return carry

    load_maps.wait()
    hc = chunk // 2
    low_hc = low_lanes(hc)
    for q in range(CHUNKS):
        r = q * chunk
        for m in range(4):
            top, bottom = mp[m, r : r + hc], mp[m, r + hc : r + chunk]
            left_s[q, m] = jnp.where(low_hc, top, swap(bottom))
            right_s[q, m] = jnp.where(low_hc, swap(top), bottom)

    pl.semaphore_wait(barrier, greetings)

    @pl.when(w >= 2)
    def _():
        for device in ((t, far_z), (t, far_mate)):
            pl.semaphore_signal(enter, inc=1, device_id=device, device_id_type=MESH)


    def transmission(s, planes):
        a = [coef[s, m] for m in range(4)]
        b = [coef[s, 4 + m] for m in range(4)]
        absorb = a[0] * planes[0] + a[1] * planes[1] + a[2] * planes[2] + a[3] * planes[3]
        phase = b[0] * planes[0] + b[1] * planes[1] + b[2] * planes[2] + b[3] * planes[3]
        damping = jnp.exp(-absorb)
        c, sn = sincos_turns(phase * (0.5 / math.pi))
        return damping * c, damping * sn

    def half_object(packed):
        def body(group, carry):
            for q in range(CHUNKS):
                planes = [packed[q, m] for m in range(4)]
                for s in group:
                    re, im = transmission(s, planes)
                    obj[s, 0, pl.ds(q * hc, hc), :] = re
                    obj[s, 1, pl.ds(q * hc, hc), :] = im
            return carry

        groups(12, body, 0)

    def waves_at_object(q, packed, pr, pi, power, fresh_low=False):
        at = pl.ds(q * hc, hc)

        def body(group, totals):
            totals = list(totals)
            planes = [packed[q, m] for m in range(4)]
            for s in group:
                nre, nim = transmission(s, planes)
                ore, oim = obj[s, 0, at, :], obj[s, 1, at, :]
                if fresh_low:
                    nre, nim, ore, oim = ore, oim, nre, nim
                for half, (re, im) in enumerate((
                    (jnp.where(low_hc, ore, swap(nre)), jnp.where(low_hc, oim, swap(nim))),
                    (jnp.where(low_hc, swap(ore), nre), jnp.where(low_hc, swap(oim), nim)),
                )):
                    rows = pl.ds(q * chunk + half * hc, hc)
                    p_re, p_im = pb[s, 0, rows, :], pb[s, 1, rows, :]
                    x = p_re * re - p_im * im
                    y = p_re * im + p_im * re
                    pr[s, rows, :] = x
                    pi[s, rows, :] = y
                    psib[s, rows, :] = x.astype(BF16)
                    psib[s, pl.ds(length + q * chunk + half * hc, hc), :] = y.astype(BF16)
                    totals[half] = totals[half] + spec_ref[s] * (x * x + y * y)
            return tuple(totals)

        zero = jnp.zeros((hc, length), F32)
        for half, total in enumerate(groups(12, body, (zero, zero))):
            power[pl.ds(q * chunk + half * hc, hc), :] = total

    def left_forward():
        def body(group, carry):
            for s in group:
                m = jnp.dot(w1[s], psib[s], preferred_element_type=F32).astype(BF16)
                midb[s, :, 0:length] = m[:length]
                midb[s, :, length : 2 * length] = m[length:]
            return carry

        groups(12, body, 0)

    def right_forward(rows_at, fr, fi, total):
        rows = pl.ds(pl.multiple_of(rows_at, mid), mid)

        def body(group, light):
            for s in group:
                far = jnp.dot(midb[s, rows, :], w2[s], preferred_element_type=F32)
                x, y = far[:, :length], far[:, length:]
                fr[s, rows, :] = x
                fi[s, rows, :] = y
                light = light + spec_ref[s] * (x * x + y * y)
            return light

        total[rows, :] = groups(12, body, jnp.zeros((mid, length), F32))

    def back_left(short, fr, fi):
        def body(group, carry):
            for s in group:
                factor = spec_ref[s] * short[...]
                d = jnp.concatenate(
                    [(factor * fr[s]).astype(BF16), (factor * fi[s]).astype(BF16)], axis=0
                )
                nb = jnp.dot(w2[s], d, preferred_element_type=F32).astype(BF16)
                nbuf[s, :, 0:length] = nb[:length]
                nbuf[s, :, length : 2 * length] = nb[length:]
            return carry

        groups(12, body, 0)

    def back_right(rows_at, pr, pi, into):
        rows = pl.ds(pl.multiple_of(rows_at, mid), mid)
        for m in range(4):
            into[m, rows, :] = jnp.zeros((mid, length), F32)

        def body(group, carry):
            back = [jnp.dot(nbuf[s, rows, :], w1[s], preferred_element_type=F32) for s in group]
            for r in range(0, mid, 16):
                part = pl.ds(pl.multiple_of(rows_at + r, 16), 16)
                sums = [into[m, part, :] for m in range(4)]
                for s, both in zip(group, back):
                    br, bi = both[r : r + 16, :length], both[r : r + 16, length:]
                    x, y = pr[s, part, :], pi[s, part, :]
                    cr = x * br + y * bi
                    ci = x * bi - y * br
                    for m in range(4):
                        sums[m] = sums[m] + (coef[s, 4 + m] * ci - coef[s, m] * cr)
                for m in range(4):
                    into[m, part, :] = sums[m]
            return carry

        groups(12, body, 0)

    at_mine, at_other = core * mid, (1 - core) * mid
    frames_here = jnp.where(first, 1.0, 2.0)
    quarter = mid // 2

    def pack_right(y):
        return jnp.where(low_lanes(quarter), swap(y[:quarter]), y[quarter:])

    def pack_left(y):
        return jnp.where(low_lanes(quarter), y[:quarter], swap(y[quarter:]))

    four = pl.ds(0, 4)
    sx_in1 = remote(XIN1, intenx.at[other], intenx_r.at[other], (t, mate))
    sx_in1b = remote(XIN1B, intenx.at[mine], intenx_r.at[mine], (t, mate))
    sx_in2 = remote(XIN2, pair_ix.at[mine], far_ix.at[mine], (t, far_z))
    sx_in2m = remote(XIN2M, pair_ix.at[mine], far_ix.at[mine], (t, far_mate))
    sx_pw1 = remote(XPW1, accx.at[4, other], accx_r.at[4], (t, mate))
    sx_pwb = remote(XPWB, lpx.at[4], lb.at[4], (t, far_z))
    sx_gr1 = remote(XGR1, accx.at[four, other], accx_r.at[four], (t, mate))
    sx_grb = remote(XGRB, lpx.at[four], lb.at[four], (t, far_z))

    def light_of_both(partial, received, pair, first_half, second_half, far_one, far_two):
        second_half.start()
        first_half.wait_recv()
        pair[mine, :] = partial[mine, :] + received[mine, :]
        far_one.start()
        far_two.start()

    def factors(partial, received, pair, far, one, two, frames, into):
        pair[other, :] = partial[other, :] + received[other, :]
        for r in range(0, length, 32):
            rows = pl.ds(r, 32)
            inv = 1.0 / jnp.maximum(pair[rows, :] + far[rows, :], FLOOR)
            into[rows, :] = jnp.sqrt(one[rows, :] * inv) + jnp.sqrt(two[rows, :] * inv) - frames

    def extra_forward():
        sx_pw1.start()
        left_forward()
        right_forward(at_other, farrx, farix, intenx)
        sx_in1.start()
        right_forward(at_mine, farrx, farix, intenx)
        light_of_both(intenx, intenx_r, pair_ix, sx_in1, sx_in1b, sx_in2, sx_in2m)
        sx_pw1.wait_recv()
        lpx[4] = pack_left(accx[4, mine, :] + accx_r[4])
        sx_pwb.start()

    def extra_shortfall():
        sx_in1b.wait_recv()
        sx_in2.wait_recv()
        sx_in2m.wait_recv()
        factors(intenx, intenx_r, pair_ix, far_ix, ms.at[1], none_m, 1.0, sfx)

    def extra_backward():
        back_left(sfx, farrx, farix)
        back_right(at_other, psirx, psiix, accx)
        sx_gr1.start()
        back_right(at_mine, psirx, psiix, accx)
        sx_gr1.wait_recv()
        for m in range(4):
            lpx[m] = pack_left(accx[m, mine, :] + accx_r[m])
        sx_grb.start()

    @pl.when(first)
    def _():
        halo_r[...] = jnp.zeros_like(halo_r)
        mb_r[...] = jnp.zeros_like(mb_r)

    @pl.when(last)
    def _():
        none_r[...] = jnp.zeros_like(none_r)
        none_m[...] = jnp.zeros_like(none_m)

    fetches = core == 1
    send_halo = [remote(HALO + q, right_s.at[q], halo_r.at[q], (up, w)) for q in range(CHUNKS)]
    pass_halo = [remote(PASS + q, halo_r.at[q], halo_r.at[q], (t, mate)) for q in range(CHUNKS)]
    send_meas = remote(MEAS, ms.at[1], mb_r, (up, w))

    @pl.when(fetches & has_up)
    def _():
        for copy in send_halo:
            copy.start()

    load_meas.wait()
    low_first = off_ref[0] < off_ref[1]
    for r in range(0, length, 32):
        rows = pl.ds(r, 32)
        one, two = ms[0, rows, :], ms[1, rows, :]
        ma_s[rows, :] = jnp.where(low_first, one, two)
        ms[1, rows, :] = jnp.where(low_first, two, one)

    groups(4, lambda group, carry: [table_slot(s, carry) for s in group][0], 0)

    half_object(left_s)

    load_probe.wait()

    def arrived(q):
        @pl.when(has_down & fetches)
        def _():
            send_halo[q].wait_recv()
            pass_halo[q].start()

    arrived(0)
    for q in range(CHUNKS):
        if q + 1 < CHUNKS:
            arrived(q + 1)

        @pl.when(has_down & jnp.logical_not(fetches))
        def _():
            pass_halo[q].wait_recv()

        waves_at_object(q, halo_r, psir, psii, acc.at[4], fresh_low=True)

        if q == 1:

            @pl.when(has_up)
            def _():
                send_meas.start()

    s_pw1 = remote(PW1, acc.at[4, other], acc_r.at[4], (t, mate))
    s_in1 = remote(IN1, inten.at[other], inten_r.at[other], (t, mate))
    s_in1b = remote(IN1B, inten.at[mine], inten_r.at[mine], (t, mate))
    s_in2 = remote(IN2, pair_i.at[mine], far_i.at[mine], (t, far_z))
    s_in2m = remote(IN2M, pair_i.at[mine], far_i.at[mine], (t, far_mate))
    s_gr1 = remote(GR1, acc.at[four, other], acc_r.at[four], (t, mate))
    s_pwr = remote(PWR, rpack.at[4], rrecv.at[4], (t, far_z))
    s_pwa = remote(PWA, lpack.at[4], la.at[4], (down, w))
    s_pwb = remote(PWB, lpack.at[4], lb.at[4], (down, far_z))
    s_grr = remote(GRR, rpack.at[four], rrecv.at[four], (t, far_z))
    s_gra = remote(GRA, lpack.at[four], la.at[four], (down, w))
    s_grb = remote(GRB, lpack.at[four], lb.at[four], (down, far_z))

    s_pw1.start()
    left_forward()
    right_forward(at_other, farr, fari, inten)
    s_in1.start()
    right_forward(at_mine, farr, fari, inten)

    @pl.when(w < 2)
    def _():
        pl.semaphore_wait(enter, 2)

    light_of_both(inten, inten_r, pair_i, s_in1, s_in1b, s_in2, s_in2m)

    s_pw1.wait_recv()
    power = frames_here * (acc[4, mine, :] + acc_r[4])
    lpack[4] = pack_left(power)
    rpack[4] = pack_right(power)

    @pl.when(last)
    def _():
        half_object(right_s)
        for q in range(CHUNKS):
            waves_at_object(q, none_r, psirx, psiix, accx.at[4])
        extra_forward()

    @pl.when(has_down)
    def _():
        send_meas.wait_recv()

    s_in1b.wait_recv()
    s_in2.wait_recv()
    s_in2m.wait_recv()
    factors(inten, inten_r, pair_i, far_i, ma_s, mb_r, frames_here, sf)
    s_pwr.start()


    @pl.when(has_down)
    def _():
        s_pwa.start()
        s_pwb.start()

    back_left(sf, farr, fari)
    back_right(at_other, psir, psii, acc)
    s_gr1.start()
    back_right(at_mine, psir, psii, acc)
    s_gr1.wait_recv()
    for m in range(4):
        y = acc[m, mine, :] + acc_r[m]
        lpack[m] = pack_left(y)
        rpack[m] = pack_right(y)

    near = w < 2

    @pl.when(has_down & near)
    def _():
        s_gra.start()

    @pl.when(has_down)
    def _():
        s_grb.start()

    s_grr.start()

    @pl.when(has_down & jnp.logical_not(near))
    def _():
        s_gra.start()

    @pl.when(last)
    def _():
        extra_shortfall()
        extra_backward()
        sx_pwb.wait_recv()
        sx_grb.wait_recv()
        la[...] = lpx[...]

    @pl.when(has_up)
    def _():
        s_pwa.wait_recv()
        s_pwb.wait_recv()
        s_gra.wait_recv()
        s_grb.wait_recv()

    s_pwr.wait_recv()
    s_grr.wait_recv()

    def totals(m):
        l = la[m] + lb[m]
        r = rpack[m] + rrecv[m]
        return jnp.where(low_lanes(quarter), r, swap(l)), jnp.where(low_lanes(quarter), swap(r), l)

    powers = [RELAX / (p + 1.0) for p in totals(4)]
    for m in range(4):
        for q, total in enumerate(totals(m)):
            rows = pl.ds(pl.multiple_of(at_mine + q * quarter, quarter), quarter)
            out_half[m, q * quarter : (q + 1) * quarter, :] = mp[m, rows, :] + total * powers[q]
    s_out = remote(OUT, out_half, out_ref.at[:, mine], (t, mate))
    s_out.start()
    keep_out = pltpu.make_async_copy(out_half, out_ref.at[:, mine], copy_sem.at[8])
    keep_out.start()

    for copy in (s_pw1, s_in1, s_in1b, s_in2, s_in2m, s_gr1, s_pwr, s_grr):
        copy.wait_send()

    @pl.when(has_up)
    def _():
        send_meas.wait_send()

    @pl.when(has_up & fetches)
    def _():
        for copy in send_halo:
            copy.wait_send()

    @pl.when(has_down & fetches)
    def _():
        for copy in pass_halo:
            copy.wait_send()

    @pl.when(has_down)
    def _():
        for copy in (s_pwa, s_pwb, s_gra, s_grb):
            copy.wait_send()

    @pl.when(last)
    def _():
        for copy in (sx_in1, sx_in1b, sx_in2, sx_in2m, sx_pw1, sx_pwb, sx_gr1, sx_grb):
            copy.wait_send()

    keep_out.wait()
    s_out.wait()


def per_device(tiles, maps, measured, offsets, probe, spectrum, wave_index, edge_band, band_coef):
    _, length, columns = maps.shape
    slots = spectrum.shape[0]
    mid = length // 2
    vmem = lambda *shape: pltpu.VMEM(shape, F32)
    vmem16 = lambda *shape: pltpu.VMEM(shape, BF16)
    plane = (length, length)
    half = (mid, length)
    quarter = (mid // 2, length)
    halo = vmem(CHUNKS, 4, length // CHUNKS // 2, length)
    scratch = [
        vmem(4, *plane), vmem(2, *plane), vmem(slots, 2, *plane),
        vmem16(slots, 2 * length, 2 * length), vmem16(slots, 2 * length, 2 * length),
        vmem(slots, 2, *half),
        vmem(slots, *plane), vmem(slots, *plane), vmem16(slots, 2 * length, length),
        vmem16(slots, length, 2 * length),
        vmem(slots, *plane), vmem(slots, *plane),
        vmem(slots, *plane), vmem(slots, *plane), vmem(slots, *plane), vmem(slots, *plane),
        vmem16(slots, length, 2 * length),
        halo, halo, halo, halo, vmem(*plane), vmem(*plane), vmem(*plane), vmem(4, *half),
        vmem(*plane), vmem(*plane), vmem(*plane), vmem(*plane), vmem(*plane),
        vmem(*plane), vmem(*plane), vmem(*plane), vmem(*plane), vmem(*plane),
        vmem(5, *plane), vmem(5, *half), vmem(5, *plane), vmem(5, *half),
        vmem(5, *quarter), vmem(5, *quarter), vmem(5, *quarter), vmem(5, *quarter),
        vmem(5, *quarter), vmem(5, *quarter),
        pltpu.SMEM(offsets.shape, jnp.int32),
        pltpu.SMEM((slots,), F32),
        pltpu.SMEM((slots,), jnp.int32),
        pltpu.SMEM((4, slots), jnp.int32),
        pltpu.SMEM((3, 2, 4), F32),
        pltpu.SMEM((slots, 8), F32),
        pltpu.SemaphoreType.REGULAR,
        pltpu.SemaphoreType.DMA((9,)),
        pltpu.SemaphoreType.DMA((MESSAGES,)),
        pltpu.SemaphoreType.DMA((MESSAGES,)),
    ]
    hbm = pl.BlockSpec(memory_space=pl.ANY)
    return pl.pallas_call(
        functools.partial(kernel, tiles),
        out_shape=pltpu.VMEM(maps.shape, F32),
        in_specs=[hbm] * 8,
        out_specs=pl.BlockSpec(memory_space=pl.ANY),
        scratch_shapes=scratch,
        compiler_params=pltpu.CompilerParams(
            collective_id=0, has_side_effects=True, vmem_limit_bytes=56 << 20
        ),
    )(maps, measured, offsets, probe, spectrum, wave_index, edge_band.T, band_coef.transpose(1, 0, 2))


def solution(mesh):
    in_specs = (
        P(None, None, "tile"),
        P("tile", None, None),
        P("tile"),
        P("wave", None, None, None),
        P("wave"),
        P("wave"),
        P("wave", None),
        P(),
    )
    return jax.shard_map(
        functools.partial(per_device, mesh.shape["tile"]),
        mesh=mesh,
        in_specs=in_specs,
        out_specs=P(None, None, "tile"),
        check_vma=False,
    )
```

```python
import functools
import math

import jax
import jax.numpy as jnp
from jax import lax
from jax.experimental import pallas as pl
from jax.experimental.pallas import tpu as pltpu
from jax.sharding import PartitionSpec as P

WAVES = 48
RELAX = 4.0
FLOOR = 1.0
MESH = pl.DeviceIdType.MESH
F32 = jnp.float32
BF16 = jnp.bfloat16

SIN = (6.283184916495429, -41.341589232688364, 81.5999433297776, -76.61447253120122, 41.34288235437901, -12.471243534763557)
COS = (0.9999999890590201, -19.739204499453688, 64.93911745988827, -85.45013953077586, 60.16763095018129, -25.96759924584206, 6.528658157862129)

MEAS, PW1, PWR, PWA, PWB, IN1, IN1B, IN2, IN2M, GR1, GRR, GRA, GRB, OUT = range(14)
XIN1, XIN1B, XIN2, XIN2M, XPW1, XPWB, XGR1, XGRB = range(14, 22)
CHUNKS = 8
HALO, PASS = (22 + CHUNKS * k for k in range(2))
MESSAGES = 22 + CHUNKS * 2


def sincos_turns(turns):
    f = turns - jnp.round(turns)
    z = f * f
    s = jnp.full_like(z, SIN[-1])
    for k in SIN[-2::-1]:
        s = s * z + k
    c = jnp.full_like(z, COS[-1])
    for k in COS[-2::-1]:
        c = c * z + k
    return c, s * f


def swap(x):
    return pltpu.roll(x, 64, x.ndim - 1)


def kernel(
    tiles,
    maps_hbm, meas_hbm, off_hbm, probe_hbm, spec_hbm, wave_hbm, edge_hbm, band_hbm,
    out_ref,
    mp, ms, pb, w1, w2, obj, psir, psii, psib, midb, farr, fari, psirx, psiix, farrx, farix, nbuf,
    left_s, right_s, halo_r, none_r, ma_s, mb_r, none_m, out_half,
    inten, inten_r, pair_i, far_i, sf, intenx, intenx_r, pair_ix, far_ix, sfx,
    acc, acc_r, accx, accx_r,
    rpack, rrecv, lpack, la, lb, lpx,
    off_ref, spec_ref, wave_ref, edge_ref, band_ref, coef, enter, copy_sem, send_sem, recv_sem,
):
    slots = spec_ref.shape[0]
    length = mp.shape[1]
    mid = length // 2
    chunk = length // CHUNKS
    t = lax.axis_index("tile")
    w = lax.axis_index("wave")
    core = lax.rem(w, 2)
    mate = w + 1 - 2 * core
    far_z = lax.rem(w + 2, 4)
    far_mate = lax.rem(mate + 2, 4)
    up = lax.rem(t + 1, tiles)
    down = lax.rem(t + tiles - 1, tiles)
    first = t == 0
    last = t == tiles - 1
    has_down = t > 0
    has_up = t < tiles - 1
    mine = pl.ds(pl.multiple_of(core * mid, mid), mid)
    other = pl.ds(pl.multiple_of((1 - core) * mid, mid), mid)

    barrier = pltpu.get_barrier_semaphore()

    def greet(device):
        pl.semaphore_signal(barrier, inc=1, device_id=device, device_id_type=MESH)

    greet((t, mate))
    @pl.when(w < 2)
    def _():
        greet((t, far_z))
        greet((t, far_mate))

    @pl.when(has_down)
    def _():
        greet((down, w))

    greetings = 1 + 2 * (w // 2) + (2 * tiles - 2 - t) // tiles

    load_maps = pltpu.make_async_copy(maps_hbm, mp, copy_sem.at[0])
    load_meas = pltpu.make_async_copy(meas_hbm, ms, copy_sem.at[1])
    load_probe = pltpu.make_async_copy(probe_hbm, pb, copy_sem.at[2])
    load_maps.start()
    small = [
        pltpu.make_async_copy(source, target, copy_sem.at[3 + k])
        for k, (source, target) in enumerate((
            (off_hbm, off_ref), (spec_hbm, spec_ref), (wave_hbm, wave_ref),
            (edge_hbm, edge_ref), (band_hbm, band_ref),
        ))
    ]
    for copy in small:
        copy.start()
    load_meas.start()
    load_probe.start()

    def remote(k, src, dst, device):
        return pltpu.make_async_remote_copy(
            src_ref=src, dst_ref=dst, send_sem=send_sem.at[k], recv_sem=recv_sem.at[k],
            device_id=device, device_id_type=MESH,
        )

    def low_lanes(rows):
        return lax.broadcasted_iota(jnp.int32, (rows, length), 1) < mid

    def slot_coefficients(s, carry):
        for m in range(4):
            e = edge_ref[m, s]
            for k in range(2):
                c = [band_ref[n, k, m] for n in range(3)]
                coef[s, 4 * k + m] = jnp.where(e == 0, c[0], jnp.where(e == 1, c[1], c[2]))
        return carry

    for copy in small:
        copy.wait()
    lax.fori_loop(0, slots, slot_coefficients, 0)

    def groups(size, body, carry):
        def step(i, carry):
            return body([i * size + j for j in range(size)], carry)

        return lax.fori_loop(0, slots // size, step, carry)

    column = lax.broadcasted_iota(jnp.int32, (32, length), 1) - mid
    row = lax.broadcasted_iota(jnp.int32, (32, length), 0) - mid
    normaliser = 1.0 / math.sqrt(length)

    def table_slot(s, carry):
        which = jnp.full((32, length), wave_ref[s], jnp.int32).astype(F32)
        sampling = (0.6 + 0.4 * which / (WAVES - 1)) * (1.0 / length)
        c, sn = sincos_turns(sampling * (row * column).astype(F32))
        c, sn = c * normaliser, sn * normaliser
        step_c, step_s = sincos_turns(sampling[0:8] * (32 * column[0:8]).astype(F32))
        step_c, step_s = jnp.tile(step_c, (4, 1)), jnp.tile(step_s, (4, 1))
        for r in range(0, length, 32):
            if r:
                c, sn = c * step_c - sn * step_s, c * step_s + sn * step_c
            re = c.astype(BF16)
            im = (-sn).astype(BF16)
            nim = sn.astype(BF16)
            top, low = pl.ds(r, 32), pl.ds(length + r, 32)
            left, right = pl.ds(0, length), pl.ds(length, length)
            w1[s, top, left] = re
            w1[s, top, right] = nim
            w1[s, low, left] = im
            w1[s, low, right] = re
            w2[s, top, left] = re
            w2[s, top, right] = im
            w2[s, low, left] = nim
            w2[s, low, right] = re
        return carry

    load_maps.wait()
    hc = chunk // 2
    low_hc = low_lanes(hc)
    for q in range(CHUNKS):
        r = q * chunk
        for m in range(4):
            top, bottom = mp[m, r : r + hc], mp[m, r + hc : r + chunk]
            left_s[q, m] = jnp.where(low_hc, top, swap(bottom))
            right_s[q, m] = jnp.where(low_hc, swap(top), bottom)

    pl.semaphore_wait(barrier, greetings)

    @pl.when(w >= 2)
    def _():
        for device in ((t, far_z), (t, far_mate)):
            pl.semaphore_signal(enter, inc=1, device_id=device, device_id_type=MESH)


    def transmission(s, planes):
        a = [coef[s, m] for m in range(4)]
        b = [coef[s, 4 + m] for m in range(4)]
        absorb = a[0] * planes[0] + a[1] * planes[1] + a[2] * planes[2] + a[3] * planes[3]
        phase = b[0] * planes[0] + b[1] * planes[1] + b[2] * planes[2] + b[3] * planes[3]
        damping = jnp.exp(-absorb)
        c, sn = sincos_turns(phase * (0.5 / math.pi))
        return damping * c, damping * sn

    def half_object(packed):
        def body(group, carry):
            for q in range(CHUNKS):
                planes = [packed[q, m] for m in range(4)]
                for s in group:
                    re, im = transmission(s, planes)
                    obj[s, 0, pl.ds(q * hc, hc), :] = re
                    obj[s, 1, pl.ds(q * hc, hc), :] = im
            return carry

        groups(12, body, 0)

    def waves_at_object(q, packed, pr, pi, power, fresh_low=False):
        at = pl.ds(q * hc, hc)

        def body(group, totals):
            totals = list(totals)
            planes = [packed[q, m] for m in range(4)]
            for s in group:
                nre, nim = transmission(s, planes)
                ore, oim = obj[s, 0, at, :], obj[s, 1, at, :]
                if fresh_low:
                    nre, nim, ore, oim = ore, oim, nre, nim
                for half, (re, im) in enumerate((
                    (jnp.where(low_hc, ore, swap(nre)), jnp.where(low_hc, oim, swap(nim))),
                    (jnp.where(low_hc, swap(ore), nre), jnp.where(low_hc, swap(oim), nim)),
                )):
                    rows = pl.ds(q * chunk + half * hc, hc)
                    p_re, p_im = pb[s, 0, rows, :], pb[s, 1, rows, :]
                    x = p_re * re - p_im * im
                    y = p_re * im + p_im * re
                    pr[s, rows, :] = x
                    pi[s, rows, :] = y
                    psib[s, rows, :] = x.astype(BF16)
                    psib[s, pl.ds(length + q * chunk + half * hc, hc), :] = y.astype(BF16)
                    totals[half] = totals[half] + spec_ref[s] * (x * x + y * y)
            return tuple(totals)

        zero = jnp.zeros((hc, length), F32)
        for half, total in enumerate(groups(12, body, (zero, zero))):
            power[pl.ds(q * chunk + half * hc, hc), :] = total

    def row_half(rows_at):
        return (
            pl.ds(pl.multiple_of(rows_at, mid), mid),
            pl.ds(pl.multiple_of(rows_at + length, mid), mid),
        )

    def half_product(table, s, rows_at, data, into):
        rows, low_rows = row_half(rows_at)
        left = jnp.concatenate([table[s, rows, :], table[s, low_rows, :]], axis=0)
        m = jnp.dot(left, data, preferred_element_type=F32).astype(BF16)
        into[s, rows, 0:length] = m[:mid]
        into[s, rows, length : 2 * length] = m[mid:]

    def left_forward(rows_at):
        for s in range(slots):
            half_product(w1, s, rows_at, psib[s], midb)

    def right_forward(rows_at, fr, fi, total):
        rows = pl.ds(pl.multiple_of(rows_at, mid), mid)

        def body(group, light):
            for s in group:
                far = jnp.dot(midb[s, rows, :], w2[s], preferred_element_type=F32)
                x, y = far[:, :length], far[:, length:]
                fr[s, rows, :] = x
                fi[s, rows, :] = y
                light = light + spec_ref[s] * (x * x + y * y)
            return light

        total[rows, :] = groups(12, body, jnp.zeros((mid, length), F32))

    def back_left(rows_at, short, fr, fi):
        for s in range(slots):
            factor = spec_ref[s] * short[...]
            d = jnp.concatenate(
                [(factor * fr[s]).astype(BF16), (factor * fi[s]).astype(BF16)], axis=0
            )
            psib[s] = d
            half_product(w2, s, rows_at, d, nbuf)

    def back_left_again(rows_at):
        for s in range(slots):
            half_product(w2, s, rows_at, psib[s], nbuf)

    def back_right(rows_at, pr, pi, into):
        rows = pl.ds(pl.multiple_of(rows_at, mid), mid)
        for m in range(4):
            into[m, rows, :] = jnp.zeros((mid, length), F32)

        def body(group, carry):
            back = [jnp.dot(nbuf[s, rows, :], w1[s], preferred_element_type=F32) for s in group]
            for r in range(0, mid, 16):
                part = pl.ds(pl.multiple_of(rows_at + r, 16), 16)
                sums = [into[m, part, :] for m in range(4)]
                for s, both in zip(group, back):
                    br, bi = both[r : r + 16, :length], both[r : r + 16, length:]
                    x, y = pr[s, part, :], pi[s, part, :]
                    cr = x * br + y * bi
                    ci = x * bi - y * br
                    for m in range(4):
                        sums[m] = sums[m] + (coef[s, 4 + m] * ci - coef[s, m] * cr)
                for m in range(4):
                    into[m, part, :] = sums[m]
            return carry

        groups(12, body, 0)

    at_mine, at_other = core * mid, (1 - core) * mid
    frames_here = jnp.where(first, 1.0, 2.0)
    quarter = mid // 2

    def pack_right(y):
        return jnp.where(low_lanes(quarter), swap(y[:quarter]), y[quarter:])

    def pack_left(y):
        return jnp.where(low_lanes(quarter), y[:quarter], swap(y[quarter:]))

    four = pl.ds(0, 4)
    sx_in1 = remote(XIN1, intenx.at[other], intenx_r.at[other], (t, mate))
    sx_in1b = remote(XIN1B, intenx.at[mine], intenx_r.at[mine], (t, mate))
    sx_in2 = remote(XIN2, pair_ix.at[mine], far_ix.at[mine], (t, far_z))
    sx_in2m = remote(XIN2M, pair_ix.at[mine], far_ix.at[mine], (t, far_mate))
    sx_pw1 = remote(XPW1, accx.at[4, other], accx_r.at[4], (t, mate))
    sx_pwb = remote(XPWB, lpx.at[4], lb.at[4], (t, far_z))
    sx_gr1 = remote(XGR1, accx.at[four, other], accx_r.at[four], (t, mate))
    sx_grb = remote(XGRB, lpx.at[four], lb.at[four], (t, far_z))

    def light_of_both(partial, received, pair, first_half, second_half, far_one, far_two):
        second_half.start()
        first_half.wait_recv()
        pair[mine, :] = partial[mine, :] + received[mine, :]
        far_one.start()
        far_two.start()

    def factors(partial, received, pair, far, one, two, frames, into):
        pair[other, :] = partial[other, :] + received[other, :]
        for r in range(0, length, 32):
            rows = pl.ds(r, 32)
            inv = 1.0 / jnp.maximum(pair[rows, :] + far[rows, :], FLOOR)
            into[rows, :] = jnp.sqrt(one[rows, :] * inv) + jnp.sqrt(two[rows, :] * inv) - frames

    def extra_forward():
        sx_pw1.start()
        left_forward(at_other)
        right_forward(at_other, farrx, farix, intenx)
        sx_in1.start()
        left_forward(at_mine)
        right_forward(at_mine, farrx, farix, intenx)
        light_of_both(intenx, intenx_r, pair_ix, sx_in1, sx_in1b, sx_in2, sx_in2m)
        sx_pw1.wait_recv()
        lpx[4] = pack_left(accx[4, mine, :] + accx_r[4])
        sx_pwb.start()

    def extra_shortfall():
        sx_in1b.wait_recv()
        sx_in2.wait_recv()
        sx_in2m.wait_recv()
        factors(intenx, intenx_r, pair_ix, far_ix, ms.at[1], none_m, 1.0, sfx)

    def extra_backward():
        back_left(at_other, sfx, farrx, farix)
        back_right(at_other, psirx, psiix, accx)
        sx_gr1.start()
        back_left_again(at_mine)
        back_right(at_mine, psirx, psiix, accx)
        sx_gr1.wait_recv()
        for m in range(4):
            lpx[m] = pack_left(accx[m, mine, :] + accx_r[m])
        sx_grb.start()

    @pl.when(first)
    def _():
        halo_r[...] = jnp.zeros_like(halo_r)
        mb_r[...] = jnp.zeros_like(mb_r)

    @pl.when(last)
    def _():
        none_r[...] = jnp.zeros_like(none_r)
        none_m[...] = jnp.zeros_like(none_m)

    fetches = core == 1
    send_halo = [remote(HALO + q, right_s.at[q], halo_r.at[q], (up, w)) for q in range(CHUNKS)]
    pass_halo = [remote(PASS + q, halo_r.at[q], halo_r.at[q], (t, mate)) for q in range(CHUNKS)]
    send_meas = remote(MEAS, ms.at[1], mb_r, (up, w))

    @pl.when(fetches & has_up)
    def _():
        for copy in send_halo:
            copy.start()

    load_meas.wait()
    low_first = off_ref[0] < off_ref[1]
    for r in range(0, length, 32):
        rows = pl.ds(r, 32)
        one, two = ms[0, rows, :], ms[1, rows, :]
        ma_s[rows, :] = jnp.where(low_first, one, two)
        ms[1, rows, :] = jnp.where(low_first, two, one)

    groups(4, lambda group, carry: [table_slot(s, carry) for s in group][0], 0)

    half_object(left_s)

    load_probe.wait()

    def arrived(q):
        @pl.when(has_down & fetches)
        def _():
            send_halo[q].wait_recv()
            pass_halo[q].start()

    arrived(0)
    for q in range(CHUNKS):
        if q + 1 < CHUNKS:
            arrived(q + 1)

        @pl.when(has_down & jnp.logical_not(fetches))
        def _():
            pass_halo[q].wait_recv()

        waves_at_object(q, halo_r, psir, psii, acc.at[4], fresh_low=True)

        if q == 1:

            @pl.when(has_up)
            def _():
                send_meas.start()

    s_pw1 = remote(PW1, acc.at[4, other], acc_r.at[4], (t, mate))
    s_in1 = remote(IN1, inten.at[other], inten_r.at[other], (t, mate))
    s_in1b = remote(IN1B, inten.at[mine], inten_r.at[mine], (t, mate))
    s_in2 = remote(IN2, pair_i.at[mine], far_i.at[mine], (t, far_z))
    s_in2m = remote(IN2M, pair_i.at[mine], far_i.at[mine], (t, far_mate))
    s_gr1 = remote(GR1, acc.at[four, other], acc_r.at[four], (t, mate))
    s_pwr = remote(PWR, rpack.at[4], rrecv.at[4], (t, far_z))
    s_pwa = remote(PWA, lpack.at[4], la.at[4], (down, w))
    s_pwb = remote(PWB, lpack.at[4], lb.at[4], (down, far_z))
    s_grr = remote(GRR, rpack.at[four], rrecv.at[four], (t, far_z))
    s_gra = remote(GRA, lpack.at[four], la.at[four], (down, w))
    s_grb = remote(GRB, lpack.at[four], lb.at[four], (down, far_z))

    s_pw1.start()
    left_forward(at_other)
    right_forward(at_other, farr, fari, inten)
    s_in1.start()
    left_forward(at_mine)
    right_forward(at_mine, farr, fari, inten)

    @pl.when(w < 2)
    def _():
        pl.semaphore_wait(enter, 2)

    light_of_both(inten, inten_r, pair_i, s_in1, s_in1b, s_in2, s_in2m)

    s_pw1.wait_recv()
    power = frames_here * (acc[4, mine, :] + acc_r[4])
    lpack[4] = pack_left(power)
    rpack[4] = pack_right(power)

    @pl.when(last)
    def _():
        half_object(right_s)
        for q in range(CHUNKS):
            waves_at_object(q, none_r, psirx, psiix, accx.at[4])
        extra_forward()

    @pl.when(has_down)
    def _():
        send_meas.wait_recv()

    s_in1b.wait_recv()
    s_in2.wait_recv()
    s_in2m.wait_recv()
    factors(inten, inten_r, pair_i, far_i, ma_s, mb_r, frames_here, sf)
    s_pwr.start()


    @pl.when(has_down)
    def _():
        s_pwa.start()
        s_pwb.start()

    back_left(at_other, sf, farr, fari)
    back_right(at_other, psir, psii, acc)
    s_gr1.start()
    back_left_again(at_mine)
    back_right(at_mine, psir, psii, acc)
    s_gr1.wait_recv()
    for m in range(4):
        y = acc[m, mine, :] + acc_r[m]
        lpack[m] = pack_left(y)
        rpack[m] = pack_right(y)

    near = w < 2

    @pl.when(has_down & near)
    def _():
        s_gra.start()

    @pl.when(has_down)
    def _():
        s_grb.start()

    s_grr.start()

    @pl.when(has_down & jnp.logical_not(near))
    def _():
        s_gra.start()

    @pl.when(last)
    def _():
        extra_shortfall()
        extra_backward()
        sx_pwb.wait_recv()
        sx_grb.wait_recv()
        la[...] = lpx[...]

    @pl.when(has_up)
    def _():
        s_pwa.wait_recv()
        s_pwb.wait_recv()
        s_gra.wait_recv()
        s_grb.wait_recv()

    s_pwr.wait_recv()
    s_grr.wait_recv()

    def totals(m):
        l = la[m] + lb[m]
        r = rpack[m] + rrecv[m]
        return jnp.where(low_lanes(quarter), r, swap(l)), jnp.where(low_lanes(quarter), swap(r), l)

    powers = [RELAX / (p + 1.0) for p in totals(4)]
    for m in range(4):
        for q, total in enumerate(totals(m)):
            rows = pl.ds(pl.multiple_of(at_mine + q * quarter, quarter), quarter)
            out_half[m, q * quarter : (q + 1) * quarter, :] = mp[m, rows, :] + total * powers[q]
    s_out = remote(OUT, out_half, out_ref.at[:, mine], (t, mate))
    s_out.start()
    keep_out = pltpu.make_async_copy(out_half, out_ref.at[:, mine], copy_sem.at[8])
    keep_out.start()

    for copy in (s_pw1, s_in1, s_in1b, s_in2, s_in2m, s_gr1, s_pwr, s_grr):
        copy.wait_send()

    @pl.when(has_up)
    def _():
        send_meas.wait_send()

    @pl.when(has_up & fetches)
    def _():
        for copy in send_halo:
            copy.wait_send()

    @pl.when(has_down & fetches)
    def _():
        for copy in pass_halo:
            copy.wait_send()

    @pl.when(has_down)
    def _():
        for copy in (s_pwa, s_pwb, s_gra, s_grb):
            copy.wait_send()

    @pl.when(last)
    def _():
        for copy in (sx_in1, sx_in1b, sx_in2, sx_in2m, sx_pw1, sx_pwb, sx_gr1, sx_grb):
            copy.wait_send()

    keep_out.wait()
    s_out.wait()


def per_device(tiles, maps, measured, offsets, probe, spectrum, wave_index, edge_band, band_coef):
    _, length, columns = maps.shape
    slots = spectrum.shape[0]
    mid = length // 2
    vmem = lambda *shape: pltpu.VMEM(shape, F32)
    vmem16 = lambda *shape: pltpu.VMEM(shape, BF16)
    plane = (length, length)
    half = (mid, length)
    quarter = (mid // 2, length)
    halo = vmem(CHUNKS, 4, length // CHUNKS // 2, length)
    scratch = [
        vmem(4, *plane), vmem(2, *plane), vmem(slots, 2, *plane),
        vmem16(slots, 2 * length, 2 * length), vmem16(slots, 2 * length, 2 * length),
        vmem(slots, 2, *half),
        vmem(slots, *plane), vmem(slots, *plane), vmem16(slots, 2 * length, length),
        vmem16(slots, length, 2 * length),
        vmem(slots, *plane), vmem(slots, *plane),
        vmem(slots, *plane), vmem(slots, *plane), vmem(slots, *plane), vmem(slots, *plane),
        vmem16(slots, length, 2 * length),
        halo, halo, halo, halo, vmem(*plane), vmem(*plane), vmem(*plane), vmem(4, *half),
        vmem(*plane), vmem(*plane), vmem(*plane), vmem(*plane), vmem(*plane),
        vmem(*plane), vmem(*plane), vmem(*plane), vmem(*plane), vmem(*plane),
        vmem(5, *plane), vmem(5, *half), vmem(5, *plane), vmem(5, *half),
        vmem(5, *quarter), vmem(5, *quarter), vmem(5, *quarter), vmem(5, *quarter),
        vmem(5, *quarter), vmem(5, *quarter),
        pltpu.SMEM(offsets.shape, jnp.int32),
        pltpu.SMEM((slots,), F32),
        pltpu.SMEM((slots,), jnp.int32),
        pltpu.SMEM((4, slots), jnp.int32),
        pltpu.SMEM((3, 2, 4), F32),
        pltpu.SMEM((slots, 8), F32),
        pltpu.SemaphoreType.REGULAR,
        pltpu.SemaphoreType.DMA((9,)),
        pltpu.SemaphoreType.DMA((MESSAGES,)),
        pltpu.SemaphoreType.DMA((MESSAGES,)),
    ]
    hbm = pl.BlockSpec(memory_space=pl.ANY)
    return pl.pallas_call(
        functools.partial(kernel, tiles),
        out_shape=pltpu.VMEM(maps.shape, F32),
        in_specs=[hbm] * 8,
        out_specs=pl.BlockSpec(memory_space=pl.ANY),
        scratch_shapes=scratch,
        compiler_params=pltpu.CompilerParams(
            collective_id=0, has_side_effects=True, vmem_limit_bytes=56 << 20
        ),
    )(maps, measured, offsets, probe, spectrum, wave_index, edge_band.T, band_coef.transpose(1, 0, 2))


def solution(mesh):
    in_specs = (
        P(None, None, "tile"),
        P("tile", None, None),
        P("tile"),
        P("wave", None, None, None),
        P("wave"),
        P("wave"),
        P("wave", None),
        P(),
    )
    return jax.shard_map(
        functools.partial(per_device, mesh.shape["tile"]),
        mesh=mesh,
        in_specs=in_specs,
        out_specs=P(None, None, "tile"),
        check_vma=False,
    )
```

```python
import functools
import math

import jax
import jax.numpy as jnp
from jax import lax
from jax.experimental import pallas as pl
from jax.experimental.pallas import tpu as pltpu
from jax.sharding import PartitionSpec as P

WAVES = 48
RELAX = 4.0
FLOOR = 1.0
MESH = pl.DeviceIdType.MESH
F32 = jnp.float32
BF16 = jnp.bfloat16

SIN = (6.283184916495429, -41.341589232688364, 81.5999433297776, -76.61447253120122, 41.34288235437901, -12.471243534763557)
COS = (0.9999999890590201, -19.739204499453688, 64.93911745988827, -85.45013953077586, 60.16763095018129, -25.96759924584206, 6.528658157862129)

MEAS, PW1, PWR, PWA, PWB, IN1, IN1B, IN2, IN2M, GR1, GRR, GRA, GRB, OUT = range(14)
XIN1, XIN1B, XIN2, XIN2M, XPW1, XPWB, XGR1, XGRB = range(14, 22)
CHUNKS = 8
HALO, PASS = (22 + CHUNKS * k for k in range(2))
MESSAGES = 22 + CHUNKS * 2


def sincos_turns(turns):
    f = turns - jnp.round(turns)
    z = f * f
    s = jnp.full_like(z, SIN[-1])
    for k in SIN[-2::-1]:
        s = s * z + k
    c = jnp.full_like(z, COS[-1])
    for k in COS[-2::-1]:
        c = c * z + k
    return c, s * f


def swap(x):
    return pltpu.roll(x, 64, x.ndim - 1)


def kernel(
    tiles,
    maps_hbm, meas_hbm, off_hbm, probe_hbm, spec_hbm, wave_hbm, edge_hbm, band_hbm,
    out_ref,
    mp, ms, pb, w1, w2, obj, psir, psii, psib, midb, farr, fari, psirx, psiix, farrx, farix, nbuf,
    left_s, right_s, halo_r, none_r, ma_s, mb_r, none_m, out_half,
    inten, inten_r, pair_i, far_i, sf, intenx, intenx_r, pair_ix, far_ix, sfx,
    acc, acc_r, accx, accx_r,
    rpack, rrecv, lpack, la, lb, lpx,
    off_ref, spec_ref, wave_ref, edge_ref, band_ref, coef, enter, copy_sem, send_sem, recv_sem,
):
    slots = spec_ref.shape[0]
    length = mp.shape[1]
    mid = length // 2
    chunk = length // CHUNKS
    t = lax.axis_index("tile")
    w = lax.axis_index("wave")
    core = lax.rem(w, 2)
    mate = w + 1 - 2 * core
    far_z = lax.rem(w + 2, 4)
    far_mate = lax.rem(mate + 2, 4)
    up = lax.rem(t + 1, tiles)
    down = lax.rem(t + tiles - 1, tiles)
    first = t == 0
    last = t == tiles - 1
    has_down = t > 0
    has_up = t < tiles - 1
    mine = pl.ds(pl.multiple_of(core * mid, mid), mid)
    other = pl.ds(pl.multiple_of((1 - core) * mid, mid), mid)

    barrier = pltpu.get_barrier_semaphore()

    def greet(device):
        pl.semaphore_signal(barrier, inc=1, device_id=device, device_id_type=MESH)

    greet((t, mate))
    @pl.when(w < 2)
    def _():
        greet((t, far_z))
        greet((t, far_mate))

    @pl.when(has_down)
    def _():
        greet((down, w))

    greetings = 1 + 2 * (w // 2) + (2 * tiles - 2 - t) // tiles

    load_maps = pltpu.make_async_copy(maps_hbm, mp, copy_sem.at[0])
    load_meas = pltpu.make_async_copy(meas_hbm, ms, copy_sem.at[1])
    load_probe = pltpu.make_async_copy(probe_hbm, pb, copy_sem.at[2])
    load_maps.start()
    small = [
        pltpu.make_async_copy(source, target, copy_sem.at[3 + k])
        for k, (source, target) in enumerate((
            (off_hbm, off_ref), (spec_hbm, spec_ref), (wave_hbm, wave_ref),
            (edge_hbm, edge_ref), (band_hbm, band_ref),
        ))
    ]
    for copy in small:
        copy.start()
    load_meas.start()
    load_probe.start()

    def remote(k, src, dst, device):
        return pltpu.make_async_remote_copy(
            src_ref=src, dst_ref=dst, send_sem=send_sem.at[k], recv_sem=recv_sem.at[k],
            device_id=device, device_id_type=MESH,
        )

    def low_lanes(rows):
        return lax.broadcasted_iota(jnp.int32, (rows, length), 1) < mid

    def slot_coefficients(s, carry):
        for m in range(4):
            e = edge_ref[m, s]
            for k in range(2):
                c = [band_ref[n, k, m] for n in range(3)]
                coef[s, 4 * k + m] = jnp.where(e == 0, c[0], jnp.where(e == 1, c[1], c[2]))
        return carry


    def groups(size, body, carry):
        def step(i, carry):
            return body([i * size + j for j in range(size)], carry)

        return lax.fori_loop(0, slots // size, step, carry)

    column = lax.broadcasted_iota(jnp.int32, (32, length), 1) - mid
    row = lax.broadcasted_iota(jnp.int32, (32, length), 0) - mid
    normaliser = 1.0 / math.sqrt(length)

    def table_slot(s, carry):
        which = jnp.full((32, length), wave_ref[s], jnp.int32).astype(F32)
        sampling = (0.6 + 0.4 * which / (WAVES - 1)) * (1.0 / length)
        c, sn = sincos_turns(sampling * (row * column).astype(F32))
        c, sn = c * normaliser, sn * normaliser
        step_c, step_s = sincos_turns(sampling[0:8] * (32 * column[0:8]).astype(F32))
        step_c, step_s = jnp.tile(step_c, (4, 1)), jnp.tile(step_s, (4, 1))
        for r in range(0, length, 32):
            if r:
                c, sn = c * step_c - sn * step_s, c * step_s + sn * step_c
            re = c.astype(BF16)
            im = (-sn).astype(BF16)
            nim = sn.astype(BF16)
            top, low = pl.ds(r, 32), pl.ds(length + r, 32)
            left, right = pl.ds(0, length), pl.ds(length, length)
            w1[s, top, left] = re
            w1[s, top, right] = nim
            w1[s, low, left] = im
            w1[s, low, right] = re
            w2[s, top, left] = re
            w2[s, top, right] = im
            w2[s, low, left] = nim
            w2[s, low, right] = re
        return carry

    load_maps.wait()
    hc = chunk // 2
    low_hc = low_lanes(hc)
    for q in range(CHUNKS):
        r = q * chunk
        for m in range(4):
            top, bottom = mp[m, r : r + hc], mp[m, r + hc : r + chunk]
            left_s[q, m] = jnp.where(low_hc, top, swap(bottom))
            right_s[q, m] = jnp.where(low_hc, swap(top), bottom)

    pl.semaphore_wait(barrier, greetings)

    @pl.when(w >= 2)
    def _():
        for device in ((t, far_z), (t, far_mate)):
            pl.semaphore_signal(enter, inc=1, device_id=device, device_id_type=MESH)


    def transmission(s, planes):
        a = [coef[s, m] for m in range(4)]
        b = [coef[s, 4 + m] for m in range(4)]
        absorb = a[0] * planes[0] + a[1] * planes[1] + a[2] * planes[2] + a[3] * planes[3]
        phase = b[0] * planes[0] + b[1] * planes[1] + b[2] * planes[2] + b[3] * planes[3]
        damping = jnp.exp(-absorb)
        c, sn = sincos_turns(phase * (0.5 / math.pi))
        return damping * c, damping * sn

    def half_object(packed):
        def body(group, carry):
            for q in range(CHUNKS):
                planes = [packed[q, m] for m in range(4)]
                for s in group:
                    re, im = transmission(s, planes)
                    obj[s, 0, pl.ds(q * hc, hc), :] = re
                    obj[s, 1, pl.ds(q * hc, hc), :] = im
            return carry

        groups(12, body, 0)

    def waves_at_object(q, packed, pr, pi, power, fresh_low=False):
        at = pl.ds(q * hc, hc)

        def body(group, totals):
            totals = list(totals)
            planes = [packed[q, m] for m in range(4)]
            for s in group:
                nre, nim = transmission(s, planes)
                ore, oim = obj[s, 0, at, :], obj[s, 1, at, :]
                if fresh_low:
                    nre, nim, ore, oim = ore, oim, nre, nim
                for half, (re, im) in enumerate((
                    (jnp.where(low_hc, ore, swap(nre)), jnp.where(low_hc, oim, swap(nim))),
                    (jnp.where(low_hc, swap(ore), nre), jnp.where(low_hc, swap(oim), nim)),
                )):
                    rows = pl.ds(q * chunk + half * hc, hc)
                    p_re, p_im = pb[s, 0, rows, :], pb[s, 1, rows, :]
                    x = p_re * re - p_im * im
                    y = p_re * im + p_im * re
                    pr[s, rows, :] = x
                    pi[s, rows, :] = y
                    psib[s, rows, :] = x.astype(BF16)
                    psib[s, pl.ds(length + q * chunk + half * hc, hc), :] = y.astype(BF16)
                    totals[half] = totals[half] + spec_ref[s] * (x * x + y * y)
            return tuple(totals)

        zero = jnp.zeros((hc, length), F32)
        for half, total in enumerate(groups(12, body, (zero, zero))):
            power[pl.ds(q * chunk + half * hc, hc), :] = total

    def row_half(rows_at):
        return (
            pl.ds(pl.multiple_of(rows_at, mid), mid),
            pl.ds(pl.multiple_of(rows_at + length, mid), mid),
        )

    def half_product(table, s, rows_at, data, into):
        rows, low_rows = row_half(rows_at)
        left = jnp.concatenate([table[s, rows, :], table[s, low_rows, :]], axis=0)
        m = jnp.dot(left, data, preferred_element_type=F32).astype(BF16)
        into[s, rows, 0:length] = m[:mid]
        into[s, rows, length : 2 * length] = m[mid:]

    def left_forward(rows_at):
        for s in range(slots):
            half_product(w1, s, rows_at, psib[s], midb)

    def right_forward(rows_at, fr, fi, total):
        rows = pl.ds(pl.multiple_of(rows_at, mid), mid)

        def body(group, light):
            for s in group:
                far = jnp.dot(midb[s, rows, :], w2[s], preferred_element_type=F32)
                x, y = far[:, :length], far[:, length:]
                fr[s, rows, :] = x
                fi[s, rows, :] = y
                light = light + spec_ref[s] * (x * x + y * y)
            return light

        total[rows, :] = groups(12, body, jnp.zeros((mid, length), F32))

    def back_left(rows_at, short, fr, fi):
        for s in range(slots):
            factor = spec_ref[s] * short[...]
            d = jnp.concatenate(
                [(factor * fr[s]).astype(BF16), (factor * fi[s]).astype(BF16)], axis=0
            )
            psib[s] = d
            half_product(w2, s, rows_at, d, nbuf)

    def back_left_again(rows_at):
        for s in range(slots):
            half_product(w2, s, rows_at, psib[s], nbuf)

    def back_right(rows_at, pr, pi, into):
        rows = pl.ds(pl.multiple_of(rows_at, mid), mid)
        for m in range(4):
            into[m, rows, :] = jnp.zeros((mid, length), F32)

        def body(group, carry):
            back = [jnp.dot(nbuf[s, rows, :], w1[s], preferred_element_type=F32) for s in group]
            for r in range(0, mid, 16):
                part = pl.ds(pl.multiple_of(rows_at + r, 16), 16)
                sums = [into[m, part, :] for m in range(4)]
                for s, both in zip(group, back):
                    br, bi = both[r : r + 16, :length], both[r : r + 16, length:]
                    x, y = pr[s, part, :], pi[s, part, :]
                    cr = x * br + y * bi
                    ci = x * bi - y * br
                    for m in range(4):
                        sums[m] = sums[m] + (coef[s, 4 + m] * ci - coef[s, m] * cr)
                for m in range(4):
                    into[m, part, :] = sums[m]
            return carry

        groups(12, body, 0)

    at_mine, at_other = core * mid, (1 - core) * mid
    frames_here = jnp.where(first, 1.0, 2.0)
    quarter = mid // 2

    def pack_right(y):
        return jnp.where(low_lanes(quarter), swap(y[:quarter]), y[quarter:])

    def pack_left(y):
        return jnp.where(low_lanes(quarter), y[:quarter], swap(y[quarter:]))

    four = pl.ds(0, 4)
    sx_in1 = remote(XIN1, intenx.at[other], intenx_r.at[other], (t, mate))
    sx_in1b = remote(XIN1B, intenx.at[mine], intenx_r.at[mine], (t, mate))
    sx_in2 = remote(XIN2, pair_ix.at[mine], far_ix.at[mine], (t, far_z))
    sx_in2m = remote(XIN2M, pair_ix.at[mine], far_ix.at[mine], (t, far_mate))
    sx_pw1 = remote(XPW1, accx.at[4, other], accx_r.at[4], (t, mate))
    sx_pwb = remote(XPWB, lpx.at[4], lb.at[4], (t, far_z))
    sx_gr1 = remote(XGR1, accx.at[four, other], accx_r.at[four], (t, mate))
    sx_grb = remote(XGRB, lpx.at[four], lb.at[four], (t, far_z))

    def light_of_both(partial, received, pair, first_half, second_half, far_one, far_two):
        second_half.start()
        first_half.wait_recv()
        pair[mine, :] = partial[mine, :] + received[mine, :]
        far_one.start()
        far_two.start()

    def factors(partial, received, pair, far, one, two, frames, into):
        pair[other, :] = partial[other, :] + received[other, :]
        for r in range(0, length, 32):
            rows = pl.ds(r, 32)
            inv = 1.0 / jnp.maximum(pair[rows, :] + far[rows, :], FLOOR)
            into[rows, :] = jnp.sqrt(one[rows, :] * inv) + jnp.sqrt(two[rows, :] * inv) - frames

    def extra_forward():
        sx_pw1.start()
        left_forward(at_other)
        right_forward(at_other, farrx, farix, intenx)
        sx_in1.start()
        left_forward(at_mine)
        right_forward(at_mine, farrx, farix, intenx)
        light_of_both(intenx, intenx_r, pair_ix, sx_in1, sx_in1b, sx_in2, sx_in2m)
        sx_pw1.wait_recv()
        lpx[4] = pack_left(accx[4, mine, :] + accx_r[4])
        sx_pwb.start()

    def extra_shortfall():
        sx_in1b.wait_recv()
        sx_in2.wait_recv()
        sx_in2m.wait_recv()
        factors(intenx, intenx_r, pair_ix, far_ix, ms.at[1], none_m, 1.0, sfx)

    def extra_backward():
        back_left(at_other, sfx, farrx, farix)
        back_right(at_other, psirx, psiix, accx)
        sx_gr1.start()
        back_left_again(at_mine)
        back_right(at_mine, psirx, psiix, accx)
        sx_gr1.wait_recv()
        for m in range(4):
            lpx[m] = pack_left(accx[m, mine, :] + accx_r[m])
        sx_grb.start()

    @pl.when(first)
    def _():
        halo_r[...] = jnp.zeros_like(halo_r)
        mb_r[...] = jnp.zeros_like(mb_r)

    @pl.when(last)
    def _():
        none_r[...] = jnp.zeros_like(none_r)
        none_m[...] = jnp.zeros_like(none_m)

    fetches = core == 1
    send_halo = [remote(HALO + q, right_s.at[q], halo_r.at[q], (up, w)) for q in range(CHUNKS)]
    pass_halo = [remote(PASS + q, halo_r.at[q], halo_r.at[q], (t, mate)) for q in range(CHUNKS)]
    send_meas = remote(MEAS, ms.at[1], mb_r, (up, w))

    @pl.when(fetches & has_up)
    def _():
        for copy in send_halo:
            copy.start()

    for copy in small:
        copy.wait()
    lax.fori_loop(0, slots, slot_coefficients, 0)
    load_meas.wait()
    low_first = off_ref[0] < off_ref[1]
    for r in range(0, length, 32):
        rows = pl.ds(r, 32)
        one, two = ms[0, rows, :], ms[1, rows, :]
        ma_s[rows, :] = jnp.where(low_first, one, two)
        ms[1, rows, :] = jnp.where(low_first, two, one)

    groups(4, lambda group, carry: [table_slot(s, carry) for s in group][0], 0)

    half_object(left_s)

    load_probe.wait()

    def arrived(q):
        @pl.when(has_down & fetches)
        def _():
            send_halo[q].wait_recv()
            pass_halo[q].start()

    arrived(0)
    for q in range(CHUNKS):
        if q + 1 < CHUNKS:
            arrived(q + 1)

        @pl.when(has_down & jnp.logical_not(fetches))
        def _():
            pass_halo[q].wait_recv()

        waves_at_object(q, halo_r, psir, psii, acc.at[4], fresh_low=True)

        if q == 1:

            @pl.when(has_up)
            def _():
                send_meas.start()

    s_pw1 = remote(PW1, acc.at[4, other], acc_r.at[4], (t, mate))
    s_in1 = remote(IN1, inten.at[other], inten_r.at[other], (t, mate))
    s_in1b = remote(IN1B, inten.at[mine], inten_r.at[mine], (t, mate))
    s_in2 = remote(IN2, pair_i.at[mine], far_i.at[mine], (t, far_z))
    s_in2m = remote(IN2M, pair_i.at[mine], far_i.at[mine], (t, far_mate))
    s_gr1 = remote(GR1, acc.at[four, other], acc_r.at[four], (t, mate))
    s_pwr = remote(PWR, rpack.at[4], rrecv.at[4], (t, far_z))
    s_pwa = remote(PWA, lpack.at[4], la.at[4], (down, w))
    s_pwb = remote(PWB, lpack.at[4], lb.at[4], (down, far_z))
    s_grr = remote(GRR, rpack.at[four], rrecv.at[four], (t, far_z))
    s_gra = remote(GRA, lpack.at[four], la.at[four], (down, w))
    s_grb = remote(GRB, lpack.at[four], lb.at[four], (down, far_z))

    s_pw1.start()
    left_forward(at_other)
    right_forward(at_other, farr, fari, inten)
    s_in1.start()
    left_forward(at_mine)
    right_forward(at_mine, farr, fari, inten)

    @pl.when(w < 2)
    def _():
        pl.semaphore_wait(enter, 2)

    light_of_both(inten, inten_r, pair_i, s_in1, s_in1b, s_in2, s_in2m)

    s_pw1.wait_recv()
    power = frames_here * (acc[4, mine, :] + acc_r[4])
    lpack[4] = pack_left(power)
    rpack[4] = pack_right(power)

    @pl.when(last)
    def _():
        half_object(right_s)
        for q in range(CHUNKS):
            waves_at_object(q, none_r, psirx, psiix, accx.at[4])
        extra_forward()

    @pl.when(has_down)
    def _():
        send_meas.wait_recv()

    s_in1b.wait_recv()
    s_in2.wait_recv()
    s_in2m.wait_recv()
    factors(inten, inten_r, pair_i, far_i, ma_s, mb_r, frames_here, sf)
    s_pwr.start()


    @pl.when(has_down)
    def _():
        s_pwa.start()
        s_pwb.start()

    back_left(at_other, sf, farr, fari)
    back_right(at_other, psir, psii, acc)
    s_gr1.start()
    back_left_again(at_mine)
    back_right(at_mine, psir, psii, acc)
    s_gr1.wait_recv()
    for m in range(4):
        y = acc[m, mine, :] + acc_r[m]
        lpack[m] = pack_left(y)
        rpack[m] = pack_right(y)

    near = w < 2

    @pl.when(has_down & near)
    def _():
        s_gra.start()

    @pl.when(has_down)
    def _():
        s_grb.start()

    s_grr.start()

    @pl.when(has_down & jnp.logical_not(near))
    def _():
        s_gra.start()

    @pl.when(last)
    def _():
        extra_shortfall()
        extra_backward()
        sx_pwb.wait_recv()
        sx_grb.wait_recv()
        la[...] = lpx[...]

    @pl.when(has_up)
    def _():
        s_pwa.wait_recv()
        s_pwb.wait_recv()
        s_gra.wait_recv()
        s_grb.wait_recv()

    s_pwr.wait_recv()
    s_grr.wait_recv()

    def totals(m):
        l = la[m] + lb[m]
        r = rpack[m] + rrecv[m]
        return jnp.where(low_lanes(quarter), r, swap(l)), jnp.where(low_lanes(quarter), swap(r), l)

    powers = [RELAX / (p + 1.0) for p in totals(4)]
    for m in range(4):
        for q, total in enumerate(totals(m)):
            rows = pl.ds(pl.multiple_of(at_mine + q * quarter, quarter), quarter)
            out_half[m, q * quarter : (q + 1) * quarter, :] = mp[m, rows, :] + total * powers[q]
    s_out = remote(OUT, out_half, out_ref.at[:, mine], (t, mate))
    s_out.start()
    keep_out = pltpu.make_async_copy(out_half, out_ref.at[:, mine], copy_sem.at[8])
    keep_out.start()

    for copy in (s_pw1, s_in1, s_in1b, s_in2, s_in2m, s_gr1, s_pwr, s_grr):
        copy.wait_send()

    @pl.when(has_up)
    def _():
        send_meas.wait_send()

    @pl.when(has_up & fetches)
    def _():
        for copy in send_halo:
            copy.wait_send()

    @pl.when(has_down & fetches)
    def _():
        for copy in pass_halo:
            copy.wait_send()

    @pl.when(has_down)
    def _():
        for copy in (s_pwa, s_pwb, s_gra, s_grb):
            copy.wait_send()

    @pl.when(last)
    def _():
        for copy in (sx_in1, sx_in1b, sx_in2, sx_in2m, sx_pw1, sx_pwb, sx_gr1, sx_grb):
            copy.wait_send()

    keep_out.wait()
    s_out.wait()


def per_device(tiles, maps, measured, offsets, probe, spectrum, wave_index, edge_band, band_coef):
    _, length, columns = maps.shape
    slots = spectrum.shape[0]
    mid = length // 2
    vmem = lambda *shape: pltpu.VMEM(shape, F32)
    vmem16 = lambda *shape: pltpu.VMEM(shape, BF16)
    plane = (length, length)
    half = (mid, length)
    quarter = (mid // 2, length)
    halo = vmem(CHUNKS, 4, length // CHUNKS // 2, length)
    scratch = [
        vmem(4, *plane), vmem(2, *plane), vmem(slots, 2, *plane),
        vmem16(slots, 2 * length, 2 * length), vmem16(slots, 2 * length, 2 * length),
        vmem(slots, 2, *half),
        vmem(slots, *plane), vmem(slots, *plane), vmem16(slots, 2 * length, length),
        vmem16(slots, length, 2 * length),
        vmem(slots, *plane), vmem(slots, *plane),
        vmem(slots, *plane), vmem(slots, *plane), vmem(slots, *plane), vmem(slots, *plane),
        vmem16(slots, length, 2 * length),
        halo, halo, halo, halo, vmem(*plane), vmem(*plane), vmem(*plane), vmem(4, *half),
        vmem(*plane), vmem(*plane), vmem(*plane), vmem(*plane), vmem(*plane),
        vmem(*plane), vmem(*plane), vmem(*plane), vmem(*plane), vmem(*plane),
        vmem(5, *plane), vmem(5, *half), vmem(5, *plane), vmem(5, *half),
        vmem(5, *quarter), vmem(5, *quarter), vmem(5, *quarter), vmem(5, *quarter),
        vmem(5, *quarter), vmem(5, *quarter),
        pltpu.SMEM(offsets.shape, jnp.int32),
        pltpu.SMEM((slots,), F32),
        pltpu.SMEM((slots,), jnp.int32),
        pltpu.SMEM((4, slots), jnp.int32),
        pltpu.SMEM((3, 2, 4), F32),
        pltpu.SMEM((slots, 8), F32),
        pltpu.SemaphoreType.REGULAR,
        pltpu.SemaphoreType.DMA((9,)),
        pltpu.SemaphoreType.DMA((MESSAGES,)),
        pltpu.SemaphoreType.DMA((MESSAGES,)),
    ]
    hbm = pl.BlockSpec(memory_space=pl.ANY)
    return pl.pallas_call(
        functools.partial(kernel, tiles),
        out_shape=pltpu.VMEM(maps.shape, F32),
        in_specs=[hbm] * 8,
        out_specs=pl.BlockSpec(memory_space=pl.ANY),
        scratch_shapes=scratch,
        compiler_params=pltpu.CompilerParams(
            collective_id=0, has_side_effects=True, vmem_limit_bytes=56 << 20
        ),
    )(maps, measured, offsets, probe, spectrum, wave_index, edge_band.T, band_coef.transpose(1, 0, 2))


def solution(mesh):
    in_specs = (
        P(None, None, "tile"),
        P("tile", None, None),
        P("tile"),
        P("wave", None, None, None),
        P("wave"),
        P("wave"),
        P("wave", None),
        P(),
    )
    return jax.shard_map(
        functools.partial(per_device, mesh.shape["tile"]),
        mesh=mesh,
        in_specs=in_specs,
        out_specs=P(None, None, "tile"),
        check_vma=False,
    )
```

```python
import functools
import math

import jax
import jax.numpy as jnp
from jax import lax
from jax.experimental import pallas as pl
from jax.experimental.pallas import tpu as pltpu
from jax.sharding import PartitionSpec as P

WAVES = 48
RELAX = 4.0
FLOOR = 1.0
MESH = pl.DeviceIdType.MESH
F32 = jnp.float32
BF16 = jnp.bfloat16

SIN = (6.283184916495429, -41.341589232688364, 81.5999433297776, -76.61447253120122, 41.34288235437901, -12.471243534763557)
COS = (0.9999999890590201, -19.739204499453688, 64.93911745988827, -85.45013953077586, 60.16763095018129, -25.96759924584206, 6.528658157862129)

MEAS, PW1, PWR, PWA, PWB, IN1, IN1B, IN2, IN2M, GR1, GRR, GRA, GRB, OUT = range(14)
XIN1, XIN1B, XIN2, XIN2M, XPW1, XPWB, XGR1, XGRB = range(14, 22)
CHUNKS = 8
HALO, PASS = (22 + CHUNKS * k for k in range(2))
MESSAGES = 22 + CHUNKS * 2


def sincos_turns(turns):
    f = turns - jnp.round(turns)
    z = f * f
    s = jnp.full_like(z, SIN[-1])
    for k in SIN[-2::-1]:
        s = s * z + k
    c = jnp.full_like(z, COS[-1])
    for k in COS[-2::-1]:
        c = c * z + k
    return c, s * f


def swap(x):
    return pltpu.roll(x, 64, x.ndim - 1)


def kernel(
    tiles,
    maps_hbm, meas_hbm, off_hbm, probe_hbm, spec_hbm, wave_hbm, edge_hbm, band_hbm,
    out_ref,
    mp, ms, pb, w1, w2, obj, psir, psii, psib, midb, farr, fari, psirx, psiix, farrx, farix, nbuf,
    left_s, right_s, halo_r, none_r, ma_s, mb_r, none_m, out_half,
    inten, inten_r, pair_i, far_i, sf, intenx, intenx_r, pair_ix, far_ix, sfx,
    acc, acc_r, accx, accx_r,
    rpack, rrecv, lpack, la, lb, lpx,
    off_ref, spec_ref, wave_ref, edge_ref, band_ref, coef, enter, copy_sem, send_sem, recv_sem,
):
    slots = spec_ref.shape[0]
    length = mp.shape[1]
    mid = length // 2
    chunk = length // CHUNKS
    t = lax.axis_index("tile")
    w = lax.axis_index("wave")
    core = lax.rem(w, 2)
    mate = w + 1 - 2 * core
    far_z = lax.rem(w + 2, 4)
    far_mate = lax.rem(mate + 2, 4)
    up = lax.rem(t + 1, tiles)
    down = lax.rem(t + tiles - 1, tiles)
    first = t == 0
    last = t == tiles - 1
    has_down = t > 0
    has_up = t < tiles - 1
    mine = pl.ds(pl.multiple_of(core * mid, mid), mid)
    other = pl.ds(pl.multiple_of((1 - core) * mid, mid), mid)

    barrier = pltpu.get_barrier_semaphore()

    def greet(device):
        pl.semaphore_signal(barrier, inc=1, device_id=device, device_id_type=MESH)

    greet((t, mate))
    @pl.when(w < 2)
    def _():
        greet((t, far_z))
        greet((t, far_mate))

    @pl.when(has_down)
    def _():
        greet((down, w))

    greetings = 1 + 2 * (w // 2) + (2 * tiles - 2 - t) // tiles

    load_maps = pltpu.make_async_copy(maps_hbm, mp, copy_sem.at[0])
    load_meas = pltpu.make_async_copy(meas_hbm, ms, copy_sem.at[1])
    load_probe = pltpu.make_async_copy(probe_hbm, pb, copy_sem.at[2])
    load_maps.start()
    small = [
        pltpu.make_async_copy(source, target, copy_sem.at[3 + k])
        for k, (source, target) in enumerate((
            (off_hbm, off_ref), (spec_hbm, spec_ref), (wave_hbm, wave_ref),
            (edge_hbm, edge_ref), (band_hbm, band_ref),
        ))
    ]
    for copy in small:
        copy.start()
    load_meas.start()
    load_probe.start()

    def remote(k, src, dst, device):
        return pltpu.make_async_remote_copy(
            src_ref=src, dst_ref=dst, send_sem=send_sem.at[min(k, HALO + k // PASS)], recv_sem=recv_sem.at[k],
            device_id=device, device_id_type=MESH,
        )

    def low_lanes(rows):
        return lax.broadcasted_iota(jnp.int32, (rows, length), 1) < mid

    def slot_coefficients(s, carry):
        for m in range(4):
            e = edge_ref[m, s]
            for k in range(2):
                c = [band_ref[n, k, m] for n in range(3)]
                coef[s, 4 * k + m] = jnp.where(e == 0, c[0], jnp.where(e == 1, c[1], c[2]))
        return carry


    def groups(size, body, carry):
        def step(i, carry):
            return body([i * size + j for j in range(size)], carry)

        return lax.fori_loop(0, slots // size, step, carry)

    column = lax.broadcasted_iota(jnp.int32, (32, length), 1) - mid
    row = lax.broadcasted_iota(jnp.int32, (32, length), 0) - mid
    normaliser = 1.0 / math.sqrt(length)

    def table_slot(s, carry):
        which = jnp.full((32, length), wave_ref[s], jnp.int32).astype(F32)
        sampling = (0.6 + 0.4 * which / (WAVES - 1)) * (1.0 / length)
        c, sn = sincos_turns(sampling * (row * column).astype(F32))
        c, sn = c * normaliser, sn * normaliser
        step_c, step_s = sincos_turns(sampling[0:8] * (32 * column[0:8]).astype(F32))
        step_c, step_s = jnp.tile(step_c, (4, 1)), jnp.tile(step_s, (4, 1))
        for r in range(0, length, 32):
            if r:
                c, sn = c * step_c - sn * step_s, c * step_s + sn * step_c
            re = c.astype(BF16)
            im = (-sn).astype(BF16)
            nim = sn.astype(BF16)
            top, low = pl.ds(r, 32), pl.ds(length + r, 32)
            left, right = pl.ds(0, length), pl.ds(length, length)
            w1[s, top, left] = re
            w1[s, top, right] = nim
            w1[s, low, left] = im
            w1[s, low, right] = re
            w2[s, top, left] = re
            w2[s, top, right] = im
            w2[s, low, left] = nim
            w2[s, low, right] = re
        return carry

    load_maps.wait()
    hc = chunk // 2
    low_hc = low_lanes(hc)
    for q in range(CHUNKS):
        r = q * chunk
        for m in range(4):
            top, bottom = mp[m, r : r + hc], mp[m, r + hc : r + chunk]
            left_s[q, m] = jnp.where(low_hc, top, swap(bottom))
            right_s[q, m] = jnp.where(low_hc, swap(top), bottom)

    pl.semaphore_wait(barrier, greetings)

    @pl.when(w >= 2)
    def _():
        for device in ((t, far_z), (t, far_mate)):
            pl.semaphore_signal(enter, inc=1, device_id=device, device_id_type=MESH)


    def transmission(s, planes):
        a = [coef[s, m] for m in range(4)]
        b = [coef[s, 4 + m] for m in range(4)]
        absorb = a[0] * planes[0] + a[1] * planes[1] + a[2] * planes[2] + a[3] * planes[3]
        phase = b[0] * planes[0] + b[1] * planes[1] + b[2] * planes[2] + b[3] * planes[3]
        damping = jnp.exp(-absorb)
        c, sn = sincos_turns(phase * (0.5 / math.pi))
        return damping * c, damping * sn

    def half_object(packed):
        def body(group, carry):
            for q in range(CHUNKS):
                planes = [packed[q, m] for m in range(4)]
                for s in group:
                    re, im = transmission(s, planes)
                    obj[s, 0, pl.ds(q * hc, hc), :] = re
                    obj[s, 1, pl.ds(q * hc, hc), :] = im
            return carry

        groups(12, body, 0)

    def waves_at_object(q, packed, pr, pi, power, fresh_low=False):
        at = pl.ds(q * hc, hc)

        def body(group, totals):
            totals = list(totals)
            planes = [packed[q, m] for m in range(4)]
            for s in group:
                nre, nim = transmission(s, planes)
                ore, oim = obj[s, 0, at, :], obj[s, 1, at, :]
                if fresh_low:
                    nre, nim, ore, oim = ore, oim, nre, nim
                for half, (re, im) in enumerate((
                    (jnp.where(low_hc, ore, swap(nre)), jnp.where(low_hc, oim, swap(nim))),
                    (jnp.where(low_hc, swap(ore), nre), jnp.where(low_hc, swap(oim), nim)),
                )):
                    rows = pl.ds(q * chunk + half * hc, hc)
                    p_re, p_im = pb[s, 0, rows, :], pb[s, 1, rows, :]
                    x = p_re * re - p_im * im
                    y = p_re * im + p_im * re
                    pr[s, rows, :] = x
                    pi[s, rows, :] = y
                    psib[s, rows, :] = x.astype(BF16)
                    psib[s, pl.ds(length + q * chunk + half * hc, hc), :] = y.astype(BF16)
                    totals[half] = totals[half] + spec_ref[s] * (x * x + y * y)
            return tuple(totals)

        zero = jnp.zeros((hc, length), F32)
        for half, total in enumerate(groups(12, body, (zero, zero))):
            power[pl.ds(q * chunk + half * hc, hc), :] = total

    def row_half(rows_at):
        return (
            pl.ds(pl.multiple_of(rows_at, mid), mid),
            pl.ds(pl.multiple_of(rows_at + length, mid), mid),
        )

    def half_product(table, s, rows_at, data, into):
        rows, low_rows = row_half(rows_at)
        left = jnp.concatenate([table[s, rows, :], table[s, low_rows, :]], axis=0)
        m = jnp.dot(left, data, preferred_element_type=F32).astype(BF16)
        into[s, rows, 0:length] = m[:mid]
        into[s, rows, length : 2 * length] = m[mid:]

    def left_forward(rows_at):
        for s in range(slots):
            half_product(w1, s, rows_at, psib[s], midb)

    def right_forward(rows_at, fr, fi, total):
        rows = pl.ds(pl.multiple_of(rows_at, mid), mid)

        def body(group, light):
            for s in group:
                far = jnp.dot(midb[s, rows, :], w2[s], preferred_element_type=F32)
                x, y = far[:, :length], far[:, length:]
                fr[s, rows, :] = x
                fi[s, rows, :] = y
                light = light + spec_ref[s] * (x * x + y * y)
            return light

        total[rows, :] = groups(12, body, jnp.zeros((mid, length), F32))

    def back_left(rows_at, short, fr, fi):
        for s in range(slots):
            factor = spec_ref[s] * short[...]
            d = jnp.concatenate(
                [(factor * fr[s]).astype(BF16), (factor * fi[s]).astype(BF16)], axis=0
            )
            psib[s] = d
            half_product(w2, s, rows_at, d, nbuf)

    def back_left_again(rows_at):
        for s in range(slots):
            half_product(w2, s, rows_at, psib[s], nbuf)

    def back_right(rows_at, pr, pi, into):
        rows = pl.ds(pl.multiple_of(rows_at, mid), mid)
        for m in range(4):
            into[m, rows, :] = jnp.zeros((mid, length), F32)

        def body(group, carry):
            back = [jnp.dot(nbuf[s, rows, :], w1[s], preferred_element_type=F32) for s in group]
            for r in range(0, mid, 16):
                part = pl.ds(pl.multiple_of(rows_at + r, 16), 16)
                sums = [into[m, part, :] for m in range(4)]
                for s, both in zip(group, back):
                    br, bi = both[r : r + 16, :length], both[r : r + 16, length:]
                    x, y = pr[s, part, :], pi[s, part, :]
                    cr = x * br + y * bi
                    ci = x * bi - y * br
                    for m in range(4):
                        sums[m] = sums[m] + (coef[s, 4 + m] * ci - coef[s, m] * cr)
                for m in range(4):
                    into[m, part, :] = sums[m]
            return carry

        groups(12, body, 0)

    at_mine, at_other = core * mid, (1 - core) * mid
    frames_here = jnp.where(first, 1.0, 2.0)
    quarter = mid // 2

    def pack_right(y):
        return jnp.where(low_lanes(quarter), swap(y[:quarter]), y[quarter:])

    def pack_left(y):
        return jnp.where(low_lanes(quarter), y[:quarter], swap(y[quarter:]))

    four = pl.ds(0, 4)
    sx_in1 = remote(XIN1, intenx.at[other], intenx_r.at[other], (t, mate))
    sx_in1b = remote(XIN1B, intenx.at[mine], intenx_r.at[mine], (t, mate))
    sx_in2 = remote(XIN2, pair_ix.at[mine], far_ix.at[mine], (t, far_z))
    sx_in2m = remote(XIN2M, pair_ix.at[mine], far_ix.at[mine], (t, far_mate))
    sx_pw1 = remote(XPW1, accx.at[4, other], accx_r.at[4], (t, mate))
    sx_pwb = remote(XPWB, lpx.at[4], lb.at[4], (t, far_z))
    sx_gr1 = remote(XGR1, accx.at[four, other], accx_r.at[four], (t, mate))
    sx_grb = remote(XGRB, lpx.at[four], lb.at[four], (t, far_z))

    def light_of_both(partial, received, pair, first_half, second_half, far_one, far_two):
        second_half.start()
        first_half.wait_recv()
        pair[mine, :] = partial[mine, :] + received[mine, :]
        far_one.start()
        far_two.start()

    def factors(partial, received, pair, far, one, two, frames, into):
        pair[other, :] = partial[other, :] + received[other, :]
        for r in range(0, length, 32):
            rows = pl.ds(r, 32)
            inv = 1.0 / jnp.maximum(pair[rows, :] + far[rows, :], FLOOR)
            into[rows, :] = jnp.sqrt(one[rows, :] * inv) + jnp.sqrt(two[rows, :] * inv) - frames

    def extra_forward():
        sx_pw1.start()
        left_forward(at_other)
        right_forward(at_other, farrx, farix, intenx)
        sx_in1.start()
        left_forward(at_mine)
        right_forward(at_mine, farrx, farix, intenx)
        light_of_both(intenx, intenx_r, pair_ix, sx_in1, sx_in1b, sx_in2, sx_in2m)
        sx_pw1.wait_recv()
        lpx[4] = pack_left(accx[4, mine, :] + accx_r[4])
        sx_pwb.start()

    def extra_shortfall():
        sx_in1b.wait_recv()
        sx_in2.wait_recv()
        sx_in2m.wait_recv()
        factors(intenx, intenx_r, pair_ix, far_ix, ms.at[1], none_m, 1.0, sfx)

    def extra_backward():
        back_left(at_other, sfx, farrx, farix)
        back_right(at_other, psirx, psiix, accx)
        sx_gr1.start()
        back_left_again(at_mine)
        back_right(at_mine, psirx, psiix, accx)
        sx_gr1.wait_recv()
        for m in range(4):
            lpx[m] = pack_left(accx[m, mine, :] + accx_r[m])
        sx_grb.start()

    @pl.when(first)
    def _():
        halo_r[...] = jnp.zeros_like(halo_r)
        mb_r[...] = jnp.zeros_like(mb_r)

    @pl.when(last)
    def _():
        none_r[...] = jnp.zeros_like(none_r)
        none_m[...] = jnp.zeros_like(none_m)

    fetches = core == 1
    send_halo = [remote(HALO + q, right_s.at[q], halo_r.at[q], (up, w)) for q in range(CHUNKS)]
    pass_halo = [remote(PASS + q, halo_r.at[q], halo_r.at[q], (t, mate)) for q in range(CHUNKS)]
    send_meas = remote(MEAS, ms.at[1], mb_r, (up, w))

    @pl.when(fetches & has_up)
    def _():
        for copy in send_halo:
            copy.start()

    for copy in small:
        copy.wait()
    lax.fori_loop(0, slots, slot_coefficients, 0)
    load_meas.wait()
    low_first = off_ref[0] < off_ref[1]
    for r in range(0, length, 32):
        rows = pl.ds(r, 32)
        one, two = ms[0, rows, :], ms[1, rows, :]
        ma_s[rows, :] = jnp.where(low_first, one, two)
        ms[1, rows, :] = jnp.where(low_first, two, one)

    groups(4, lambda group, carry: [table_slot(s, carry) for s in group][0], 0)

    half_object(left_s)

    load_probe.wait()

    def arrived(q):
        @pl.when(has_down & fetches)
        def _():
            send_halo[q].wait_recv()
            pass_halo[q].start()

    arrived(0)
    for q in range(CHUNKS):
        if q + 1 < CHUNKS:
            arrived(q + 1)

        @pl.when(has_down & jnp.logical_not(fetches))
        def _():
            pass_halo[q].wait_recv()

        waves_at_object(q, halo_r, psir, psii, acc.at[4], fresh_low=True)

        if q == 1:

            @pl.when(has_up)
            def _():
                send_meas.start()

    s_pw1 = remote(PW1, acc.at[4, other], acc_r.at[4], (t, mate))
    s_in1 = remote(IN1, inten.at[other], inten_r.at[other], (t, mate))
    s_in1b = remote(IN1B, inten.at[mine], inten_r.at[mine], (t, mate))
    s_in2 = remote(IN2, pair_i.at[mine], far_i.at[mine], (t, far_z))
    s_in2m = remote(IN2M, pair_i.at[mine], far_i.at[mine], (t, far_mate))
    s_gr1 = remote(GR1, acc.at[four, other], acc_r.at[four], (t, mate))
    s_pwr = remote(PWR, rpack.at[4], rrecv.at[4], (t, far_z))
    s_pwa = remote(PWA, lpack.at[4], la.at[4], (down, w))
    s_pwb = remote(PWB, lpack.at[4], lb.at[4], (down, far_z))
    s_grr = remote(GRR, rpack.at[four], rrecv.at[four], (t, far_z))
    s_gra = remote(GRA, lpack.at[four], la.at[four], (down, w))
    s_grb = remote(GRB, lpack.at[four], lb.at[four], (down, far_z))

    s_pw1.start()
    left_forward(at_other)
    right_forward(at_other, farr, fari, inten)
    s_in1.start()
    left_forward(at_mine)
    right_forward(at_mine, farr, fari, inten)

    @pl.when(w < 2)
    def _():
        pl.semaphore_wait(enter, 2)

    light_of_both(inten, inten_r, pair_i, s_in1, s_in1b, s_in2, s_in2m)

    s_pw1.wait_recv()
    power = frames_here * (acc[4, mine, :] + acc_r[4])
    lpack[4] = pack_left(power)
    rpack[4] = pack_right(power)

    @pl.when(last)
    def _():
        half_object(right_s)
        for q in range(CHUNKS):
            waves_at_object(q, none_r, psirx, psiix, accx.at[4])
        extra_forward()

    @pl.when(has_down)
    def _():
        send_meas.wait_recv()

    s_in1b.wait_recv()
    s_in2.wait_recv()
    s_in2m.wait_recv()
    factors(inten, inten_r, pair_i, far_i, ma_s, mb_r, frames_here, sf)
    s_pwr.start()


    @pl.when(has_down)
    def _():
        s_pwa.start()
        s_pwb.start()

    back_left(at_other, sf, farr, fari)
    back_right(at_other, psir, psii, acc)
    s_gr1.start()
    back_left_again(at_mine)
    back_right(at_mine, psir, psii, acc)
    s_gr1.wait_recv()
    for m in range(4):
        y = acc[m, mine, :] + acc_r[m]
        lpack[m] = pack_left(y)
        rpack[m] = pack_right(y)

    near = w < 2

    @pl.when(has_down & near)
    def _():
        s_gra.start()

    @pl.when(has_down)
    def _():
        s_grb.start()

    s_grr.start()

    @pl.when(has_down & jnp.logical_not(near))
    def _():
        s_gra.start()

    @pl.when(last)
    def _():
        extra_shortfall()
        extra_backward()
        sx_pwb.wait_recv()
        sx_grb.wait_recv()
        la[...] = lpx[...]

    @pl.when(has_up)
    def _():
        s_pwa.wait_recv()
        s_pwb.wait_recv()
        s_gra.wait_recv()
        s_grb.wait_recv()

    s_pwr.wait_recv()
    s_grr.wait_recv()

    def totals(m):
        l = la[m] + lb[m]
        r = rpack[m] + rrecv[m]
        return jnp.where(low_lanes(quarter), r, swap(l)), jnp.where(low_lanes(quarter), swap(r), l)

    powers = [RELAX / (p + 1.0) for p in totals(4)]
    for m in range(4):
        for q, total in enumerate(totals(m)):
            rows = pl.ds(pl.multiple_of(at_mine + q * quarter, quarter), quarter)
            out_half[m, q * quarter : (q + 1) * quarter, :] = mp[m, rows, :] + total * powers[q]
    s_out = remote(OUT, out_half, out_ref.at[:, mine], (t, mate))
    s_out.start()
    keep_out = pltpu.make_async_copy(out_half, out_ref.at[:, mine], copy_sem.at[8])
    keep_out.start()

    for copy in (s_pw1, s_in1, s_in1b, s_in2, s_in2m, s_gr1, s_pwr, s_grr):
        copy.wait_send()

    @pl.when(has_up)
    def _():
        send_meas.wait_send()

    @pl.when(has_up & fetches)
    def _():
        remote(HALO, right_s, halo_r, (up, w)).wait_send()

    @pl.when(has_down & fetches)
    def _():
        remote(PASS, halo_r, halo_r, (t, mate)).wait_send()

    @pl.when(has_down)
    def _():
        for copy in (s_pwa, s_pwb, s_gra, s_grb):
            copy.wait_send()

    @pl.when(last)
    def _():
        for copy in (sx_in1, sx_in1b, sx_in2, sx_in2m, sx_pw1, sx_pwb, sx_gr1, sx_grb):
            copy.wait_send()

    keep_out.wait()
    s_out.wait()


def per_device(tiles, maps, measured, offsets, probe, spectrum, wave_index, edge_band, band_coef):
    _, length, columns = maps.shape
    slots = spectrum.shape[0]
    mid = length // 2
    vmem = lambda *shape: pltpu.VMEM(shape, F32)
    vmem16 = lambda *shape: pltpu.VMEM(shape, BF16)
    plane = (length, length)
    half = (mid, length)
    quarter = (mid // 2, length)
    halo = vmem(CHUNKS, 4, length // CHUNKS // 2, length)
    scratch = [
        vmem(4, *plane), vmem(2, *plane), vmem(slots, 2, *plane),
        vmem16(slots, 2 * length, 2 * length), vmem16(slots, 2 * length, 2 * length),
        vmem(slots, 2, *half),
        vmem(slots, *plane), vmem(slots, *plane), vmem16(slots, 2 * length, length),
        vmem16(slots, length, 2 * length),
        vmem(slots, *plane), vmem(slots, *plane),
        vmem(slots, *plane), vmem(slots, *plane), vmem(slots, *plane), vmem(slots, *plane),
        vmem16(slots, length, 2 * length),
        halo, halo, halo, halo, vmem(*plane), vmem(*plane), vmem(*plane), vmem(4, *half),
        vmem(*plane), vmem(*plane), vmem(*plane), vmem(*plane), vmem(*plane),
        vmem(*plane), vmem(*plane), vmem(*plane), vmem(*plane), vmem(*plane),
        vmem(5, *plane), vmem(5, *half), vmem(5, *plane), vmem(5, *half),
        vmem(5, *quarter), vmem(5, *quarter), vmem(5, *quarter), vmem(5, *quarter),
        vmem(5, *quarter), vmem(5, *quarter),
        pltpu.SMEM(offsets.shape, jnp.int32),
        pltpu.SMEM((slots,), F32),
        pltpu.SMEM((slots,), jnp.int32),
        pltpu.SMEM((4, slots), jnp.int32),
        pltpu.SMEM((3, 2, 4), F32),
        pltpu.SMEM((slots, 8), F32),
        pltpu.SemaphoreType.REGULAR,
        pltpu.SemaphoreType.DMA((9,)),
        pltpu.SemaphoreType.DMA((HALO + 2,)),
        pltpu.SemaphoreType.DMA((MESSAGES,)),
    ]
    hbm = pl.BlockSpec(memory_space=pl.ANY)
    return pl.pallas_call(
        functools.partial(kernel, tiles),
        out_shape=pltpu.VMEM(maps.shape, F32),
        in_specs=[hbm] * 8,
        out_specs=pl.BlockSpec(memory_space=pl.ANY),
        scratch_shapes=scratch,
        compiler_params=pltpu.CompilerParams(
            collective_id=0, has_side_effects=True, vmem_limit_bytes=56 << 20
        ),
    )(maps, measured, offsets, probe, spectrum, wave_index, edge_band.T, band_coef.transpose(1, 0, 2))


def solution(mesh):
    in_specs = (
        P(None, None, "tile"),
        P("tile", None, None),
        P("tile"),
        P("wave", None, None, None),
        P("wave"),
        P("wave"),
        P("wave", None),
        P(),
    )
    return jax.shard_map(
        functools.partial(per_device, mesh.shape["tile"]),
        mesh=mesh,
        in_specs=in_specs,
        out_specs=P(None, None, "tile"),
        check_vma=False,
    )
```
